32 devices in a mesh: section: 2 (over y), dp: 16 (over z, x, core).
Axes of the slice: x: 2, y: 2, z: 4, core: 2. Of those that a mesh axis runs over, the one named last changes fastest.
Arguments:
- patches: bfloat16 [2, 16, 256, 384], P(None, 'dp'), may hold values from -6 to 6
- condition: bfloat16 [2, 16, 384], P(None, 'dp'), may hold values from -6 to 6
- valid_count: int32 [2, 16], P(None, 'dp'), may hold values from 128 to 256, as said below
- cotangent: bfloat16 [2, 16, 256, 384], P(None, 'dp'), may hold values from -6 to 6
- ada_weight: bfloat16 [2, 384, 2304], P('section'), may hold values from -0.3125 to 0.3125
- conv_weight: bfloat16 [2, 3, 384], P('section'), may hold values from -3 to 3
- proj_weight: bfloat16 [2, 384, 1536], P('section'), may hold values from -0.3125 to 0.3125
- out_weight: bfloat16 [2, 384, 384], P('section'), may hold values from -0.625 to 0.625
- up_weight: bfloat16 [2, 384, 1536], P('section'), may hold values from -0.3125 to 0.3125
- down_weight: bfloat16 [2, 1536, 384], P('section'), may hold values from -0.3125 to 0.3125
Outputs:
- activations: bfloat16 [2, 2, 16, 256, 384], P('section', None, 'dp')
- input_grads: bfloat16 [2, 2, 16, 256, 384], P('section', None, 'dp')
- condition_grad: float32 [2, 16, 384], P(None, 'dp')
- ada_grad: float32 [2, 384, 2304], P('section', 'dp')
- conv_grad: float32 [2, 3, 384], P('section', None, 'dp')
- proj_grad: float32 [2, 384, 1536], P('section', 'dp')
- out_grad: float32 [2, 384, 384], P('section', 'dp')
- up_grad: float32 [2, 384, 1536], P('section', 'dp')
- down_grad: float32 [2, 1536, 384], P('section', 'dp')
The draws below stay inside these ranges and needn't reach their ends.
Inputs may be any that keep to these rules, and one draw needn't show every extreme that they name: Patches of an image at positions below its valid_count are real, the others are padding; some image has all 256 valid and some exactly 128.
All inputs are finite; a program needn't handle non-finite values.
Results may differ from the reference program's by a relative error of at most 0.025.
Values may be sent and summed in bfloat16 or wider, within the bound.
A program may use at most 128 MiB of HBM per device.

```python
import math
import jax
import jax.numpy as jnp
from jax import lax

D = 384
HEADS = 6
HD = 64
FF = 1536
BLOCK = 64
KW = 3
MB = 2
L = 256
IMAGES = 16


def draw_valid_count(key, part):
    lengths = jax.random.randint(key, (MB, IMAGES), L // 2, L + 1)
    lengths = lengths.at[0, 0].set(L)
    return lengths.at[MB - 1, IMAGES - 1].set(L // 2)


def strengthened(array, rng, source, target, blocks, factor):
    def block_of(dim):
        return (jnp.arange(array.shape[dim]) // (array.shape[dim] // blocks)).reshape((-1,) + (1,) * (array.ndim - 1 - dim))

    near = jax.random.permutation(rng, blocks)[block_of(target)]
    other_side = (block_of(target) + blocks // 2) % blocks
    return jnp.where((block_of(source) == near) | (block_of(source) == other_side), factor * array, array)


def level_of(key, extent, shards, least, largest):
    def one(dim, parts):
        steps = jax.random.uniform(jax.random.fold_in(jax.random.fold_in(key, 6), dim), (parts,), jnp.float32, least / len(shards), largest / len(shards))
        return jnp.repeat(jnp.exp(steps), extent[dim] // parts).reshape((-1,) + (1,) * (len(extent) - dim - 1))

    gain = one(*shards[0])
    for cut in shards[1:]:
        gain = gain * one(*cut)
    return gain


def noise(own_key, dims, deviation, bound, split=(), held_as=jnp.bfloat16):
    entries = deviation * jax.random.normal(own_key, dims, jnp.float32)
    if split:
        entries = entries * level_of(own_key, dims, split, -0.22, 0.18)
    return jnp.clip(entries, -bound, bound).astype(held_as)


def noise_with(own_key, extent, scale, most, split, heavy, held_as=jnp.bfloat16):
    values = scale * jax.random.normal(own_key, extent, jnp.float32)
    if split:
        values = values * level_of(own_key, extent, split, -0.22, 0.18)
    return jnp.clip(strengthened(values, jax.random.fold_in(own_key, 3), *heavy), -most, most).astype(held_as)


def setup_inputs(seed: int = 0) -> dict:
    key_of = jax.random.split(jax.random.key(seed), 11)
    patches = noise(key_of[0], (MB, IMAGES, L, D), 1.0, 6.0, ((1, 16),))
    condition = noise_with(key_of[1], (MB, IMAGES, D), 1.0, 6.0, ((1, 16),), (1, 2, 16, 2.0))
    valid_count = draw_valid_count(jax.random.fold_in(key_of[10], 71), 0)
    cotangent = noise(key_of[3], (MB, IMAGES, L, D), 1.0, 6.0, ((1, 16),))
    ada_weight = noise(key_of[4], (2, D, 6 * D), D ** -0.5, 0.3125, ((0, 2),))
    conv_weight = noise(key_of[5], (2, KW, D), 0.6, 3.0, ((0, 2),))
    proj_weight = noise(key_of[6], (2, D, 4 * D), D ** -0.5, 0.3125, ((0, 2),))
    out_weight = noise(key_of[7], (2, D, D), (D // 4) ** -0.5, 0.625, ((0, 2),))
    up_weight = noise(key_of[8], (2, D, FF), D ** -0.5, 0.3125, ((0, 2),))
    down_weight = noise(key_of[9], (2, FF, D), (FF // 4) ** -0.5, 0.3125, ((0, 2),))
    return {"patches": patches, "condition": condition, "valid_count": valid_count, "cotangent": cotangent, "ada_weight": ada_weight, "conv_weight": conv_weight, "proj_weight": proj_weight, "out_weight": out_weight, "up_weight": up_weight, "down_weight": down_weight}


@jax.custom_vjp
def low(v):
    return lax.optimization_barrier(v.astype(jnp.bfloat16)).astype(jnp.float32)

@jax.custom_vjp
def low_back(v):
    return v

def low_keep(v):
    return (low(v), None)

def low_pass(kept, grad):
    return (grad,)

def back_keep(v):
    return (v, None)

def back_low(kept, grad):
    return (low(grad),)
low.defvjp(low_keep, low_pass)
low_back.defvjp(back_keep, back_low)

def matmul(left, right):
    return jnp.dot(left, right, precision=lax.Precision.HIGHEST, preferred_element_type=jnp.float32)

def contract(formula, left, right):
    return jnp.einsum(formula, left, right, precision=lax.Precision.HIGHEST, preferred_element_type=jnp.float32)

def layer_norm(values):
    centred = values - lax.optimization_barrier(jnp.mean(values, -1, keepdims=True))
    return centred * lax.rsqrt(lax.optimization_barrier(jnp.mean(centred * centred, -1, keepdims=True)) + 1e-06)

def orient(values, second):
    if second:
        return jnp.flip(values, 1)
    return values

def causal_conv(values, kernel):
    padded = jnp.pad(values, ((0, 0), (KW - 1, 0), (0, 0)))
    summed = jnp.zeros_like(values)
    for offset in range(KW):
        begin_at = KW - 1 - offset
        summed = summed + kernel[offset] * padded[:, begin_at:begin_at + L]
    return summed

def split_heads(values):
    return values.reshape(values.shape[0], L // BLOCK, BLOCK, HEADS, HD)

def attend(query, keyed, valued):
    images_here = query.shape[0]
    query_h = split_heads(query)
    keyed_h = split_heads(keyed)
    valued_h = split_heads(valued)
    lower_tri = jnp.tril(jnp.ones((BLOCK, BLOCK), bool))
    scores = contract('bnqhd,bnkhd->bnhqk', query_h, keyed_h)
    weights = low(low_back(jnp.where(lower_tri, scores, 0.0) * HD ** (-0.5)))
    intra = contract('bnhqk,bnkhd->bnqhd', weights, valued_h)
    terms = low_back(contract('bnkhd,bnkhe->bnhde', keyed_h, valued_h))
    running = jnp.cumsum(terms, 1)
    states = low(jnp.concatenate([jnp.zeros_like(terms[:, :1]), running[:, :-1]], 1))
    inter = contract('bnqhd,bnhde->bnqhe', query_h, states) * HD ** (-0.5)
    return (intra + inter).reshape(images_here, L, D)

def layer(inflow, cond_rows, mask_rows, params, second):
    ada_matrix, conv_kernel, proj_matrix, out_matrix, up_matrix, down_matrix = params
    cond_act = low(jax.nn.silu(cond_rows))
    modulation = low_back(matmul(cond_act, ada_matrix))
    pieces = [modulation[:, None, index * D:(index + 1) * D] for index in range(6)]
    mixed = (layer_norm(inflow) * (1.0 + pieces[1]) + pieces[0]) * mask_rows[..., None]
    turned = orient(mixed, second)
    turned_mask = orient(mask_rows, second)[..., None]
    conv_out = low(causal_conv(turned, conv_kernel) * turned_mask)
    projected = low_back(matmul(conv_out, proj_matrix))
    query = low(projected[..., :D])
    keyed = low(projected[..., D:2 * D])
    valued = low(projected[..., 2 * D:3 * D])
    gate_pre = projected[..., 3 * D:]
    attended = low_back(attend(query, keyed, valued))
    attend_normed = attended * lax.rsqrt(lax.optimization_barrier(jnp.mean(attended * attended, -1, keepdims=True)) + 1e-06)
    gated = low(orient(attend_normed * jax.nn.silu(gate_pre), second))
    branch = low_back(matmul(gated, out_matrix))
    hidden = inflow + pieces[2] * branch
    mixed_two = low(layer_norm(hidden) * (1.0 + pieces[4]) + pieces[3])
    hidden_pre = low_back(matmul(mixed_two, up_matrix))
    hidden_act = low(jax.nn.gelu(hidden_pre, approximate=True))
    ffn_out = low_back(matmul(hidden_act, down_matrix))
    return hidden + pieces[5] * ffn_out

def forward(inflow, cond_rows, mask_rows, first_set, second_set, nudge):
    first_out = layer(inflow, cond_rows, mask_rows, first_set, False)
    sent = low_back(low(first_out))
    final_out = layer(sent + nudge, cond_rows, mask_rows, second_set, True)
    return (final_out, first_out)

def reference(patches, condition, valid_count, cotangent, ada_weight, conv_weight, proj_weight, out_weight, up_weight, down_weight):
    image_rows = MB * IMAGES
    group_size = math.gcd(image_rows, max(1, 4096 // L))
    group_count = image_rows // group_size
    weights_all = tuple((member.astype(jnp.float32) for member in (ada_weight, conv_weight, proj_weight, out_weight, up_weight, down_weight)))
    first_params = tuple((member[0] for member in weights_all))
    second_params = tuple((member[1] for member in weights_all))
    inputs_f = patches.astype(jnp.float32).reshape(group_count, group_size, L, D)
    conds_f = condition.astype(jnp.float32).reshape(group_count, group_size, D)
    positions = jnp.arange(L, dtype=jnp.int32)
    counts = valid_count.reshape(image_rows).astype(jnp.int32)
    masks_f = (positions[None, :] < counts[:, None]).astype(jnp.float32).reshape(group_count, group_size, L)
    cots_f = cotangent.astype(jnp.float32).reshape(group_count, group_size, L, D)

    def one_group(totals, group_data):
        inflow, cond_rows, mask_rows, upstream = group_data

        def wrapped(inflow_arg, cond_arg, first_set, second_set, nudge):
            return forward(inflow_arg, cond_arg, mask_rows, first_set, second_set, nudge)
        final_out, backward, first_out = jax.vjp(wrapped, inflow, cond_rows, first_params, second_params, jnp.zeros_like(inflow), has_aux=True)
        d_inflow, d_cond, d_first, d_second, d_nudge = backward(upstream)
        totals = jax.tree.map(lambda summed, addend: summed + addend, totals, (d_first, d_second))
        return (totals, (first_out.astype(jnp.bfloat16), final_out.astype(jnp.bfloat16), d_inflow.astype(jnp.bfloat16), d_nudge.astype(jnp.bfloat16), d_cond))
    zero_totals = jax.tree.map(jnp.zeros_like, (first_params, second_params))
    totals, stacked = lax.scan(one_group, zero_totals, (inputs_f, conds_f, masks_f, cots_f))
    first_b, final_b, input_b, middle_b, cond_grads = stacked
    whole_shape = (MB, IMAGES, L, D)
    activations = jnp.stack([first_b.reshape(whole_shape), final_b.reshape(whole_shape)])
    input_grads = jnp.stack([input_b.reshape(whole_shape), middle_b.reshape(whole_shape)])
    condition_grad = cond_grads.reshape(MB, IMAGES, D)
    grads = [jnp.stack([totals[0][index], totals[1][index]]) for index in range(6)]
    return (activations, input_grads, condition_grad, grads[0], grads[1], grads[2], grads[3], grads[4], grads[5])
```

```python
import jax
import jax.numpy as jnp
from jax import lax
from jax.experimental import pallas as pl
from jax.experimental.pallas import tpu as pltpu
from jax.sharding import PartitionSpec as P

F32, BF = jnp.float32, jnp.bfloat16
HD = 64
TAPS = 3
GROUP = 16
R = 64
MESH = pl.DeviceIdType.MESH
SCALE = HD**-0.5


def mm(a, b):
    return jnp.dot(a, b, preferred_element_type=F32)


def nt(a, b):
    return lax.dot_general(a, b, (((1,), (1,)), ((), ())), preferred_element_type=F32)


def tn(a, b):
    return lax.dot_general(a, b, (((0,), (0,)), ((), ())), preferred_element_type=F32)


def fold(v):
    return jnp.sum(v.reshape(v.shape[0] // 8, 8, v.shape[1]), 0)


def wide(col):
    return jnp.broadcast_to(col, (col.shape[0], 128))


def sigmoid(v):
    return 1.0 / (1.0 + jnp.exp(-v))


def stats(v):
    c = v - jnp.mean(v, -1, keepdims=True)
    s = lax.rsqrt(jnp.mean(c * c, -1, keepdims=True) + 1e-6)
    return c * s, s


def norm_back(g, n, s):
    return s * (g - jnp.mean(g, -1, keepdims=True) - n * jnp.mean(g * n, -1, keepdims=True))


def rows(r, extra=0):
    return pl.ds(pl.multiple_of(r * R, R), R + extra)


def loop(n, body, init=0):
    return lax.fori_loop(0, n, body, init)


class Refs:
    def __init__(self, names, refs):
        self.__dict__.update(zip(names, refs, strict=True))


def triangle(second, length):
    sign = jnp.where(second, -1, 1)
    query = lax.broadcasted_iota(jnp.int32, (length, length), 0)
    key = lax.broadcasted_iota(jnp.int32, (length, length), 1)
    return (query - key) * sign >= 0


def forward(s, i, second, count, loaded):
    length, features = s.inflow.shape[1:]
    hidden = s.wu.shape[1]
    mod = s.mod.at[i]
    tok = pl.ds(pl.multiple_of(i * length, length), length)

    def trow(r):
        return pl.ds(pl.multiple_of(i * length + r * R, R), R)

    def place(r):
        return r * R + lax.broadcasted_iota(jnp.int32, (R, 1), 0)

    def first_norm(r, c):
        n, sc = stats(s.inflow[i, rows(r), :].astype(F32))
        s.n1[i, rows(r), :] = n
        s.r1[i, rows(r), :] = wide(sc)
        m = jnp.where(place(r) < count, n * (1.0 + mod[1:2, :]) + mod[0:1, :], 0.0)
        s.mixed[i, pl.ds(pl.multiple_of(r * R + 8, 8), R), :] = m
        return c

    loop(length // R, first_norm)
    loaded("wc")

    def conv(second):
        def one(r, c):
            buf = s.mixed[i, rows(r, 16), :]
            v = jnp.zeros((R, features), F32)
            for j in range(TAPS):
                lo = 8 + j if second else 8 - j
                v = v + s.wc[j : j + 1, :].astype(F32) * buf[lo : lo + R]
            s.conv[trow(r), :] = jnp.where(place(r) < count, v, 0.0).astype(BF)
            return c

        loop(length // R, one)

    pl.when(jnp.logical_not(second))(lambda: conv(False))
    pl.when(second)(lambda: conv(True))
    loaded("wp")
    cv = s.conv[tok, :]
    for c in range(3):
        p = mm(cv, s.wp[:, c * features : (c + 1) * features])
        s.qkv[i, :, c * features : (c + 1) * features] = (p * SCALE if c == 0 else p).astype(BF)
    s.wide_a[...] = mm(cv, s.wp[:, 3 * features :])
    keep = triangle(second, length)
    lane = lax.broadcasted_iota(jnp.int32, (length, 2 * HD), 1) < HD

    def pair(p, c):
        def at(k):
            return pl.ds(pl.multiple_of(k * features + p * 2 * HD, 2 * HD), 2 * HD)

        q, k, v = (s.qkv[i, :, at(n)] for n in range(3))
        z = jnp.zeros_like(q)
        tot = None
        for h in range(2):
            mine = lane if h == 0 else jnp.logical_not(lane)
            sw = jnp.where(keep, nt(jnp.where(mine, q, z), k), 0.0).astype(BF)
            s.sw[i, 2 * p + h] = sw
            part = mm(sw, jnp.where(mine, v, z))
            tot = part if tot is None else tot + part
        s.an[i, :, at(0)] = tot
        return c

    loop(features // (2 * HD), pair)

    def gate(r, c):
        a = s.an[i, rows(r), :]
        sc = lax.rsqrt(jnp.mean(a * a, -1, keepdims=True) + 1e-6)
        an = a * sc
        g = s.wide_a[rows(r), :]
        sg = sigmoid(g)
        act = g * sg
        s.an[i, rows(r), :] = an
        s.ra[i, rows(r), :] = wide(sc)
        s.act[i, rows(r), :] = act
        s.dact[i, rows(r), :] = sg + act * (1.0 - sg)
        s.gated[trow(r), :] = (an * act).astype(BF)
        return c

    loop(length // R, gate)
    loaded("wo")
    s.branch[i] = mm(s.gated[tok, :], s.wo[...])

    def second_norm(r, c):
        v = s.inflow[i, rows(r), :].astype(F32) + mod[2:3, :] * s.branch[i, rows(r), :]
        n, sc = stats(v)
        s.hid[rows(r), :] = v
        s.n2[i, rows(r), :] = n
        s.r2[i, rows(r), :] = wide(sc)
        s.m2[trow(r), :] = (n * (1.0 + mod[4:5, :]) + mod[3:4, :]).astype(BF)
        return c

    loop(length // R, second_norm)
    loaded("wu")
    loaded("wd")
    width = 256
    s.ffn[i] = jnp.zeros((length, features), F32)

    def feed(c, carry):
        at = pl.ds(pl.multiple_of(c * width, width), width)
        h = mm(s.m2[tok, :], s.wu[:, at])
        k0, k1 = 0.7978845608028654, 0.044715
        hh = h * h
        t = jnp.tanh(h * (k0 + (k0 * k1) * hh))
        half = 0.5 * (1.0 + t)
        a = (h * half).astype(BF)
        s.ha[tok, at] = a
        s.dgelu[i, :, at] = half + (0.5 * h) * (1.0 - t * t) * (k0 + (3 * k0 * k1) * hh)
        s.ffn[i] += mm(a, s.wd[at, :])
        return carry

    loop(hidden // width, feed)

    def last(r, c):
        s.result[i, rows(r), :] = (s.hid[rows(r), :] + mod[5:6, :] * s.ffn[i, rows(r), :]).astype(BF)
        return c

    loop(length // R, last)


def backward(s, i, second, count, hook):
    length, features = s.inflow.shape[1:]
    hidden = s.wu.shape[1]
    mod, dmod, up = s.mod.at[i], s.dmod.at[i], s.ups.at[i]
    tok = pl.ds(pl.multiple_of(i * length, length), length)

    def trow(r):
        return pl.ds(pl.multiple_of(i * length + r * R, R), R)

    def place(r):
        return r * R + lax.broadcasted_iota(jnp.int32, (R, 1), 0)

    zero = jnp.zeros((8, features), F32)

    def start(r, acc):
        u = up[rows(r), :].astype(F32)
        s.dffn[trow(r), :] = (mod[5:6, :] * u).astype(BF)
        return acc + fold(u * s.ffn[i, rows(r), :])

    acc = loop(length // R, start, zero)
    dmod[5:6, :] = jnp.sum(acc, 0, keepdims=True)
    hook("down")
    width = 256
    s.wide_a[...] = jnp.zeros((length, features), F32)

    def feed(c, carry):
        at = pl.ds(pl.multiple_of(c * width, width), width)
        d = nt(s.dffn[tok, :], s.wd[at, :])
        dp = (d * s.dgelu[i, :, at]).astype(BF)
        s.dpre[tok, at] = dp
        s.wide_a[...] += nt(dp, s.wu[:, at])
        return carry

    loop(hidden // width, feed)
    hook("up")

    def mid(r, acc):
        dm = s.wide_a[rows(r), :]
        n = s.n2[i, rows(r), :]
        dh = up[rows(r), :].astype(F32) + norm_back(
            dm * (1.0 + mod[4:5, :]), n, s.r2[i, rows(r), :][:, :1]
        )
        s.hid[rows(r), :] = dh
        s.dbr[trow(r), :] = (mod[2:3, :] * dh).astype(BF)
        new = (fold(dm), fold(dm * n), fold(dh * s.branch[i, rows(r), :]))
        return tuple(a + b for a, b in zip(acc, new))

    acc = loop(length // R, mid, (zero,) * 3)
    for k, a in zip((3, 4, 2), acc):
        dmod[k : k + 1, :] = jnp.sum(a, 0, keepdims=True)
    hook("out")
    s.wide_a[...] = nt(s.dbr[tok, :], s.wo[...])

    def gate(r, c):
        dg = s.wide_a[rows(r), :]
        an = s.an[i, rows(r), :]
        dn = dg * s.act[i, rows(r), :]
        s.dproj[trow(r), 3 * features :] = (dg * an * s.dact[i, rows(r), :]).astype(BF)
        da = s.ra[i, rows(r), :][:, :1] * (dn - an * jnp.mean(dn * an, -1, keepdims=True))
        s.datt[rows(r), :] = da.astype(BF)
        return c

    loop(length // R, gate)
    hook("attend")
    keep = triangle(second, length)
    lane = lax.broadcasted_iota(jnp.int32, (length, 2 * HD), 1) < HD

    def pair(p, c):
        def at(k):
            return pl.ds(pl.multiple_of(k * features + p * 2 * HD, 2 * HD), 2 * HD)

        q, k, v = (s.qkv[i, :, at(n)] for n in range(3))
        g = s.datt[:, at(0)]
        z = jnp.zeros_like(q)
        dq = dk = dv = None
        for h in range(2):
            mine = lane if h == 0 else jnp.logical_not(lane)
            gm = jnp.where(mine, g, z)
            ds = jnp.where(keep, nt(gm, v), 0.0).astype(BF)
            a = mm(ds, jnp.where(mine, k, z))
            b = tn(ds, jnp.where(mine, q, z))
            e = tn(s.sw[i, 2 * p + h], gm)
            dq = a if dq is None else dq + a
            dk = b if dk is None else dk + b
            dv = e if dv is None else dv + e
        s.dproj[tok, at(0)] = (dq * SCALE).astype(BF)
        s.dproj[tok, at(1)] = dk.astype(BF)
        s.dproj[tok, at(2)] = dv.astype(BF)
        return c

    loop(features // (2 * HD), pair)
    hook("proj")
    s.dcv[8 : length + 8, :] = nt(s.dproj[tok, :], s.wp[...])

    def mask_rows(r, c):
        at = pl.ds(pl.multiple_of(r * R + 8, 8), R)
        s.dcv[at, :] = jnp.where(place(r) < count, s.dcv[at, :], 0.0)
        return c

    loop(length // R, mask_rows)

    def conv(second):
        def one(r, acc):
            dbuf = s.dcv[rows(r, 16), :]
            mbuf = s.mixed[i, rows(r, 16), :]
            here = dbuf[8 : 8 + R]
            d = jnp.zeros((R, features), F32)
            taps = []
            for j in range(TAPS):
                lo, hi = (8 + j, 8 - j) if second else (8 - j, 8 + j)
                d = d + s.wc[j : j + 1, :].astype(F32) * dbuf[hi : hi + R]
                taps.append(fold(here * mbuf[lo : lo + R]))
            d = jnp.where(place(r) < count, d, 0.0)
            n = s.n1[i, rows(r), :]
            res = s.hid[rows(r), :] + norm_back(
                d * (1.0 + mod[1:2, :]), n, s.r1[i, rows(r), :][:, :1]
            )
            s.dx[i, rows(r), :] = res.astype(BF)
            return tuple(a + b for a, b in zip(acc, (fold(d), fold(d * n), *taps)))

        acc = loop(length // R, one, (zero,) * (2 + TAPS))
        for k in range(2):
            dmod[k : k + 1, :] = jnp.sum(acc[k], 0, keepdims=True)
        for j in range(TAPS):
            s.dwc[j : j + 1, :] += jnp.sum(acc[2 + j], 0, keepdims=True)

    pl.when(jnp.logical_not(second))(lambda: conv(False))
    pl.when(second)(lambda: conv(True))


NAMES = ("down", "up", "out", "proj")
ORDER = (0, 1, 2, 3)


def spot(chunk):
    p = 0
    for bit in ORDER:
        p = 2 * p + ((chunk >> bit) & 1)
    return p


class Halving:
    def __init__(self, s, name, section, spread, me):
        self.g = getattr(s, "g_" + name)
        self.got = [getattr(s, f"got{k}_" + name) for k in range(4)]
        self.sent = getattr(s, "sent_" + name)
        self.fin = getattr(s, "fin_" + name)
        index = NAMES.index(name)
        self.send_sem = [s.rs_send.at[index, k] for k in range(4)]
        self.recv_sem = [s.rs_recv.at[index, k] for k in range(4)]
        height = self.g.shape[0]
        low = 0
        self.keep, self.give, self.peer = [], [], []
        self.bit = [lax.rem(lax.div(me, 1 << b), 2) for b in ORDER]
        for k, b in enumerate(ORDER):
            half = height >> (k + 1)
            step = half if half % 16 == 0 else 8
            self.keep.append(pl.multiple_of(low + self.bit[k] * half, step))
            self.give.append(pl.multiple_of(low + (1 - self.bit[k]) * half, step))
            low = self.keep[-1]
            other = me + (1 - 2 * self.bit[k]) * (1 << b)
            self.peer.append((section, spread(other)))

    def copy(self, k):
        half = self.g.shape[0] >> (k + 1)
        src = self.sent if k == 3 else self.g.at[pl.ds(self.give[k], half)]
        return pltpu.make_async_remote_copy(
            src_ref=src,
            dst_ref=self.got[k],
            send_sem=self.send_sem[k],
            recv_sem=self.recv_sem[k],
            device_id=self.peer[k],
            device_id_type=MESH,
        )

    def start(self, k):
        self.copy(k).start()

    def add(self, k):
        self.copy(k).wait_recv()
        height, got = self.g.shape[0], self.got[k]
        if k < 2:
            part = height // 8
            n = (height >> (k + 1)) // part

            def one(r, c):
                at = pl.ds(pl.multiple_of(self.keep[k] + r * part, 16), part)
                self.g[at, :] = (
                    self.g[at, :].astype(F32)
                    + got[pl.ds(pl.multiple_of(r * part, 16), part), :].astype(F32)
                ).astype(BF)
                return c

            loop(n, one)
        elif k == 2:
            part = height // 16
            v = self.g[pl.ds(self.keep[2], 2 * part), :].astype(F32) + got[...].astype(F32)
            upper = self.bit[3] == 1
            self.sent[...] = jnp.where(upper, v[:part], v[part:]).astype(BF)
            self.fin[...] = jnp.where(upper, v[part:], v[:part])
        else:
            self.fin[...] += got[...].astype(F32)

    def step(self, k):
        self.add(k)
        if k < 3:
            self.start(k + 1)

    def end(self):
        for k in range(4):
            self.copy(k).wait_send()


def group_rows(val, chunks):
    height = val.shape[0] // chunks
    order = [0] * chunks
    for c in range(chunks):
        order[spot(c)] = c
    return jnp.concatenate([val[c * height : (c + 1) * height] for c in order], 0)


def weight_gradient(s, name):
    if name == "down":
        features = s.dffn.shape[1]
        chunk = s.g_down.shape[0] // GROUP
        per = features // chunk

        def one(c, carry):
            at = pl.ds(pl.multiple_of(c * features, features), features)
            v = tn(s.ha[:, at], s.dffn[...]).astype(BF)
            for j in range(per):
                n = c * per + j
                p = 0
                for bit in ORDER:
                    p = 2 * p + lax.rem(lax.div(n, 1 << bit), 2)
                s.g_down[pl.ds(pl.multiple_of(p * chunk, chunk), chunk), :] = v[j * chunk : (j + 1) * chunk]
            return carry

        loop(s.ha.shape[1] // features, one)
        return
    left, right, out = {
        "up": (s.m2, s.dpre, s.g_up),
        "out": (s.gated, s.dbr, s.g_out),
        "proj": (s.conv, s.dproj, s.g_proj),
    }[name]
    width = 384

    def one(c, carry):
        at = pl.ds(pl.multiple_of(c * width, width), width)
        out[:, at] = group_rows(tn(left[...], right[:, at]), GROUP).astype(BF)
        return carry

    loop(out.shape[1] // width, one)


OUTS = ("o_act", "o_dx", "o_cond", "o_ada", "o_conv", "o_proj", "o_out", "o_up", "o_down")
INS = ("patches", "condition", "count", "cotangent", "w_ada", "w_conv", "w_proj", "w_out", "w_up", "w_down")


def kernel(names, *refs):
    s = Refs(names, refs)
    section, place = lax.axis_index("section"), lax.axis_index("dp")
    stride = lax.axis_size("dp") // GROUP
    me, low = lax.div(place, stride), lax.rem(place, stride)
    first, second = section == 0, section == 1

    def spread(member):
        return member * stride + low

    partner = (1 - section, place)
    micro, length, features = s.inflow.shape

    loads = {
        "ada": (s.w_ada.at[0], s.ada),
        "cond": (s.condition, s.cond),
        "wc": (s.w_conv.at[0], s.wc),
        "wp": (s.w_proj.at[0], s.wp),
        "wo": (s.w_out.at[0], s.wo),
        "wu": (s.w_up.at[0], s.wu),
        "wd": (s.w_down.at[0], s.wd),
    }
    order = list(loads)

    def load(name):
        return pltpu.make_async_copy(*loads[name], s.load_sem.at[order.index(name)])

    def load_patches():
        return pltpu.make_async_copy(s.patches.at[:, 0], s.inflow, s.load_sem.at[len(order)])

    def load_cotangent():
        return pltpu.make_async_copy(s.cotangent.at[:, 0], s.ups, s.load_sem.at[len(order)])

    load("cond").start()
    load("ada").start()
    pl.when(first)(lambda: load_patches().start())
    for name in order[2:]:
        load(name).start()
    pl.when(second)(lambda: load_cotangent().start())

    barrier = pltpu.get_barrier_semaphore()

    def greet(j, c):
        other = lax.rem(me + j, GROUP)
        pl.semaphore_signal(barrier, 1, device_id=(section, spread(other)), device_id_type=MESH)
        return c

    lax.fori_loop(1, GROUP, greet, 0)
    pl.semaphore_signal(barrier, 1, device_id=partner, device_id_type=MESH)

    zero = jnp.zeros((8, features), F32)
    for i in range(micro):
        s.mixed[i, 0:8, :] = zero
        s.mixed[i, length + 8 :, :] = zero
    s.dcv[0:8, :] = zero
    s.dcv[length + 8 :, :] = zero
    s.dwc[...] = zero

    load("cond").wait()
    conds = [s.cond[i].astype(F32) for i in range(micro)]
    silus = [(v * sigmoid(v)).astype(BF).astype(F32) for v in conds]
    row = lax.broadcasted_iota(jnp.int32, (16, features), 0)
    act_rows = jnp.where(
        row < 6,
        jnp.broadcast_to(silus[0], (16, features)),
        jnp.where(row < 12, jnp.broadcast_to(silus[1], (16, features)), 0.0),
    ).astype(BF)
    s.own_act[...] = act_rows
    load("ada").wait()
    for k in range(6):
        m = mm(act_rows, s.ada[:, k * features : (k + 1) * features])
        for i in range(micro):
            s.mod[i, k : k + 1, :] = m[6 * i : 6 * i + 1, :]

    def result_copy(i):
        return pltpu.make_async_remote_copy(
            src_ref=s.result.at[i],
            dst_ref=s.inflow.at[i],
            send_sem=s.hop_send.at[i],
            recv_sem=s.hop_recv.at[i],
            device_id=partner,
            device_id_type=MESH,
        )

    def dx_copy(i):
        return pltpu.make_async_remote_copy(
            src_ref=s.dx.at[i],
            dst_ref=s.ups.at[i],
            send_sem=s.hop_send.at[i],
            recv_sem=s.hop_recv.at[i],
            device_id=partner,
            device_id_type=MESH,
        )

    def result_out(i):
        return pltpu.make_async_copy(s.result.at[i], s.o_act.at[0, i, 0], s.out_sem.at[i])

    def dx_out(i):
        return pltpu.make_async_copy(s.dx.at[i], s.o_dx.at[0, i, 0], s.out_sem.at[2 + i])

    def gather_copy(j, src, dst, send, recv):
        other = lax.rem(me + j, GROUP)
        return pltpu.make_async_remote_copy(
            src_ref=src,
            dst_ref=dst.at[me],
            send_sem=send.at[j],
            recv_sem=recv.at[me],
            device_id=(section, spread(other)),
            device_id_type=MESH,
        )

    def gathered(j, src, dst, send, recv):
        other = lax.rem(me + j, GROUP)
        return pltpu.make_async_remote_copy(
            src_ref=src,
            dst_ref=dst.at[other],
            send_sem=send.at[j],
            recv_sem=recv.at[other],
            device_id=(section, spread(other)),
            device_id_type=MESH,
        )

    acts = (s.own_act, s.all_act, s.act_send, s.act_recv)
    mods = (s.own_mod, s.all_mod, s.mod_send, s.mod_recv)

    def each_peer(fn):
        def one(j, c):
            fn(j)
            return c

        lax.fori_loop(1, GROUP, one, 0)

    def do_forward(i, c):
        @pl.when(jnp.logical_and(first, i == 0))
        def _():
            load_patches().wait()

        pl.when(second)(lambda: result_copy(i).wait_recv())

        def loaded(name):
            pl.when(i == 0)(lambda: load(name).wait())

        @pl.when(jnp.logical_and(second, i == 0))
        def _():
            load_cotangent().wait()

        forward(s, i, second, s.count[i, 0], loaded)
        result_out(i).start()
        pl.when(first)(lambda: result_copy(i).start())
        return c

    pl.semaphore_wait(barrier, GROUP)
    each_peer(lambda j: gather_copy(j, *acts).start())
    loop(micro, do_forward)

    jobs = {name: Halving(s, name, section, spread, me) for name in NAMES}

    def do_backward(i, c):
        pl.when(first)(lambda: dx_copy(i).wait_recv())

        def hook(name):
            @pl.when(i == micro - 1)
            def _():
                if name in jobs:
                    weight_gradient(s, name)
                    jobs[name].start(0)
                if name == "up":
                    jobs["down"].step(0)
                if name == "attend":
                    jobs["up"].step(0)
                    jobs["out"].step(0)
                if name == "proj":
                    jobs["down"].step(1)

        backward(s, i, second, s.count[i, 0], hook)
        pl.when(second)(lambda: dx_copy(i).start())
        dx_out(i).start()
        return c

    loop(micro, do_backward)

    for i in range(micro):
        for k in range(6):
            s.stage[6 * i + k : 6 * i + k + 1, :] = s.dmod[i, k : k + 1, :]
    s.stage[12 : 12 + TAPS, :] = s.dwc[0:TAPS, :]
    s.stage[15:16, :] = jnp.zeros((1, features), F32)
    own = s.stage[...].astype(BF)
    s.own_mod[...] = own
    each_peer(lambda j: gather_copy(j, *mods).start())
    jobs["proj"].step(0)

    tot = jnp.zeros((16, features), F32)
    for k in range(6):
        part = nt(own, s.ada[:, k * features : (k + 1) * features])
        tot = tot + jnp.where(jnp.logical_or(row == k, row == 6 + k), part, 0.0)
    for i in range(micro):
        sg = sigmoid(conds[i])
        slope = sg + conds[i] * sg * (1.0 - sg)
        s.own_cond[i, :, :] = jnp.sum(tot[6 * i : 6 * i + 6], 0, keepdims=True) * slope
    cond_copy = pltpu.make_async_remote_copy(
        src_ref=s.own_cond,
        dst_ref=s.got_cond,
        send_sem=s.cond_sem.at[0],
        recv_sem=s.cond_sem.at[1],
        device_id=partner,
        device_id_type=MESH,
    )
    cond_copy.start()
    jobs["up"].step(1)
    jobs["out"].step(1)
    jobs["down"].step(2)
    jobs["proj"].step(1)
    jobs["up"].step(2)
    jobs["out"].step(2)
    jobs["down"].step(3)
    jobs["proj"].step(2)
    jobs["up"].step(3)
    jobs["out"].step(3)

    s.all_act[me] = act_rows
    s.all_mod[me] = own
    each_peer(lambda j: gathered(j, *acts).wait_recv())
    each_peer(lambda j: gathered(j, *mods).wait_recv())
    chunk = features // GROUP
    n_rows = GROUP * 16
    flat_act = s.all_act[...].reshape(n_rows, features)
    flat_mod = s.all_mod[...].reshape(n_rows, features)
    pick = (
        lax.broadcasted_iota(jnp.int32, (chunk, features), 1)
        == me * chunk + lax.broadcasted_iota(jnp.int32, (chunk, features), 0)
    ).astype(F32).astype(BF)
    left = nt(pick, flat_act)
    lane = lax.rem(lax.broadcasted_iota(jnp.int32, (chunk, n_rows), 1), 16)
    for k in range(6):
        mine = jnp.logical_or(lane == k, lane == 6 + k)
        s.fin_ada[:, k * features : (k + 1) * features] = mm(
            jnp.where(mine, left, 0.0).astype(BF), flat_mod
        )
    picked = nt(flat_mod, pick).astype(BF)
    tap = lax.broadcasted_iota(jnp.int32, (8, n_rows), 0)
    at_tap = lax.rem(lax.broadcasted_iota(jnp.int32, (8, n_rows), 1), 16) == 12 + tap
    sums = mm(jnp.where(jnp.logical_and(at_tap, tap < TAPS), 1.0, 0.0).astype(BF), picked)
    s.fin_conv[...] = sums[0:TAPS, :]

    cond_copy.wait()
    s.fin_cond[...] = s.own_cond[...] + s.got_cond[...]
    jobs["proj"].step(3)

    outs = [
        (s.fin_cond, s.o_cond),
        (s.fin_ada, s.o_ada.at[0]),
        (s.fin_conv, s.o_conv.at[0]),
        (s.fin_proj, s.o_proj.at[0]),
        (s.fin_out, s.o_out.at[0]),
        (s.fin_up, s.o_up.at[0]),
        (s.fin_down, s.o_down.at[0]),
    ]
    copies = [pltpu.make_async_copy(a, b, s.out_sem.at[4 + n]) for n, (a, b) in enumerate(outs)]
    for c in copies:
        c.start()
    for i in range(micro):
        result_out(i).wait()
        dx_out(i).wait()
        pl.when(first)(lambda i=i: result_copy(i).wait_send())
        pl.when(second)(lambda i=i: dx_copy(i).wait_send())
    for job in jobs.values():
        job.end()
    each_peer(lambda j: gather_copy(j, *acts).wait_send())
    each_peer(lambda j: gather_copy(j, *mods).wait_send())
    for c in copies:
        c.wait()


def body(patches, condition, valid_count, cotangent, ada_weight, conv_weight, proj_weight, out_weight, up_weight, down_weight):
    micro, images, length, features = patches.shape
    hidden = up_weight.shape[2]
    heads = features // HD
    tokens = micro * length
    chunk, deep = features // GROUP, hidden // GROUP
    arrays = dict(
        ada=((features, 6 * features), BF),
        cond=((micro, 1, features), BF),
        wc=((TAPS, features), BF),
        wp=((features, 4 * features), BF),
        wo=((features, features), BF),
        wu=((features, hidden), BF),
        wd=((hidden, features), BF),
        inflow=((micro, length, features), BF),
        ups=((micro, length, features), BF),
        result=((micro, length, features), BF),
        dx=((micro, length, features), BF),
        mod=((micro, 8, features), F32),
        dmod=((micro, 8, features), F32),
        dwc=((8, features), F32),
        n1=((micro, length, features), F32),
        r1=((micro, length, 128), F32),
        mixed=((micro, length + 16, features), F32),
        conv=((tokens, features), BF),
        qkv=((micro, length, 3 * features), BF),
        sw=((micro, heads, length, length), BF),
        an=((micro, length, features), F32),
        ra=((micro, length, 128), F32),
        act=((micro, length, features), F32),
        dact=((micro, length, features), F32),
        gated=((tokens, features), BF),
        branch=((micro, length, features), F32),
        hid=((length, features), F32),
        wide_a=((length, features), F32),
        n2=((micro, length, features), F32),
        r2=((micro, length, 128), F32),
        m2=((tokens, features), BF),
        ffn=((micro, length, features), F32),
        ha=((tokens, hidden), BF),
        dgelu=((micro, length, hidden), F32),
        dffn=((tokens, features), BF),
        dpre=((tokens, hidden), BF),
        dbr=((tokens, features), BF),
        datt=((length, features), BF),
        dproj=((tokens, 4 * features), BF),
        dcv=((length + 16, features), F32),
        own_act=((16, features), BF),
        all_act=((GROUP, 16, features), BF),
        own_mod=((16, features), BF),
        all_mod=((GROUP, 16, features), BF),
        stage=((16, features), F32),
        own_cond=((micro, 1, features), F32),
        got_cond=((micro, 1, features), F32),
        fin_cond=((micro, 1, features), F32),
        fin_ada=((chunk, 6 * features), F32),
        fin_conv=((TAPS, chunk), F32),
    )
    for name, (height, width) in dict(
        down=(hidden, features), up=(features, hidden), out=(features, features), proj=(features, 4 * features)
    ).items():
        arrays["g_" + name] = ((height, width), BF)
        for k in range(4):
            arrays[f"got{k}_{name}"] = ((height >> (k + 1), width), BF)
        arrays["sent_" + name] = ((height // 16, width), BF)
        arrays["fin_" + name] = ((height // 16, width), F32)
    sems = dict(
        load_sem=(8,),
        hop_send=(2,),
        hop_recv=(2,),
        out_sem=(11,),
        rs_send=(4, 4),
        rs_recv=(4, 4),
        act_send=(GROUP,),
        act_recv=(GROUP,),
        mod_send=(GROUP,),
        mod_recv=(GROUP,),
        cond_sem=(2,),
    )
    names = (*INS, *OUTS, *arrays, *sems)
    any_spec = pl.BlockSpec(memory_space=pl.ANY)
    out_shape = (
        ((1, micro, 1, length, features), BF),
        ((1, micro, 1, length, features), BF),
        ((micro, 1, features), F32),
        ((1, chunk, 6 * features), F32),
        ((1, TAPS, chunk), F32),
        ((1, chunk, 4 * features), F32),
        ((1, chunk, features), F32),
        ((1, chunk, hidden), F32),
        ((1, deep, features), F32),
    )
    outs = pl.pallas_call(
        lambda *refs: kernel(names, *refs),
        out_shape=[jax.ShapeDtypeStruct(*o) for o in out_shape],
        in_specs=[pl.BlockSpec(memory_space=pltpu.SMEM) if n == "count" else any_spec for n in INS],
        out_specs=[any_spec] * len(OUTS),
        scratch_shapes=[pltpu.VMEM(*a) for a in arrays.values()]
        + [pltpu.SemaphoreType.DMA(n) for n in sems.values()],
        compiler_params=pltpu.CompilerParams(
            collective_id=0, has_side_effects=True, vmem_limit_bytes=60000 * 1024
        ),
        name="relay",
    )(patches, condition, valid_count, cotangent, ada_weight, conv_weight, proj_weight, out_weight, up_weight, down_weight)
    stride = lax.axis_size("dp") // GROUP
    if stride > 1:
        teams = [[t * stride + j for j in range(stride)] for t in range(GROUP)]
        outs = [
            lax.psum_scatter(o, "dp", scatter_dimension=2 if n == 4 else 1, axis_index_groups=teams, tiled=True)
            if n >= 3
            else o
            for n, o in enumerate(outs)
        ]
    return tuple(outs)


def solution(mesh):
    by_section = P("section", None, None)
    placed = (
        P(None, "dp", None, None),
        P(None, "dp", None),
        P(None, "dp"),
        P(None, "dp", None, None),
        *(by_section,) * 6,
    )
    rows_out = P("section", "dp", None)
    return jax.shard_map(
        body,
        mesh=mesh,
        in_specs=placed,
        out_specs=(
            P("section", None, "dp", None, None),
            P("section", None, "dp", None, None),
            P(None, "dp", None),
            rows_out,
            P("section", None, "dp"),
            rows_out,
            rows_out,
            rows_out,
            rows_out,
        ),
        check_vma=False,
    )
```

```python
import jax
import jax.numpy as jnp
from jax import lax
from jax.experimental import pallas as pl
from jax.experimental.pallas import tpu as pltpu
from jax.sharding import PartitionSpec as P

F32, BF = jnp.float32, jnp.bfloat16
HD = 64
TAPS = 3
GROUP = 16
R = 64
MESH = pl.DeviceIdType.MESH
SCALE = HD**-0.5


def mm(a, b):
    return jnp.dot(a, b, preferred_element_type=F32)


def nt(a, b):
    return lax.dot_general(a, b, (((1,), (1,)), ((), ())), preferred_element_type=F32)


def tn(a, b):
    return lax.dot_general(a, b, (((0,), (0,)), ((), ())), preferred_element_type=F32)


def fold(v):
    return jnp.sum(v.reshape(v.shape[0] // 8, 8, v.shape[1]), 0)


def wide(col):
    return jnp.broadcast_to(col, (col.shape[0], 128))


def sigmoid(v):
    return 1.0 / (1.0 + jnp.exp(-v))


def stats(v):
    c = v - jnp.mean(v, -1, keepdims=True)
    s = lax.rsqrt(jnp.mean(c * c, -1, keepdims=True) + 1e-6)
    return c * s, s


def norm_back(g, n, s):
    return s * (g - jnp.mean(g, -1, keepdims=True) - n * jnp.mean(g * n, -1, keepdims=True))


def rows(r, extra=0):
    return pl.ds(r * R, R + extra)


def steps(n, body, init=0):
    for r in range(n):
        init = body(r, init)
    return init


def loop(n, body, init=0):
    return lax.fori_loop(0, n, body, init)


class Refs:
    def __init__(self, names, refs):
        self.__dict__.update(zip(names, refs, strict=True))


def triangle(second, length):
    sign = jnp.where(second, -1, 1)
    query = lax.broadcasted_iota(jnp.int32, (length, length), 0)
    key = lax.broadcasted_iota(jnp.int32, (length, length), 1)
    return (query - key) * sign >= 0


def shifted(buf, j, second):
    return jnp.where(second, buf[8 + j : 8 + j + R], buf[8 - j : 8 - j + R])


def forward(s, i, second, count, loaded):
    length, features = s.inflow.shape[1:]
    hidden = s.wu.shape[1]
    mod = s.mod.at[i]
    tok = pl.ds(pl.multiple_of(i * length, length), length)

    def trow(r):
        return pl.ds(pl.multiple_of(i * length + r * R, R), R)

    def place(r):
        return r * R + lax.broadcasted_iota(jnp.int32, (R, 1), 0)

    def first_norm(r, c):
        n, sc = stats(s.inflow[i, rows(r), :].astype(F32))
        s.n1[i, rows(r), :] = n
        s.r1[i, rows(r), :] = wide(sc)
        m = jnp.where(place(r) < count, n * (1.0 + mod[1:2, :]) + mod[0:1, :], 0.0)
        s.mixed[i, pl.ds(r * R + 8, R), :] = m
        return c

    steps(length // R, first_norm)
    loaded("wc")

    def conv(r, c):
        buf = s.mixed[i, rows(r, 16), :]
        v = s.wc[0:1, :].astype(F32) * buf[8 : 8 + R]
        for j in range(1, TAPS):
            v = v + s.wc[j : j + 1, :].astype(F32) * shifted(buf, j, second)
        s.conv[trow(r), :] = jnp.where(place(r) < count, v, 0.0).astype(BF)
        return c

    steps(length // R, conv)
    loaded("wp")
    cv = s.conv[tok, :]
    for c in range(3):
        p = mm(cv, s.wp[:, c * features : (c + 1) * features])
        s.qkv[i, :, c * features : (c + 1) * features] = (p * SCALE if c == 0 else p).astype(BF)
    s.wide_a[...] = mm(cv, s.wp[:, 3 * features :])
    keep = triangle(second, length)
    lane = lax.broadcasted_iota(jnp.int32, (length, 2 * HD), 1) < HD

    def pair(p, c):
        def at(k):
            return pl.ds(k * features + p * 2 * HD, 2 * HD)

        q, k, v = (s.qkv[i, :, at(n)] for n in range(3))
        z = jnp.zeros_like(q)
        tot = None
        for h in range(2):
            mine = lane if h == 0 else jnp.logical_not(lane)
            sw = jnp.where(keep, nt(jnp.where(mine, q, z), k), 0.0).astype(BF)
            s.sw[i, 2 * p + h] = sw
            part = mm(sw, jnp.where(mine, v, z))
            tot = part if tot is None else tot + part
        s.an[i, :, at(0)] = tot
        return c

    steps(features // (2 * HD), pair)

    def gate(r, c):
        a = s.an[i, rows(r), :]
        sc = lax.rsqrt(jnp.mean(a * a, -1, keepdims=True) + 1e-6)
        an = a * sc
        g = s.wide_a[rows(r), :]
        sg = sigmoid(g)
        act = g * sg
        s.an[i, rows(r), :] = an
        s.ra[i, rows(r), :] = wide(sc)
        s.act[i, rows(r), :] = act
        s.dact[i, rows(r), :] = sg + act * (1.0 - sg)
        s.gated[trow(r), :] = (an * act).astype(BF)
        return c

    steps(length // R, gate)
    loaded("wo")
    s.branch[i] = mm(s.gated[tok, :], s.wo[...])

    def second_norm(r, c):
        v = s.inflow[i, rows(r), :].astype(F32) + mod[2:3, :] * s.branch[i, rows(r), :]
        n, sc = stats(v)
        s.hid[rows(r), :] = v
        s.n2[i, rows(r), :] = n
        s.r2[i, rows(r), :] = wide(sc)
        s.m2[trow(r), :] = (n * (1.0 + mod[4:5, :]) + mod[3:4, :]).astype(BF)
        return c

    steps(length // R, second_norm)
    loaded("wu")
    loaded("wd")
    width = 256

    def feed(c, carry):
        at = pl.ds(c * width, width)
        h = mm(s.m2[tok, :], s.wu[:, at])
        k0, k1 = 0.7978845608028654, 0.044715
        hh = h * h
        t = jnp.tanh(h * (k0 + (k0 * k1) * hh))
        half = 0.5 * (1.0 + t)
        a = (h * half).astype(BF)
        s.ha[tok, at] = a
        s.dgelu[i, :, at] = half + (0.5 * h) * (1.0 - t * t) * (k0 + (3 * k0 * k1) * hh)
        return carry

    steps(hidden // width, feed)
    s.ffn[i] = mm(s.ha[tok, :], s.wd[...])

    def last(r, c):
        s.result[i, rows(r), :] = (s.hid[rows(r), :] + mod[5:6, :] * s.ffn[i, rows(r), :]).astype(BF)
        return c

    steps(length // R, last)


def backward(s, i, second, count, hook):
    length, features = s.inflow.shape[1:]
    hidden = s.wu.shape[1]
    mod, dmod, up = s.mod.at[i], s.dmod.at[i], s.ups.at[i]
    tok = pl.ds(pl.multiple_of(i * length, length), length)

    def trow(r):
        return pl.ds(pl.multiple_of(i * length + r * R, R), R)

    def place(r):
        return r * R + lax.broadcasted_iota(jnp.int32, (R, 1), 0)

    zero = jnp.zeros((8, features), F32)

    def start(r, acc):
        u = up[rows(r), :].astype(F32)
        s.dffn[trow(r), :] = (mod[5:6, :] * u).astype(BF)
        return acc + fold(u * s.ffn[i, rows(r), :])

    acc = steps(length // R, start, zero)
    dmod[5:6, :] = jnp.sum(acc, 0, keepdims=True)
    hook("down")
    width = 256

    def feed(c, carry):
        at = pl.ds(c * width, width)
        d = nt(s.dffn[tok, :], s.wd[at, :])
        dp = (d * s.dgelu[i, :, at]).astype(BF)
        s.dpre[tok, at] = dp
        return carry

    steps(hidden // width, feed)
    s.wide_a[...] = nt(s.dpre[tok, :], s.wu[...])
    hook("up")

    def mid(r, acc):
        dm = s.wide_a[rows(r), :]
        n = s.n2[i, rows(r), :]
        dh = up[rows(r), :].astype(F32) + norm_back(
            dm * (1.0 + mod[4:5, :]), n, s.r2[i, rows(r), :][:, :1]
        )
        s.hid[rows(r), :] = dh
        s.dbr[trow(r), :] = (mod[2:3, :] * dh).astype(BF)
        new = (fold(dm), fold(dm * n), fold(dh * s.branch[i, rows(r), :]))
        return tuple(a + b for a, b in zip(acc, new))

    acc = steps(length // R, mid, (zero,) * 3)
    for k, a in zip((3, 4, 2), acc):
        dmod[k : k + 1, :] = jnp.sum(a, 0, keepdims=True)
    hook("out")
    s.wide_a[...] = nt(s.dbr[tok, :], s.wo[...])

    def gate(r, c):
        dg = s.wide_a[rows(r), :]
        an = s.an[i, rows(r), :]
        dn = dg * s.act[i, rows(r), :]
        s.dproj[trow(r), 3 * features :] = (dg * an * s.dact[i, rows(r), :]).astype(BF)
        da = s.ra[i, rows(r), :][:, :1] * (dn - an * jnp.mean(dn * an, -1, keepdims=True))
        s.datt[rows(r), :] = da.astype(BF)
        return c

    steps(length // R, gate)
    hook("attend")
    keep = triangle(second, length)
    lane = lax.broadcasted_iota(jnp.int32, (length, 2 * HD), 1) < HD

    def pair(p, c):
        def at(k):
            return pl.ds(k * features + p * 2 * HD, 2 * HD)

        q, k, v = (s.qkv[i, :, at(n)] for n in range(3))
        g = s.datt[:, at(0)]
        z = jnp.zeros_like(q)
        dq = dk = dv = None
        for h in range(2):
            mine = lane if h == 0 else jnp.logical_not(lane)
            gm = jnp.where(mine, g, z)
            ds = jnp.where(keep, nt(gm, v), 0.0).astype(BF)
            a = mm(ds, jnp.where(mine, k, z))
            b = tn(ds, jnp.where(mine, q, z))
            e = tn(s.sw[i, 2 * p + h], gm)
            dq = a if dq is None else dq + a
            dk = b if dk is None else dk + b
            dv = e if dv is None else dv + e
        s.dproj[tok, at(0)] = (dq * SCALE).astype(BF)
        s.dproj[tok, at(1)] = dk.astype(BF)
        s.dproj[tok, at(2)] = dv.astype(BF)
        return c

    steps(features // (2 * HD), pair)
    hook("proj")
    s.dcv[8 : length + 8, :] = nt(s.dproj[tok, :], s.wp[...])

    def mask_rows(r, c):
        at = pl.ds(r * R + 8, R)
        s.dcv[at, :] = jnp.where(place(r) < count, s.dcv[at, :], 0.0)
        return c

    steps(length // R, mask_rows)

    def conv(r, acc):
        dbuf = s.dcv[rows(r, 16), :]
        mbuf = s.mixed[i, rows(r, 16), :]
        here = dbuf[8 : 8 + R]
        d = s.wc[0:1, :].astype(F32) * here
        taps = [fold(here * mbuf[8 : 8 + R])]
        for j in range(1, TAPS):
            d = d + s.wc[j : j + 1, :].astype(F32) * shifted(dbuf, j, jnp.logical_not(second))
            taps.append(fold(here * shifted(mbuf, j, second)))
        d = jnp.where(place(r) < count, d, 0.0)
        n = s.n1[i, rows(r), :]
        res = s.hid[rows(r), :] + norm_back(d * (1.0 + mod[1:2, :]), n, s.r1[i, rows(r), :][:, :1])
        s.dx[i, rows(r), :] = res.astype(BF)
        return tuple(a + b for a, b in zip(acc, (fold(d), fold(d * n), *taps)))

    acc = steps(length // R, conv, (zero,) * (2 + TAPS))
    for k in range(2):
        dmod[k : k + 1, :] = jnp.sum(acc[k], 0, keepdims=True)
    for j in range(TAPS):
        s.dwc[j : j + 1, :] += jnp.sum(acc[2 + j], 0, keepdims=True)


NAMES = ("down", "up", "out", "proj")
ORDER = (0, 1, 2, 3)


def spot(chunk):
    p = 0
    for bit in ORDER:
        p = 2 * p + ((chunk >> bit) & 1)
    return p


class Halving:
    def __init__(self, s, name, section, spread, me):
        self.g = getattr(s, "g_" + name)
        self.got = [getattr(s, f"got{k}_" + name) for k in range(4)]
        self.sent = getattr(s, "sent_" + name)
        self.fin = getattr(s, "fin_" + name)
        index = NAMES.index(name)
        self.send_sem = [s.rs_send.at[index, k] for k in range(4)]
        self.recv_sem = [s.rs_recv.at[index, k] for k in range(4)]
        height = self.g.shape[0]
        low = 0
        self.keep, self.give, self.peer = [], [], []
        self.bit = [lax.rem(lax.div(me, 1 << b), 2) for b in ORDER]
        for k, b in enumerate(ORDER):
            half = height >> (k + 1)
            step = half if half % 16 == 0 else 8
            self.keep.append(pl.multiple_of(low + self.bit[k] * half, step))
            self.give.append(pl.multiple_of(low + (1 - self.bit[k]) * half, step))
            low = self.keep[-1]
            other = me + (1 - 2 * self.bit[k]) * (1 << b)
            self.peer.append((section, spread(other)))

    def copy(self, k):
        half = self.g.shape[0] >> (k + 1)
        src = self.sent if k == 3 else self.g.at[pl.ds(self.give[k], half)]
        return pltpu.make_async_remote_copy(
            src_ref=src,
            dst_ref=self.got[k],
            send_sem=self.send_sem[k],
            recv_sem=self.recv_sem[k],
            device_id=self.peer[k],
            device_id_type=MESH,
        )

    def start(self, k):
        self.copy(k).start()

    def add(self, k):
        self.copy(k).wait_recv()
        height, got = self.g.shape[0], self.got[k]
        if k < 2:
            part = height // 8
            n = (height >> (k + 1)) // part

            def one(r, c):
                at = pl.ds(pl.multiple_of(self.keep[k] + r * part, 16), part)
                self.g[at, :] = (
                    self.g[at, :].astype(F32)
                    + got[pl.ds(pl.multiple_of(r * part, 16), part), :].astype(F32)
                ).astype(BF)
                return c

            loop(n, one)
        elif k == 2:
            part = height // 16
            v = self.g[pl.ds(self.keep[2], 2 * part), :].astype(F32) + got[...].astype(F32)
            upper = self.bit[3] == 1
            self.sent[...] = jnp.where(upper, v[:part], v[part:]).astype(BF)
            self.fin[...] = jnp.where(upper, v[part:], v[:part])
        else:
            self.fin[...] += got[...].astype(F32)

    def step(self, k):
        self.add(k)
        if k < 3:
            self.start(k + 1)

    def end(self):
        for k in range(4):
            self.copy(k).wait_send()


def group_rows(val, chunks):
    height = val.shape[0] // chunks
    order = [0] * chunks
    for c in range(chunks):
        order[spot(c)] = c
    return jnp.concatenate([val[c * height : (c + 1) * height] for c in order], 0)


def weight_gradient(s, name):
    if name == "down":
        features = s.dffn.shape[1]
        chunk = s.g_down.shape[0] // GROUP
        per = features // chunk

        def one(c, carry):
            at = pl.ds(pl.multiple_of(c * features, features), features)
            v = tn(s.ha[:, at], s.dffn[...]).astype(BF)
            for j in range(per):
                n = c * per + j
                p = 0
                for bit in ORDER:
                    p = 2 * p + lax.rem(lax.div(n, 1 << bit), 2)
                s.g_down[pl.ds(pl.multiple_of(p * chunk, chunk), chunk), :] = v[j * chunk : (j + 1) * chunk]
            return carry

        loop(s.ha.shape[1] // features, one)
        return
    left, right, out = {
        "up": (s.m2, s.dpre, s.g_up),
        "out": (s.gated, s.dbr, s.g_out),
        "proj": (s.conv, s.dproj, s.g_proj),
    }[name]
    width = 384

    def one(c, carry):
        at = pl.ds(pl.multiple_of(c * width, width), width)
        out[:, at] = group_rows(tn(left[...], right[:, at]), GROUP).astype(BF)
        return carry

    loop(out.shape[1] // width, one)


OUTS = ("o_act", "o_dx", "o_cond", "o_ada", "o_conv", "o_proj", "o_out", "o_up", "o_down")
INS = ("patches", "condition", "count", "cotangent", "w_ada", "w_conv", "w_proj", "w_out", "w_up", "w_down")


def kernel(names, *refs):
    s = Refs(names, refs)
    section, place = lax.axis_index("section"), lax.axis_index("dp")
    stride = lax.axis_size("dp") // GROUP
    me, low = lax.div(place, stride), lax.rem(place, stride)
    first, second = section == 0, section == 1

    def spread(member):
        return member * stride + low

    partner = (1 - section, place)
    micro, length, features = s.inflow.shape

    loads = {
        "ada": (s.w_ada.at[0], s.ada),
        "cond": (s.condition, s.cond),
        "wc": (s.w_conv.at[0], s.wc),
        "wp": (s.w_proj.at[0], s.wp),
        "wo": (s.w_out.at[0], s.wo),
        "wu": (s.w_up.at[0], s.wu),
        "wd": (s.w_down.at[0], s.wd),
    }
    order = list(loads)

    def load(name):
        return pltpu.make_async_copy(*loads[name], s.load_sem.at[order.index(name)])

    def load_patches():
        return pltpu.make_async_copy(s.patches.at[:, 0], s.inflow, s.load_sem.at[len(order)])

    def load_cotangent():
        return pltpu.make_async_copy(s.cotangent.at[:, 0], s.ups, s.load_sem.at[len(order)])

    load("cond").start()
    load("ada").start()
    pl.when(first)(lambda: load_patches().start())
    for name in order[2:]:
        load(name).start()
    pl.when(second)(lambda: load_cotangent().start())

    barrier = pltpu.get_barrier_semaphore()

    def greet(j, c):
        other = lax.rem(me + j, GROUP)
        pl.semaphore_signal(barrier, 1, device_id=(section, spread(other)), device_id_type=MESH)
        return c

    lax.fori_loop(1, GROUP, greet, 0)
    pl.semaphore_signal(barrier, 1, device_id=partner, device_id_type=MESH)

    zero = jnp.zeros((8, features), F32)
    for i in range(micro):
        s.mixed[i, 0:8, :] = zero
        s.mixed[i, length + 8 :, :] = zero
    s.dcv[0:8, :] = zero
    s.dcv[length + 8 :, :] = zero
    s.dwc[...] = zero

    load("cond").wait()
    conds = [s.cond[i : i + 1, :].astype(F32) for i in range(micro)]
    silus = [(v * sigmoid(v)).astype(BF).astype(F32) for v in conds]
    row = lax.broadcasted_iota(jnp.int32, (16, features), 0)
    act_rows = jnp.where(
        row < 6,
        jnp.broadcast_to(silus[0], (16, features)),
        jnp.where(row < 12, jnp.broadcast_to(silus[1], (16, features)), 0.0),
    ).astype(BF)
    s.own_act[...] = act_rows
    load("ada").wait()
    for k in range(6):
        m = mm(act_rows, s.ada[:, k * features : (k + 1) * features])
        for i in range(micro):
            s.mod[i, k : k + 1, :] = m[6 * i : 6 * i + 1, :]

    def result_copy(i):
        return pltpu.make_async_remote_copy(
            src_ref=s.result.at[i],
            dst_ref=s.inflow.at[i],
            send_sem=s.hop_send.at[i],
            recv_sem=s.hop_recv.at[i],
            device_id=partner,
            device_id_type=MESH,
        )

    def dx_copy(i):
        return pltpu.make_async_remote_copy(
            src_ref=s.dx.at[i],
            dst_ref=s.ups.at[i],
            send_sem=s.hop_send.at[i],
            recv_sem=s.hop_recv.at[i],
            device_id=partner,
            device_id_type=MESH,
        )

    def result_out(i):
        return pltpu.make_async_copy(s.result.at[i], s.o_act.at[0, i, 0], s.out_sem.at[i])

    def dx_out(i):
        return pltpu.make_async_copy(s.dx.at[i], s.o_dx.at[0, i, 0], s.out_sem.at[2 + i])

    def gather_copy(j, src, dst, send, recv):
        other = lax.rem(me + j, GROUP)
        return pltpu.make_async_remote_copy(
            src_ref=src,
            dst_ref=dst.at[me],
            send_sem=send.at[j],
            recv_sem=recv.at[me],
            device_id=(section, spread(other)),
            device_id_type=MESH,
        )

    def gathered(j, src, dst, send, recv):
        other = lax.rem(me + j, GROUP)
        return pltpu.make_async_remote_copy(
            src_ref=src,
            dst_ref=dst.at[other],
            send_sem=send.at[j],
            recv_sem=recv.at[other],
            device_id=(section, spread(other)),
            device_id_type=MESH,
        )

    acts = (s.own_act, s.all_act, s.act_send, s.act_recv)
    mods = (s.own_mod, s.all_mod, s.mod_send, s.mod_recv)

    def each_peer(fn):
        def one(j, c):
            fn(j)
            return c

        lax.fori_loop(1, GROUP, one, 0)

    def do_forward(i):
        @pl.when(jnp.logical_and(first, i == 0))
        def _():
            load_patches().wait()

        pl.when(second)(lambda: result_copy(i).wait_recv())

        def loaded(name):
            pl.when(i == 0)(lambda: load(name).wait())

        @pl.when(jnp.logical_and(second, i == 0))
        def _():
            load_cotangent().wait()

        forward(s, i, second, s.count[i], loaded)
        result_out(i).start()

        @pl.when(i == 0)
        def _():
            pl.semaphore_wait(barrier, GROUP)
            each_peer(lambda j: gather_copy(j, *acts).start())

        pl.when(first)(lambda: result_copy(i).start())

    jobs = {name: Halving(s, name, section, spread, me) for name in NAMES}

    def do_backward(i):
        pl.when(first)(lambda: dx_copy(i).wait_recv())
        last = i == micro - 1

        def hook(name):
            @pl.when(jnp.logical_and(first, last))
            def _():
                if name in jobs:
                    weight_gradient(s, name)
                    jobs[name].start(0)
                if name == "up":
                    jobs["down"].step(0)
                if name == "attend":
                    jobs["up"].step(0)
                    jobs["out"].step(0)

        backward(s, i, second, s.count[i], hook)
        dx_out(i).start()

        @pl.when(second)
        def _():
            dx_copy(i).start()

            @pl.when(last)
            def _():
                for name in NAMES:
                    weight_gradient(s, name)
                    jobs[name].start(0)
                for name in NAMES[:-1]:
                    jobs[name].step(0)

    def turn(n, c):
        ahead = jnp.logical_or(n == 0, jnp.where(first, n == 1, n == micro))
        i = jnp.where(first, lax.rem(n, micro), lax.div(n, 2))
        pl.when(ahead)(lambda: do_forward(i))
        pl.when(jnp.logical_not(ahead))(lambda: do_backward(i))
        return c

    loop(2 * micro, turn)

    for i in range(micro):
        for k in range(6):
            s.stage[6 * i + k : 6 * i + k + 1, :] = s.dmod[i, k : k + 1, :]
    s.stage[12 : 12 + TAPS, :] = s.dwc[0:TAPS, :]
    s.stage[15:16, :] = jnp.zeros((1, features), F32)
    own = s.stage[...].astype(BF)
    s.own_mod[...] = own
    each_peer(lambda j: gather_copy(j, *mods).start())
    jobs["proj"].step(0)

    tot = jnp.zeros((16, features), F32)
    for k in range(6):
        part = nt(own, s.ada[:, k * features : (k + 1) * features])
        tot = tot + jnp.where(jnp.logical_or(row == k, row == 6 + k), part, 0.0)
    for i in range(micro):
        sg = sigmoid(conds[i])
        slope = sg + conds[i] * sg * (1.0 - sg)
        s.own_cond[i, :, :] = jnp.sum(tot[6 * i : 6 * i + 6], 0, keepdims=True) * slope
    cond_copy = pltpu.make_async_remote_copy(
        src_ref=s.own_cond,
        dst_ref=s.got_cond,
        send_sem=s.cond_sem.at[0],
        recv_sem=s.cond_sem.at[1],
        device_id=partner,
        device_id_type=MESH,
    )
    cond_copy.start()
    jobs["down"].step(1)
    jobs["up"].step(1)
    jobs["out"].step(1)
    jobs["down"].step(2)
    jobs["proj"].step(1)
    jobs["up"].step(2)
    jobs["out"].step(2)
    jobs["down"].step(3)
    jobs["proj"].step(2)
    jobs["up"].step(3)
    jobs["out"].step(3)

    s.all_act[me] = act_rows
    s.all_mod[me] = own
    each_peer(lambda j: gathered(j, *acts).wait_recv())
    each_peer(lambda j: gathered(j, *mods).wait_recv())
    chunk = features // GROUP
    n_rows = GROUP * 16
    flat_act = s.all_act[...].reshape(n_rows, features)
    flat_mod = s.all_mod[...].reshape(n_rows, features)
    pick = (
        lax.broadcasted_iota(jnp.int32, (chunk, features), 1)
        == me * chunk + lax.broadcasted_iota(jnp.int32, (chunk, features), 0)
    ).astype(F32).astype(BF)
    left = nt(pick, flat_act)
    lane = lax.rem(lax.broadcasted_iota(jnp.int32, (chunk, n_rows), 1), 16)
    for k in range(6):
        mine = jnp.logical_or(lane == k, lane == 6 + k)
        s.fin_ada[:, k * features : (k + 1) * features] = mm(
            jnp.where(mine, left, 0.0).astype(BF), flat_mod
        )
    picked = nt(flat_mod, pick).astype(BF)
    tap = lax.broadcasted_iota(jnp.int32, (8, n_rows), 0)
    at_tap = lax.rem(lax.broadcasted_iota(jnp.int32, (8, n_rows), 1), 16) == 12 + tap
    sums = mm(jnp.where(jnp.logical_and(at_tap, tap < TAPS), 1.0, 0.0).astype(BF), picked)
    for j in range(TAPS):
        s.fin_conv[j, :, :] = sums[j : j + 1, :]

    cond_copy.wait()
    s.fin_cond[...] = s.own_cond[...] + s.got_cond[...]
    jobs["proj"].step(3)

    outs = [
        (s.fin_cond, s.o_cond),
        (s.fin_ada, s.o_ada.at[0]),
        (s.fin_conv, s.o_conv),
        (s.fin_proj, s.o_proj.at[0]),
        (s.fin_out, s.o_out.at[0]),
        (s.fin_up, s.o_up.at[0]),
        (s.fin_down, s.o_down.at[0]),
    ]
    copies = [pltpu.make_async_copy(a, b, s.out_sem.at[4 + n]) for n, (a, b) in enumerate(outs)]
    for c in copies:
        c.start()
    for i in range(micro):
        result_out(i).wait()
        dx_out(i).wait()
        pl.when(first)(lambda i=i: result_copy(i).wait_send())
        pl.when(second)(lambda i=i: dx_copy(i).wait_send())
    for job in jobs.values():
        job.end()
    each_peer(lambda j: gather_copy(j, *acts).wait_send())
    each_peer(lambda j: gather_copy(j, *mods).wait_send())
    for c in copies:
        c.wait()


def finish(n, *refs):
    held, given, sems = refs[:n], refs[n : 2 * n], refs[2 * n]
    outward = [pltpu.make_async_copy(a, b, sems.at[k]) for k, (a, b) in enumerate(zip(held, given))]
    for o in outward:
        o.start()
    for o in outward:
        o.wait()


def body(patches, condition, valid_count, cotangent, ada_weight, conv_weight, proj_weight, out_weight, up_weight, down_weight):
    micro, images, length, features = patches.shape
    hidden = up_weight.shape[2]
    heads = features // HD
    tokens = micro * length
    chunk, deep = features // GROUP, hidden // GROUP
    arrays = dict(
        ada=((features, 6 * features), BF),
        cond=((micro, features), BF),
        wc=((TAPS, features), BF),
        wp=((features, 4 * features), BF),
        wo=((features, features), BF),
        wu=((features, hidden), BF),
        wd=((hidden, features), BF),
        inflow=((micro, length, features), BF),
        ups=((micro, length, features), BF),
        result=((micro, length, features), BF),
        dx=((micro, length, features), BF),
        mod=((micro, 8, features), F32),
        dmod=((micro, 8, features), F32),
        dwc=((8, features), F32),
        n1=((micro, length, features), F32),
        r1=((micro, length, 128), F32),
        mixed=((micro, length + 16, features), F32),
        conv=((tokens, features), BF),
        qkv=((micro, length, 3 * features), BF),
        sw=((micro, heads, length, length), BF),
        an=((micro, length, features), F32),
        ra=((micro, length, 128), F32),
        act=((micro, length, features), F32),
        dact=((micro, length, features), F32),
        gated=((tokens, features), BF),
        branch=((micro, length, features), F32),
        hid=((length, features), F32),
        wide_a=((length, features), F32),
        n2=((micro, length, features), F32),
        r2=((micro, length, 128), F32),
        m2=((tokens, features), BF),
        ffn=((micro, length, features), F32),
        ha=((tokens, hidden), BF),
        dgelu=((micro, length, hidden), F32),
        dffn=((tokens, features), BF),
        dpre=((tokens, hidden), BF),
        dbr=((tokens, features), BF),
        datt=((length, features), BF),
        dproj=((tokens, 4 * features), BF),
        dcv=((length + 16, features), F32),
        own_act=((16, features), BF),
        all_act=((GROUP, 16, features), BF),
        own_mod=((16, features), BF),
        all_mod=((GROUP, 16, features), BF),
        stage=((16, features), F32),
        own_cond=((micro, 1, features), F32),
        got_cond=((micro, 1, features), F32),
        fin_cond=((micro, 1, features), F32),
        fin_ada=((chunk, 6 * features), F32),
        fin_conv=((TAPS, 1, chunk), F32),
    )
    for name, (height, width) in dict(
        down=(hidden, features), up=(features, hidden), out=(features, features), proj=(features, 4 * features)
    ).items():
        arrays["g_" + name] = ((height, width), BF)
        for k in range(4):
            arrays[f"got{k}_{name}"] = ((height >> (k + 1), width), BF)
        arrays["sent_" + name] = ((height // 16, width), BF)
        arrays["fin_" + name] = ((height // 16, width), F32)
    sems = dict(
        load_sem=(8,),
        hop_send=(2,),
        hop_recv=(2,),
        out_sem=(11,),
        rs_send=(4, 4),
        rs_recv=(4, 4),
        act_send=(GROUP,),
        act_recv=(GROUP,),
        mod_send=(GROUP,),
        mod_recv=(GROUP,),
        cond_sem=(2,),
    )
    names = (*INS, *OUTS, *arrays, *sems)
    any_spec = pl.BlockSpec(memory_space=pl.ANY)
    out_shape = (
        ((1, micro, 1, length, features), BF),
        ((1, micro, 1, length, features), BF),
        ((micro, 1, features), F32),
        ((1, chunk, 6 * features), F32),
        ((TAPS, 1, chunk), F32),
        ((1, chunk, 4 * features), F32),
        ((1, chunk, features), F32),
        ((1, chunk, hidden), F32),
        ((1, deep, features), F32),
    )
    outs = pl.pallas_call(
        lambda *refs: kernel(names, *refs),
        out_shape=[jax.ShapeDtypeStruct(*o) for o in out_shape],
        in_specs=[pl.BlockSpec(memory_space=pltpu.SMEM if n == "count" else pltpu.HBM) for n in INS],
        out_specs=[any_spec] * len(OUTS),
        scratch_shapes=[pltpu.VMEM(*a) for a in arrays.values()]
        + [pltpu.SemaphoreType.DMA(n) for n in sems.values()],
        compiler_params=pltpu.CompilerParams(
            collective_id=0, has_side_effects=True, vmem_limit_bytes=60000 * 1024
        ),
        name="relay",
    )(
        patches,
        condition.reshape(micro, features),
        valid_count.reshape(micro),
        cotangent, ada_weight, conv_weight, proj_weight, out_weight, up_weight, down_weight)
    outs = pl.pallas_call(
        lambda *refs: finish(len(out_shape), *refs),
        out_shape=[jax.ShapeDtypeStruct(*o) for o in out_shape],
        in_specs=[pl.BlockSpec(memory_space=pltpu.VMEM)] * len(out_shape),
        out_specs=[pl.BlockSpec(memory_space=pltpu.HBM)] * len(out_shape),
        scratch_shapes=[pltpu.SemaphoreType.DMA((len(out_shape),))],
        name="finish",
    )(*outs)
    outs = list(outs)
    outs[4] = outs[4].reshape(1, TAPS, chunk)
    stride = lax.axis_size("dp") // GROUP
    if stride > 1:
        teams = [[t * stride + j for j in range(stride)] for t in range(GROUP)]
        outs = [
            lax.psum_scatter(o, "dp", scatter_dimension=2 if n == 4 else 1, axis_index_groups=teams, tiled=True)
            if n >= 3
            else o
            for n, o in enumerate(outs)
        ]
    return tuple(outs)


def solution(mesh):
    by_section = P("section", None, None)
    placed = (
        P(None, "dp", None, None),
        P(None, "dp", None),
        P(None, "dp"),
        P(None, "dp", None, None),
        *(by_section,) * 6,
    )
    rows_out = P("section", "dp", None)
    return jax.shard_map(
        body,
        mesh=mesh,
        in_specs=placed,
        out_specs=(
            P("section", None, "dp", None, None),
            P("section", None, "dp", None, None),
            P(None, "dp", None),
            rows_out,
            P("section", None, "dp"),
            rows_out,
            rows_out,
            rows_out,
            rows_out,
        ),
        check_vma=False,
    )
```

```python
import jax
import jax.numpy as jnp
from jax import lax
from jax.experimental import pallas as pl
from jax.experimental.pallas import tpu as pltpu
from jax.sharding import PartitionSpec as P

F32, BF = jnp.float32, jnp.bfloat16
HD = 64
TAPS = 3
GROUP = 16
R = 64
MESH = pl.DeviceIdType.MESH
SCALE = HD**-0.5


def mm(a, b):
    return jnp.dot(a, b, preferred_element_type=F32)


def nt(a, b):
    return lax.dot_general(a, b, (((1,), (1,)), ((), ())), preferred_element_type=F32)


def tn(a, b):
    return lax.dot_general(a, b, (((0,), (0,)), ((), ())), preferred_element_type=F32)


def fold(v):
    return jnp.sum(v.reshape(v.shape[0] // 8, 8, v.shape[1]), 0)


def wide(col):
    return jnp.broadcast_to(col, (col.shape[0], 128))


def sigmoid(v):
    return 1.0 / (1.0 + jnp.exp(-v))


def stats(v):
    c = v - jnp.mean(v, -1, keepdims=True)
    s = lax.rsqrt(jnp.mean(c * c, -1, keepdims=True) + 1e-6)
    return c * s, s


def norm_back(g, n, s):
    return s * (g - jnp.mean(g, -1, keepdims=True) - n * jnp.mean(g * n, -1, keepdims=True))


def rows(r, extra=0):
    return pl.ds(r * R, R + extra)


def steps(n, body, init=0):
    for r in range(n):
        init = body(r, init)
    return init


def loop(n, body, init=0):
    return lax.fori_loop(0, n, body, init)


class Refs:
    def __init__(self, names, refs):
        self.__dict__.update(zip(names, refs, strict=True))


def triangle(second, length):
    sign = jnp.where(second, -1, 1)
    query = lax.broadcasted_iota(jnp.int32, (length, length), 0)
    key = lax.broadcasted_iota(jnp.int32, (length, length), 1)
    return (query - key) * sign >= 0


def shifted(buf, j, second):
    return jnp.where(second, buf[8 + j : 8 + j + R], buf[8 - j : 8 - j + R])


def forward(s, i, second, count, loaded):
    length, features = s.inflow.shape[1:]
    hidden = s.wu.shape[1]
    mod = s.mod.at[i]
    tok = pl.ds(pl.multiple_of(i * length, length), length)

    def trow(r):
        return pl.ds(pl.multiple_of(i * length + r * R, R), R)

    def place(r):
        return r * R + lax.broadcasted_iota(jnp.int32, (R, 1), 0)

    def first_norm(r, c):
        n, sc = stats(s.inflow[i, rows(r), :].astype(F32))
        s.n1[i, rows(r), :] = n
        s.r1[i, rows(r), :] = wide(sc)
        m = jnp.where(place(r) < count, n * (1.0 + mod[1:2, :]) + mod[0:1, :], 0.0)
        s.mixed[i, pl.ds(r * R + 8, R), :] = m
        return c

    steps(length // R, first_norm)
    loaded("wc")

    def conv(r, c):
        buf = s.mixed[i, rows(r, 16), :]
        v = s.wc[0:1, :].astype(F32) * buf[8 : 8 + R]
        for j in range(1, TAPS):
            v = v + s.wc[j : j + 1, :].astype(F32) * shifted(buf, j, second)
        s.conv[trow(r), :] = jnp.where(place(r) < count, v, 0.0).astype(BF)
        return c

    steps(length // R, conv)
    loaded("wp")
    cv = s.conv[tok, :]
    for c in range(3):
        p = mm(cv, s.wp[:, c * features : (c + 1) * features])
        s.qkv[i, :, c * features : (c + 1) * features] = (p * SCALE if c == 0 else p).astype(BF)
    s.wide_a[...] = mm(cv, s.wp[:, 3 * features :])
    keep = triangle(second, length)
    lane = lax.broadcasted_iota(jnp.int32, (length, 2 * HD), 1) < HD

    def pair(p, c):
        def at(k):
            return pl.ds(k * features + p * 2 * HD, 2 * HD)

        q, k, v = (s.qkv[i, :, at(n)] for n in range(3))
        z = jnp.zeros_like(q)
        tot = None
        for h in range(2):
            mine = lane if h == 0 else jnp.logical_not(lane)
            sw = jnp.where(keep, nt(jnp.where(mine, q, z), k), 0.0).astype(BF)
            s.sw[i, 2 * p + h] = sw
            part = mm(sw, jnp.where(mine, v, z))
            tot = part if tot is None else tot + part
        s.an[i, :, at(0)] = tot
        return c

    steps(features // (2 * HD), pair)

    def gate(r, c):
        a = s.an[i, rows(r), :]
        sc = lax.rsqrt(jnp.mean(a * a, -1, keepdims=True) + 1e-6)
        an = a * sc
        g = s.wide_a[rows(r), :]
        sg = sigmoid(g)
        act = g * sg
        s.an[i, rows(r), :] = an
        s.ra[i, rows(r), :] = wide(sc)
        s.act[i, rows(r), :] = act
        s.dact[i, rows(r), :] = sg + act * (1.0 - sg)
        s.gated[trow(r), :] = (an * act).astype(BF)
        return c

    steps(length // R, gate)
    loaded("wo")
    s.branch[i] = mm(s.gated[tok, :], s.wo[...])

    def second_norm(r, c):
        v = s.inflow[i, rows(r), :].astype(F32) + mod[2:3, :] * s.branch[i, rows(r), :]
        n, sc = stats(v)
        s.hid[rows(r), :] = v
        s.n2[i, rows(r), :] = n
        s.r2[i, rows(r), :] = wide(sc)
        s.m2[trow(r), :] = (n * (1.0 + mod[4:5, :]) + mod[3:4, :]).astype(BF)
        return c

    steps(length // R, second_norm)
    loaded("wu")
    loaded("wd")
    width = 256

    def feed(c, carry):
        at = pl.ds(c * width, width)
        h = mm(s.m2[tok, :], s.wu[:, at])
        k0, k1 = 0.7978845608028654, 0.044715
        hh = h * h
        t = jnp.tanh(h * (k0 + (k0 * k1) * hh))
        half = 0.5 * (1.0 + t)
        a = (h * half).astype(BF)
        s.ha[tok, at] = a
        s.dgelu[i, :, at] = half + (0.5 * h) * (1.0 - t * t) * (k0 + (3 * k0 * k1) * hh)
        return carry

    steps(hidden // width, feed)
    s.ffn[i] = mm(s.ha[tok, :], s.wd[...])

    def last(r, c):
        s.result[i, rows(r), :] = (s.hid[rows(r), :] + mod[5:6, :] * s.ffn[i, rows(r), :]).astype(BF)
        return c

    steps(length // R, last)


def backward(s, i, second, count, hook):
    length, features = s.inflow.shape[1:]
    hidden = s.wu.shape[1]
    mod, dmod, up = s.mod.at[i], s.dmod.at[i], s.ups.at[i]
    tok = pl.ds(pl.multiple_of(i * length, length), length)

    def trow(r):
        return pl.ds(pl.multiple_of(i * length + r * R, R), R)

    def place(r):
        return r * R + lax.broadcasted_iota(jnp.int32, (R, 1), 0)

    zero = jnp.zeros((8, features), F32)

    def start(r, acc):
        u = up[rows(r), :].astype(F32)
        s.dffn[trow(r), :] = (mod[5:6, :] * u).astype(BF)
        return acc + fold(u * s.ffn[i, rows(r), :])

    acc = steps(length // R, start, zero)
    dmod[5:6, :] = jnp.sum(acc, 0, keepdims=True)
    hook("down")
    width = 256

    def feed(c, carry):
        at = pl.ds(c * width, width)
        d = nt(s.dffn[tok, :], s.wd[at, :])
        dp = (d * s.dgelu[i, :, at]).astype(BF)
        s.dpre[tok, at] = dp
        return carry

    steps(hidden // width, feed)
    s.wide_a[...] = nt(s.dpre[tok, :], s.wu[...])
    hook("up")

    def mid(r, acc):
        dm = s.wide_a[rows(r), :]
        n = s.n2[i, rows(r), :]
        dh = up[rows(r), :].astype(F32) + norm_back(
            dm * (1.0 + mod[4:5, :]), n, s.r2[i, rows(r), :][:, :1]
        )
        s.hid[rows(r), :] = dh
        s.dbr[trow(r), :] = (mod[2:3, :] * dh).astype(BF)
        new = (fold(dm), fold(dm * n), fold(dh * s.branch[i, rows(r), :]))
        return tuple(a + b for a, b in zip(acc, new))

    acc = steps(length // R, mid, (zero,) * 3)
    for k, a in zip((3, 4, 2), acc):
        dmod[k : k + 1, :] = jnp.sum(a, 0, keepdims=True)
    hook("out")
    s.wide_a[...] = nt(s.dbr[tok, :], s.wo[...])

    def gate(r, c):
        dg = s.wide_a[rows(r), :]
        an = s.an[i, rows(r), :]
        dn = dg * s.act[i, rows(r), :]
        s.dproj[trow(r), 3 * features :] = (dg * an * s.dact[i, rows(r), :]).astype(BF)
        da = s.ra[i, rows(r), :][:, :1] * (dn - an * jnp.mean(dn * an, -1, keepdims=True))
        s.datt[rows(r), :] = da.astype(BF)
        return c

    steps(length // R, gate)
    hook("attend")
    keep = triangle(second, length)
    lane = lax.broadcasted_iota(jnp.int32, (length, 2 * HD), 1) < HD

    def pair(p, c):
        def at(k):
            return pl.ds(k * features + p * 2 * HD, 2 * HD)

        q, k, v = (s.qkv[i, :, at(n)] for n in range(3))
        g = s.datt[:, at(0)]
        z = jnp.zeros_like(q)
        dq = dk = dv = None
        for h in range(2):
            mine = lane if h == 0 else jnp.logical_not(lane)
            gm = jnp.where(mine, g, z)
            ds = jnp.where(keep, nt(gm, v), 0.0).astype(BF)
            a = mm(ds, jnp.where(mine, k, z))
            b = tn(ds, jnp.where(mine, q, z))
            e = tn(s.sw[i, 2 * p + h], gm)
            dq = a if dq is None else dq + a
            dk = b if dk is None else dk + b
            dv = e if dv is None else dv + e
        s.dproj[tok, at(0)] = (dq * SCALE).astype(BF)
        s.dproj[tok, at(1)] = dk.astype(BF)
        s.dproj[tok, at(2)] = dv.astype(BF)
        return c

    steps(features // (2 * HD), pair)
    hook("proj")
    s.dcv[8 : length + 8, :] = nt(s.dproj[tok, :], s.wp[...])

    def mask_rows(r, c):
        at = pl.ds(r * R + 8, R)
        s.dcv[at, :] = jnp.where(place(r) < count, s.dcv[at, :], 0.0)
        return c

    steps(length // R, mask_rows)

    def conv(r, acc):
        dbuf = s.dcv[rows(r, 16), :]
        mbuf = s.mixed[i, rows(r, 16), :]
        here = dbuf[8 : 8 + R]
        d = s.wc[0:1, :].astype(F32) * here
        taps = [fold(here * mbuf[8 : 8 + R])]
        for j in range(1, TAPS):
            d = d + s.wc[j : j + 1, :].astype(F32) * shifted(dbuf, j, jnp.logical_not(second))
            taps.append(fold(here * shifted(mbuf, j, second)))
        d = jnp.where(place(r) < count, d, 0.0)
        n = s.n1[i, rows(r), :]
        res = s.hid[rows(r), :] + norm_back(d * (1.0 + mod[1:2, :]), n, s.r1[i, rows(r), :][:, :1])
        s.dx[i, rows(r), :] = res.astype(BF)
        return tuple(a + b for a, b in zip(acc, (fold(d), fold(d * n), *taps)))

    acc = steps(length // R, conv, (zero,) * (2 + TAPS))
    for k in range(2):
        dmod[k : k + 1, :] = jnp.sum(acc[k], 0, keepdims=True)
    for j in range(TAPS):
        s.dwc[j : j + 1, :] += jnp.sum(acc[2 + j], 0, keepdims=True)


ACROSS, ALONG = (0, 1, 2, 3), (0, 2, 3, 1)
PIECES = {
    "d0": ("down", 0, 256, ACROSS),
    "d1": ("down", 256, 128, ALONG),
    "u0": ("up", 0, 512, ACROSS),
    "u1": ("up", 512, 512, ACROSS),
    "u2": ("up", 1024, 512, ACROSS),
    "o0": ("out", 0, 384, ALONG),
    "p0": ("proj", 0, 512, ACROSS),
    "p1": ("proj", 512, 512, ACROSS),
    "p2": ("proj", 1024, 512, ACROSS),
}


def spot(chunk, order):
    p = 0
    for bit in order:
        p = 2 * p + ((chunk >> bit) & 1)
    return p


class Halving:
    def __init__(self, s, name, section, spread, me):
        self.whole, self.at, self.width, self.order = PIECES[name]
        self.g = getattr(s, "g_" + name)
        self.got = [getattr(s, f"got{k}_" + name) for k in range(4)]
        self.sent = getattr(s, "sent_" + name)
        self.fin = getattr(s, "fin_" + self.whole).at[:, pl.ds(self.at, self.width)]
        index = list(PIECES).index(name)
        self.send_sem = [s.rs_send.at[index, k] for k in range(4)]
        self.recv_sem = [s.rs_recv.at[index, k] for k in range(4)]
        height = self.g.shape[0]
        low = 0
        self.keep, self.give, self.peer = [], [], []
        self.bit = [lax.rem(lax.div(me, 1 << b), 2) for b in self.order]
        for k, b in enumerate(self.order):
            half = height >> (k + 1)
            step = half if half % 16 == 0 else 8
            self.keep.append(pl.multiple_of(low + self.bit[k] * half, step))
            self.give.append(pl.multiple_of(low + (1 - self.bit[k]) * half, step))
            low = self.keep[-1]
            other = me + (1 - 2 * self.bit[k]) * (1 << b)
            self.peer.append((section, spread(other)))

    def copy(self, k):
        half = self.g.shape[0] >> (k + 1)
        src = self.sent if k == 3 else self.g.at[pl.ds(self.give[k], half)]
        return pltpu.make_async_remote_copy(
            src_ref=src,
            dst_ref=self.got[k],
            send_sem=self.send_sem[k],
            recv_sem=self.recv_sem[k],
            device_id=self.peer[k],
            device_id_type=MESH,
        )

    def start(self, k):
        self.copy(k).start()

    def step(self, k):
        self.copy(k).wait_recv()
        got = self.got[k]
        if k < 2:
            at = pl.ds(self.keep[k], got.shape[0])
            self.g[at, :] = (self.g[at, :].astype(F32) + got[...].astype(F32)).astype(BF)
        elif k == 2:
            part = got.shape[0] // 2
            v = self.g[pl.ds(self.keep[2], 2 * part), :].astype(F32) + got[...].astype(F32)
            upper = self.bit[3] == 1
            self.sent[...] = jnp.where(upper, v[:part], v[part:]).astype(BF)
            self.fin[...] = jnp.where(upper, v[part:], v[:part])
        else:
            self.fin[...] += got[...].astype(F32)
        if k < 3:
            self.start(k + 1)

    def end(self):
        for k in range(4):
            self.copy(k).wait_send()


def group_rows(val, order):
    height = val.shape[0] // GROUP
    at = [0] * GROUP
    for c in range(GROUP):
        at[spot(c, order)] = c
    return jnp.concatenate([val[c * height : (c + 1) * height] for c in at], 0)


def weight_gradient(s, name, jobs):
    mine = [job for job in jobs.values() if job.whole == name]
    if name == "down":
        features = s.dffn.shape[1]
        chunk = mine[0].g.shape[0] // GROUP
        per = features // chunk
        for c in range(s.ha.shape[1] // features):
            v = tn(s.ha[:, c * features : (c + 1) * features], s.dffn[...]).astype(BF)
            for j in range(per):
                for job in mine:
                    p = spot(c * per + j, job.order) * chunk
                    job.g[p : p + chunk, :] = v[j * chunk : (j + 1) * chunk, job.at : job.at + job.width]
        for job in mine:
            job.start(0)
        return
    left, right = {"up": (s.m2, s.dpre), "out": (s.gated, s.dbr), "proj": (s.conv, s.dproj)}[name]
    for job in mine:
        at = pl.ds(job.at, job.width)
        job.g[...] = group_rows(tn(left[...], right[:, at]), job.order).astype(BF)
        job.start(0)


OUTS = ("o_act", "o_dx", "o_cond", "o_ada", "o_conv", "o_proj", "o_out", "o_up", "o_down")
INS = ("patches", "condition", "count", "cotangent", "w_ada", "w_conv", "w_proj", "w_out", "w_up", "w_down")


def kernel(names, *refs):
    s = Refs(names, refs)
    section, place = lax.axis_index("section"), lax.axis_index("dp")
    stride = lax.axis_size("dp") // GROUP
    me, low = lax.div(place, stride), lax.rem(place, stride)
    first, second = section == 0, section == 1

    def spread(member):
        return member * stride + low

    partner = (1 - section, place)
    micro, length, features = s.inflow.shape

    loads = {
        "ada": (s.w_ada.at[0], s.ada),
        "cond": (s.condition, s.cond),
        "wc": (s.w_conv.at[0], s.wc),
        "wp": (s.w_proj.at[0], s.wp),
        "wo": (s.w_out.at[0], s.wo),
        "wu": (s.w_up.at[0], s.wu),
        "wd": (s.w_down.at[0], s.wd),
    }
    order = list(loads)

    def load(name):
        return pltpu.make_async_copy(*loads[name], s.load_sem.at[order.index(name)])

    def load_patches():
        return pltpu.make_async_copy(s.patches.at[:, 0], s.inflow, s.load_sem.at[len(order)])

    def load_cotangent():
        return pltpu.make_async_copy(s.cotangent.at[:, 0], s.ups, s.load_sem.at[len(order)])

    load("cond").start()
    load("ada").start()
    pl.when(first)(lambda: load_patches().start())
    for name in order[2:]:
        load(name).start()
    pl.when(second)(lambda: load_cotangent().start())

    barrier = pltpu.get_barrier_semaphore()

    def greet(j, c):
        other = lax.rem(me + j, GROUP)
        pl.semaphore_signal(barrier, 1, device_id=(section, spread(other)), device_id_type=MESH)
        return c

    lax.fori_loop(1, GROUP, greet, 0)
    pl.semaphore_signal(barrier, 1, device_id=partner, device_id_type=MESH)

    zero = jnp.zeros((8, features), F32)
    for i in range(micro):
        s.mixed[i, 0:8, :] = zero
        s.mixed[i, length + 8 :, :] = zero
    s.dcv[0:8, :] = zero
    s.dcv[length + 8 :, :] = zero
    s.dwc[...] = zero

    load("cond").wait()
    conds = [s.cond[i : i + 1, :].astype(F32) for i in range(micro)]
    silus = [(v * sigmoid(v)).astype(BF).astype(F32) for v in conds]
    row = lax.broadcasted_iota(jnp.int32, (16, features), 0)
    act_rows = jnp.where(
        row < 6,
        jnp.broadcast_to(silus[0], (16, features)),
        jnp.where(row < 12, jnp.broadcast_to(silus[1], (16, features)), 0.0),
    ).astype(BF)
    s.own_act[...] = act_rows
    load("ada").wait()
    for k in range(6):
        m = mm(act_rows, s.ada[:, k * features : (k + 1) * features])
        for i in range(micro):
            s.mod[i, k : k + 1, :] = m[6 * i : 6 * i + 1, :]

    def result_copy(i):
        return pltpu.make_async_remote_copy(
            src_ref=s.result.at[i],
            dst_ref=s.inflow.at[i],
            send_sem=s.hop_send.at[i],
            recv_sem=s.hop_recv.at[i],
            device_id=partner,
            device_id_type=MESH,
        )

    def dx_copy(i):
        return pltpu.make_async_remote_copy(
            src_ref=s.dx.at[i],
            dst_ref=s.ups.at[i],
            send_sem=s.hop_send.at[i],
            recv_sem=s.hop_recv.at[i],
            device_id=partner,
            device_id_type=MESH,
        )

    def result_out(i):
        return pltpu.make_async_copy(s.result.at[i], s.o_act.at[0, i, 0], s.out_sem.at[i])

    def dx_out(i):
        return pltpu.make_async_copy(s.dx.at[i], s.o_dx.at[0, i, 0], s.out_sem.at[2 + i])

    def gather_copy(j, src, dst, send, recv):
        other = lax.rem(me + j, GROUP)
        return pltpu.make_async_remote_copy(
            src_ref=src,
            dst_ref=dst.at[me],
            send_sem=send.at[j],
            recv_sem=recv.at[me],
            device_id=(section, spread(other)),
            device_id_type=MESH,
        )

    def gathered(j, src, dst, send, recv):
        other = lax.rem(me + j, GROUP)
        return pltpu.make_async_remote_copy(
            src_ref=src,
            dst_ref=dst.at[other],
            send_sem=send.at[j],
            recv_sem=recv.at[other],
            device_id=(section, spread(other)),
            device_id_type=MESH,
        )

    acts = (s.own_act, s.all_act, s.act_send, s.act_recv)
    mods = (s.own_mod, s.all_mod, s.mod_send, s.mod_recv)

    def each_peer(fn):
        def one(j, c):
            fn(j)
            return c

        lax.fori_loop(1, GROUP, one, 0)

    def do_forward(i):
        @pl.when(jnp.logical_and(first, i == 0))
        def _():
            load_patches().wait()

        pl.when(second)(lambda: result_copy(i).wait_recv())

        def loaded(name):
            pl.when(i == 0)(lambda: load(name).wait())

        @pl.when(jnp.logical_and(second, i == 0))
        def _():
            load_cotangent().wait()

        forward(s, i, second, s.count[i], loaded)
        result_out(i).start()

        @pl.when(i == 0)
        def _():
            pl.semaphore_wait(barrier, GROUP)
            each_peer(lambda j: gather_copy(j, *acts).start())

        pl.when(first)(lambda: result_copy(i).start())

    jobs = {name: Halving(s, name, section, spread, me) for name in PIECES}

    def take(text):
        for word in text.split():
            jobs[word[:2]].step(int(word[2]))

    def do_backward(i):
        pl.when(first)(lambda: dx_copy(i).wait_recv())
        last = i == micro - 1

        def hook(name):
            @pl.when(jnp.logical_and(first, last))
            def _():
                if name == "up":
                    take("d00 d10")
                if name == "proj":
                    take("o00 d11")
                if name != "attend":
                    weight_gradient(s, name, jobs)
                else:
                    take("u00 u10 u20")

        backward(s, i, second, s.count[i], hook)
        dx_out(i).start()

        @pl.when(second)
        def _():
            dx_copy(i).start()

            @pl.when(last)
            def _():
                for name in ("down", "up", "out", "proj"):
                    weight_gradient(s, name, jobs)
                take("d00 d10 u00 u10 u20 o00 d11")

    def turn(n, c):
        ahead = jnp.logical_or(n == 0, jnp.where(first, n == 1, n == micro))
        i = jnp.where(first, lax.rem(n, micro), lax.div(n, 2))
        pl.when(ahead)(lambda: do_forward(i))
        pl.when(jnp.logical_not(ahead))(lambda: do_backward(i))
        return c

    loop(2 * micro, turn)

    for i in range(micro):
        for k in range(6):
            s.stage[6 * i + k : 6 * i + k + 1, :] = s.dmod[i, k : k + 1, :]
    s.stage[12 : 12 + TAPS, :] = s.dwc[0:TAPS, :]
    s.stage[15:16, :] = jnp.zeros((1, features), F32)
    own = s.stage[...].astype(BF)
    s.own_mod[...] = own
    each_peer(lambda j: gather_copy(j, *mods).start())
    take("p00 p10 p20 d01")

    tot = jnp.zeros((16, features), F32)
    for k in range(6):
        part = nt(own, s.ada[:, k * features : (k + 1) * features])
        tot = tot + jnp.where(jnp.logical_or(row == k, row == 6 + k), part, 0.0)
    for i in range(micro):
        sg = sigmoid(conds[i])
        slope = sg + conds[i] * sg * (1.0 - sg)
        s.own_cond[i, :, :] = jnp.sum(tot[6 * i : 6 * i + 6], 0, keepdims=True) * slope
    cond_copy = pltpu.make_async_remote_copy(
        src_ref=s.own_cond,
        dst_ref=s.got_cond,
        send_sem=s.cond_sem.at[0],
        recv_sem=s.cond_sem.at[1],
        device_id=partner,
        device_id_type=MESH,
    )
    cond_copy.start()
    take("o01 u01 d12 d02 u11 u02 o02 u21 u12 d03 p01 u03 u22 u13 p11 p02 u23 p21 p12 d13 o03")

    s.all_act[me] = act_rows
    s.all_mod[me] = own
    each_peer(lambda j: gathered(j, *acts).wait_recv())
    each_peer(lambda j: gathered(j, *mods).wait_recv())
    chunk = features // GROUP
    n_rows = GROUP * 16
    flat_act = s.all_act[...].reshape(n_rows, features)
    flat_mod = s.all_mod[...].reshape(n_rows, features)
    pick = (
        lax.broadcasted_iota(jnp.int32, (chunk, features), 1)
        == me * chunk + lax.broadcasted_iota(jnp.int32, (chunk, features), 0)
    ).astype(F32).astype(BF)
    left = nt(pick, flat_act)
    lane = lax.rem(lax.broadcasted_iota(jnp.int32, (chunk, n_rows), 1), 16)
    for k in range(6):
        mine = jnp.logical_or(lane == k, lane == 6 + k)
        s.fin_ada[:, k * features : (k + 1) * features] = mm(
            jnp.where(mine, left, 0.0).astype(BF), flat_mod
        )
    picked = nt(flat_mod, pick).astype(BF)
    tap = lax.broadcasted_iota(jnp.int32, (8, n_rows), 0)
    at_tap = lax.rem(lax.broadcasted_iota(jnp.int32, (8, n_rows), 1), 16) == 12 + tap
    sums = mm(jnp.where(jnp.logical_and(at_tap, tap < TAPS), 1.0, 0.0).astype(BF), picked)
    for j in range(TAPS):
        s.fin_conv[j, :, :] = sums[j : j + 1, :]

    cond_copy.wait()
    s.fin_cond[...] = s.own_cond[...] + s.got_cond[...]
    take("p03 p22 p13 p23")

    outs = [
        (s.fin_cond, s.o_cond),
        (s.fin_ada, s.o_ada.at[0]),
        (s.fin_conv, s.o_conv),
        (s.fin_proj, s.o_proj.at[0]),
        (s.fin_out, s.o_out.at[0]),
        (s.fin_up, s.o_up.at[0]),
        (s.fin_down, s.o_down.at[0]),
    ]
    copies = [pltpu.make_async_copy(a, b, s.out_sem.at[4 + n]) for n, (a, b) in enumerate(outs)]
    for c in copies:
        c.start()
    for i in range(micro):
        result_out(i).wait()
        dx_out(i).wait()
        pl.when(first)(lambda i=i: result_copy(i).wait_send())
        pl.when(second)(lambda i=i: dx_copy(i).wait_send())
    for job in jobs.values():
        job.end()
    each_peer(lambda j: gather_copy(j, *acts).wait_send())
    each_peer(lambda j: gather_copy(j, *mods).wait_send())
    for c in copies:
        c.wait()


def finish(n, *refs):
    held, given, sems = refs[:n], refs[n : 2 * n], refs[2 * n]
    outward = [pltpu.make_async_copy(a, b, sems.at[k]) for k, (a, b) in enumerate(zip(held, given))]
    for o in outward:
        o.start()
    for o in outward:
        o.wait()


def body(patches, condition, valid_count, cotangent, ada_weight, conv_weight, proj_weight, out_weight, up_weight, down_weight):
    micro, images, length, features = patches.shape
    hidden = up_weight.shape[2]
    heads = features // HD
    tokens = micro * length
    chunk, deep = features // GROUP, hidden // GROUP
    arrays = dict(
        ada=((features, 6 * features), BF),
        cond=((micro, features), BF),
        wc=((TAPS, features), BF),
        wp=((features, 4 * features), BF),
        wo=((features, features), BF),
        wu=((features, hidden), BF),
        wd=((hidden, features), BF),
        inflow=((micro, length, features), BF),
        ups=((micro, length, features), BF),
        result=((micro, length, features), BF),
        dx=((micro, length, features), BF),
        mod=((micro, 8, features), F32),
        dmod=((micro, 8, features), F32),
        dwc=((8, features), F32),
        n1=((micro, length, features), F32),
        r1=((micro, length, 128), F32),
        mixed=((micro, length + 16, features), F32),
        conv=((tokens, features), BF),
        qkv=((micro, length, 3 * features), BF),
        sw=((micro, heads, length, length), BF),
        an=((micro, length, features), F32),
        ra=((micro, length, 128), F32),
        act=((micro, length, features), F32),
        dact=((micro, length, features), F32),
        gated=((tokens, features), BF),
        branch=((micro, length, features), F32),
        hid=((length, features), F32),
        wide_a=((length, features), F32),
        n2=((micro, length, features), F32),
        r2=((micro, length, 128), F32),
        m2=((tokens, features), BF),
        ffn=((micro, length, features), F32),
        ha=((tokens, hidden), BF),
        dgelu=((micro, length, hidden), F32),
        dffn=((tokens, features), BF),
        dpre=((tokens, hidden), BF),
        dbr=((tokens, features), BF),
        datt=((length, features), BF),
        dproj=((tokens, 4 * features), BF),
        dcv=((length + 16, features), F32),
        own_act=((16, features), BF),
        all_act=((GROUP, 16, features), BF),
        own_mod=((16, features), BF),
        all_mod=((GROUP, 16, features), BF),
        stage=((16, features), F32),
        own_cond=((micro, 1, features), F32),
        got_cond=((micro, 1, features), F32),
        fin_cond=((micro, 1, features), F32),
        fin_ada=((chunk, 6 * features), F32),
        fin_conv=((TAPS, 1, chunk), F32),
    )
    tall = dict(down=hidden, up=features, out=features, proj=features)
    across = dict(down=features, up=hidden, out=features, proj=4 * features)
    for name, height in tall.items():
        arrays["fin_" + name] = ((height // GROUP, across[name]), F32)
    for name, (whole, at, width, order) in PIECES.items():
        arrays["g_" + name] = ((tall[whole], width), BF)
        for k in range(4):
            arrays[f"got{k}_{name}"] = ((tall[whole] >> (k + 1), width), BF)
        arrays["sent_" + name] = ((tall[whole] // GROUP, width), BF)
    sems = dict(
        load_sem=(8,),
        hop_send=(2,),
        hop_recv=(2,),
        out_sem=(11,),
        rs_send=(len(PIECES), 4),
        rs_recv=(len(PIECES), 4),
        act_send=(GROUP,),
        act_recv=(GROUP,),
        mod_send=(GROUP,),
        mod_recv=(GROUP,),
        cond_sem=(2,),
    )
    names = (*INS, *OUTS, *arrays, *sems)
    any_spec = pl.BlockSpec(memory_space=pl.ANY)
    out_shape = (
        ((1, micro, 1, length, features), BF),
        ((1, micro, 1, length, features), BF),
        ((micro, 1, features), F32),
        ((1, chunk, 6 * features), F32),
        ((TAPS, 1, chunk), F32),
        ((1, chunk, 4 * features), F32),
        ((1, chunk, features), F32),
        ((1, chunk, hidden), F32),
        ((1, deep, features), F32),
    )
    outs = pl.pallas_call(
        lambda *refs: kernel(names, *refs),
        out_shape=[jax.ShapeDtypeStruct(*o) for o in out_shape],
        in_specs=[pl.BlockSpec(memory_space=pltpu.SMEM if n == "count" else pltpu.HBM) for n in INS],
        out_specs=[any_spec] * len(OUTS),
        scratch_shapes=[pltpu.VMEM(*a) for a in arrays.values()]
        + [pltpu.SemaphoreType.DMA(n) for n in sems.values()],
        compiler_params=pltpu.CompilerParams(
            collective_id=0, has_side_effects=True, vmem_limit_bytes=60000 * 1024
        ),
        name="relay",
    )(
        patches,
        condition.reshape(micro, features),
        valid_count.reshape(micro),
        cotangent, ada_weight, conv_weight, proj_weight, out_weight, up_weight, down_weight)
    outs = pl.pallas_call(
        lambda *refs: finish(len(out_shape), *refs),
        out_shape=[jax.ShapeDtypeStruct(*o) for o in out_shape],
        in_specs=[pl.BlockSpec(memory_space=pltpu.VMEM)] * len(out_shape),
        out_specs=[pl.BlockSpec(memory_space=pltpu.HBM)] * len(out_shape),
        scratch_shapes=[pltpu.SemaphoreType.DMA((len(out_shape),))],
        name="finish",
    )(*outs)
    outs = list(outs)
    outs[4] = outs[4].reshape(1, TAPS, chunk)
    stride = lax.axis_size("dp") // GROUP
    if stride > 1:
        teams = [[t * stride + j for j in range(stride)] for t in range(GROUP)]
        outs = [
            lax.psum_scatter(o, "dp", scatter_dimension=2 if n == 4 else 1, axis_index_groups=teams, tiled=True)
            if n >= 3
            else o
            for n, o in enumerate(outs)
        ]
    return tuple(outs)


def solution(mesh):
    by_section = P("section", None, None)
    placed = (
        P(None, "dp", None, None),
        P(None, "dp", None),
        P(None, "dp"),
        P(None, "dp", None, None),
        *(by_section,) * 6,
    )
    rows_out = P("section", "dp", None)
    return jax.shard_map(
        body,
        mesh=mesh,
        in_specs=placed,
        out_specs=(
            P("section", None, "dp", None, None),
            P("section", None, "dp", None, None),
            P(None, "dp", None),
            rows_out,
            P("section", None, "dp"),
            rows_out,
            rows_out,
            rows_out,
            rows_out,
        ),
        check_vma=False,
    )
```

```python
import jax
import jax.numpy as jnp
from jax import lax
from jax.experimental import pallas as pl
from jax.experimental.pallas import tpu as pltpu
from jax.sharding import PartitionSpec as P

F32, BF = jnp.float32, jnp.bfloat16
HD = 64
TAPS = 3
GROUP = 16
R = 64
MESH = pl.DeviceIdType.MESH
SCALE = HD**-0.5


def mm(a, b):
    return jnp.dot(a, b, preferred_element_type=F32)


def nt(a, b):
    return lax.dot_general(a, b, (((1,), (1,)), ((), ())), preferred_element_type=F32)


def tn(a, b):
    return lax.dot_general(a, b, (((0,), (0,)), ((), ())), preferred_element_type=F32)


def fold(v):
    return jnp.sum(v.reshape(v.shape[0] // 8, 8, v.shape[1]), 0)


def wide(col):
    return jnp.broadcast_to(col, (col.shape[0], 128))


def sigmoid(v):
    return 1.0 / (1.0 + jnp.exp(-v))


def stats(v):
    c = v - jnp.mean(v, -1, keepdims=True)
    s = lax.rsqrt(jnp.mean(c * c, -1, keepdims=True) + 1e-6)
    return c * s, s


def norm_back(g, n, s):
    return s * (g - jnp.mean(g, -1, keepdims=True) - n * jnp.mean(g * n, -1, keepdims=True))


def rows(r, extra=0):
    return pl.ds(r * R, R + extra)


def steps(n, body, init=0):
    for r in range(n):
        init = body(r, init)
    return init


def loop(n, body, init=0):
    return lax.fori_loop(0, n, body, init)


class Refs:
    def __init__(self, names, refs):
        self.__dict__.update(zip(names, refs, strict=True))


def triangle(second, length):
    sign = jnp.where(second, -1, 1)
    query = lax.broadcasted_iota(jnp.int32, (length, length), 0)
    key = lax.broadcasted_iota(jnp.int32, (length, length), 1)
    return (query - key) * sign >= 0


def shifted(buf, j, second):
    return jnp.where(second, buf[8 + j : 8 + j + R], buf[8 - j : 8 - j + R])


def forward(s, i, second, count, loaded):
    length, features = s.inflow.shape[1:]
    hidden = s.wu.shape[1]
    mod = s.mod.at[i]
    tok = pl.ds(pl.multiple_of(i * length, length), length)

    def trow(r):
        return pl.ds(pl.multiple_of(i * length + r * R, R), R)

    def place(r):
        return r * R + lax.broadcasted_iota(jnp.int32, (R, 1), 0)

    def first_norm(r, c):
        n, sc = stats(s.inflow[i, rows(r), :].astype(F32))
        s.n1[i, rows(r), :] = n
        s.r1[i, rows(r), :] = wide(sc)
        m = jnp.where(place(r) < count, n * (1.0 + mod[1:2, :]) + mod[0:1, :], 0.0)
        s.mixed[i, pl.ds(r * R + 8, R), :] = m
        return c

    steps(length // R, first_norm)
    loaded("wc")

    def conv(r, c):
        buf = s.mixed[i, rows(r, 16), :]
        v = s.wc[0:1, :].astype(F32) * buf[8 : 8 + R]
        for j in range(1, TAPS):
            v = v + s.wc[j : j + 1, :].astype(F32) * shifted(buf, j, second)
        s.conv[trow(r), :] = jnp.where(place(r) < count, v, 0.0).astype(BF)
        return c

    steps(length // R, conv)
    loaded("wp")
    cv = s.conv[tok, :]
    for c in range(3):
        p = mm(cv, s.wp[:, c * features : (c + 1) * features])
        s.qkv[i, :, c * features : (c + 1) * features] = (p * SCALE if c == 0 else p).astype(BF)
    s.wide_a[...] = mm(cv, s.wp[:, 3 * features :])
    keep = triangle(second, length)
    lane = lax.broadcasted_iota(jnp.int32, (length, 2 * HD), 1) < HD

    def pair(p, c):
        def at(k):
            return pl.ds(k * features + p * 2 * HD, 2 * HD)

        q, k, v = (s.qkv[i, :, at(n)] for n in range(3))
        z = jnp.zeros_like(q)
        tot = None
        for h in range(2):
            mine = lane if h == 0 else jnp.logical_not(lane)
            sw = jnp.where(keep, nt(jnp.where(mine, q, z), k), 0.0).astype(BF)
            s.sw[i, 2 * p + h] = sw
            part = mm(sw, jnp.where(mine, v, z))
            tot = part if tot is None else tot + part
        s.an[i, :, at(0)] = tot
        return c

    steps(features // (2 * HD), pair)

    def gate(r, c):
        a = s.an[i, rows(r), :]
        sc = lax.rsqrt(jnp.mean(a * a, -1, keepdims=True) + 1e-6)
        an = a * sc
        g = s.wide_a[rows(r), :]
        sg = sigmoid(g)
        act = g * sg
        s.an[i, rows(r), :] = an
        s.ra[i, rows(r), :] = wide(sc)
        s.act[i, rows(r), :] = act
        s.dact[i, rows(r), :] = sg + act * (1.0 - sg)
        s.gated[trow(r), :] = (an * act).astype(BF)
        return c

    steps(length // R, gate)
    loaded("wo")
    s.branch[i] = mm(s.gated[tok, :], s.wo[...])

    def second_norm(r, c):
        v = s.inflow[i, rows(r), :].astype(F32) + mod[2:3, :] * s.branch[i, rows(r), :]
        n, sc = stats(v)
        s.hid[rows(r), :] = v
        s.n2[i, rows(r), :] = n
        s.r2[i, rows(r), :] = wide(sc)
        s.m2[trow(r), :] = (n * (1.0 + mod[4:5, :]) + mod[3:4, :]).astype(BF)
        return c

    steps(length // R, second_norm)
    loaded("wu")
    loaded("wd")
    width = 256

    def feed(c, carry):
        at = pl.ds(c * width, width)
        h = mm(s.m2[tok, :], s.wu[:, at])
        k0, k1 = 0.7978845608028654, 0.044715
        hh = h * h
        t = jnp.tanh(h * (k0 + (k0 * k1) * hh))
        half = 0.5 * (1.0 + t)
        a = (h * half).astype(BF)
        s.ha[tok, at] = a
        s.dgelu[i, :, at] = half + (0.5 * h) * (1.0 - t * t) * (k0 + (3 * k0 * k1) * hh)
        return carry

    steps(hidden // width, feed)
    s.ffn[i] = mm(s.ha[tok, :], s.wd[...])

    def last(r, c):
        s.result[i, rows(r), :] = (s.hid[rows(r), :] + mod[5:6, :] * s.ffn[i, rows(r), :]).astype(BF)
        return c

    steps(length // R, last)


def backward(s, i, second, count, hook):
    length, features = s.inflow.shape[1:]
    hidden = s.wu.shape[1]
    mod, dmod, up = s.mod.at[i], s.dmod.at[i], s.ups.at[i]
    tok = pl.ds(pl.multiple_of(i * length, length), length)

    def trow(r):
        return pl.ds(pl.multiple_of(i * length + r * R, R), R)

    def place(r):
        return r * R + lax.broadcasted_iota(jnp.int32, (R, 1), 0)

    zero = jnp.zeros((8, features), F32)

    def start(r, acc):
        u = up[rows(r), :].astype(F32)
        s.dffn[trow(r), :] = (mod[5:6, :] * u).astype(BF)
        return acc + fold(u * s.ffn[i, rows(r), :])

    acc = steps(length // R, start, zero)
    dmod[5:6, :] = jnp.sum(acc, 0, keepdims=True)
    hook("down")
    width = 256

    def feed(c, carry):
        at = pl.ds(c * width, width)
        d = nt(s.dffn[tok, :], s.wd[at, :])
        dp = (d * s.dgelu[i, :, at]).astype(BF)
        s.dpre[tok, at] = dp
        return carry

    steps(hidden // width, feed)
    s.wide_a[...] = nt(s.dpre[tok, :], s.wu[...])
    hook("up")

    def mid(r, acc):
        dm = s.wide_a[rows(r), :]
        n = s.n2[i, rows(r), :]
        dh = up[rows(r), :].astype(F32) + norm_back(
            dm * (1.0 + mod[4:5, :]), n, s.r2[i, rows(r), :][:, :1]
        )
        s.hid[rows(r), :] = dh
        s.dbr[trow(r), :] = (mod[2:3, :] * dh).astype(BF)
        new = (fold(dm), fold(dm * n), fold(dh * s.branch[i, rows(r), :]))
        return tuple(a + b for a, b in zip(acc, new))

    acc = steps(length // R, mid, (zero,) * 3)
    for k, a in zip((3, 4, 2), acc):
        dmod[k : k + 1, :] = jnp.sum(a, 0, keepdims=True)
    hook("out")
    s.wide_a[...] = nt(s.dbr[tok, :], s.wo[...])

    def gate(r, c):
        dg = s.wide_a[rows(r), :]
        an = s.an[i, rows(r), :]
        dn = dg * s.act[i, rows(r), :]
        s.dproj[trow(r), 3 * features :] = (dg * an * s.dact[i, rows(r), :]).astype(BF)
        da = s.ra[i, rows(r), :][:, :1] * (dn - an * jnp.mean(dn * an, -1, keepdims=True))
        s.datt[rows(r), :] = da.astype(BF)
        return c

    steps(length // R, gate)
    hook("attend")
    keep = triangle(second, length)
    lane = lax.broadcasted_iota(jnp.int32, (length, 2 * HD), 1) < HD

    def pair(p, c):
        def at(k):
            return pl.ds(k * features + p * 2 * HD, 2 * HD)

        q, k, v = (s.qkv[i, :, at(n)] for n in range(3))
        g = s.datt[:, at(0)]
        z = jnp.zeros_like(q)
        dq = dk = dv = None
        for h in range(2):
            mine = lane if h == 0 else jnp.logical_not(lane)
            gm = jnp.where(mine, g, z)
            ds = jnp.where(keep, nt(gm, v), 0.0).astype(BF)
            a = mm(ds, jnp.where(mine, k, z))
            b = tn(ds, jnp.where(mine, q, z))
            e = tn(s.sw[i, 2 * p + h], gm)
            dq = a if dq is None else dq + a
            dk = b if dk is None else dk + b
            dv = e if dv is None else dv + e
        s.dproj[tok, at(0)] = (dq * SCALE).astype(BF)
        s.dproj[tok, at(1)] = dk.astype(BF)
        s.dproj[tok, at(2)] = dv.astype(BF)
        return c

    steps(features // (2 * HD), pair)
    hook("proj")
    s.dcv[8 : length + 8, :] = nt(s.dproj[tok, :], s.wp[...])

    def mask_rows(r, c):
        at = pl.ds(r * R + 8, R)
        s.dcv[at, :] = jnp.where(place(r) < count, s.dcv[at, :], 0.0)
        return c

    steps(length // R, mask_rows)

    def conv(r, acc):
        dbuf = s.dcv[rows(r, 16), :]
        mbuf = s.mixed[i, rows(r, 16), :]
        here = dbuf[8 : 8 + R]
        d = s.wc[0:1, :].astype(F32) * here
        taps = [fold(here * mbuf[8 : 8 + R])]
        for j in range(1, TAPS):
            d = d + s.wc[j : j + 1, :].astype(F32) * shifted(dbuf, j, jnp.logical_not(second))
            taps.append(fold(here * shifted(mbuf, j, second)))
        d = jnp.where(place(r) < count, d, 0.0)
        n = s.n1[i, rows(r), :]
        res = s.hid[rows(r), :] + norm_back(d * (1.0 + mod[1:2, :]), n, s.r1[i, rows(r), :][:, :1])
        s.dx[i, rows(r), :] = res.astype(BF)
        return tuple(a + b for a, b in zip(acc, (fold(d), fold(d * n), *taps)))

    acc = steps(length // R, conv, (zero,) * (2 + TAPS))
    for k in range(2):
        dmod[k : k + 1, :] = jnp.sum(acc[k], 0, keepdims=True)
    for j in range(TAPS):
        s.dwc[j : j + 1, :] += jnp.sum(acc[2 + j], 0, keepdims=True)


ACROSS, ALONG, BETWEEN = (0, 1, 2, 3), (0, 2, 3, 1), (0, 2, 1, 3)
PIECES = {
    "d0": ("down", 0, 128, ALONG),
    "d1": ("down", 128, 128, ACROSS),
    "d2": ("down", 256, 128, ACROSS),
    "u0": ("up", 0, 512, BETWEEN),
    "u1": ("up", 512, 128, ACROSS),
    "u2": ("up", 640, 512, ACROSS),
    "u3": ("up", 1152, 384, BETWEEN),
    "o0": ("out", 0, 384, ACROSS),
    "p0": ("proj", 0, 512, ACROSS),
    "p1": ("proj", 512, 384, ACROSS),
    "p2": ("proj", 896, 256, ALONG),
    "p3": ("proj", 1152, 256, ALONG),
    "p4": ("proj", 1408, 128, ACROSS),
}
TURNS = {
    "down": ("Wd",),
    "up": ("Wu0", "Wu1", "d00", "Wu2", "d10", "Wu3", "d20"),
    "out": ("Wo",),
    "attend": ("u00", "u10", "u20", "u30"),
    "proj": ("o00", "Wp0", "d01", "Wp1", "Wp2", "d11", "Wp3", "Wp4"),
    "tail": ("p00", "p10", "GATHER", "p20", "p30", "p40", "u01", "COND", "d21", "u11", "u31", "d02", "u21", "d12", "o01", "p21", "p31", "p01", "d13", "d22", "u12", "p11", "u22", "p22", "p32", "p41", "o02", "SHARE", "d23", "u02", "u13", "u32", "p02", "u23", "d03", "ADA", "p23", "p33", "o03", "p12", "p42", "u03", "u33", "p03", "p13", "p43"),
}


def spot(chunk, order):
    p = 0
    for bit in order:
        p = 2 * p + ((chunk >> bit) & 1)
    return p


class Halving:
    def __init__(self, s, name, section, spread, me):
        self.whole, self.at, self.width, self.order = PIECES[name]
        self.g = getattr(s, "g_" + name)
        self.got = [getattr(s, f"got{k}_" + name) for k in range(4)]
        self.sent = getattr(s, "sent_" + name)
        self.fin = getattr(s, "fin_" + self.whole).at[:, pl.ds(self.at, self.width)]
        index = list(PIECES).index(name)
        self.send_sem = [s.rs_send.at[index, k] for k in range(4)]
        self.recv_sem = [s.rs_recv.at[index, k] for k in range(4)]
        height = self.g.shape[0]
        low = 0
        self.keep, self.give, self.peer = [], [], []
        self.bit = [lax.rem(lax.div(me, 1 << b), 2) for b in self.order]
        for k, b in enumerate(self.order):
            half = height >> (k + 1)
            step = half if half % 16 == 0 else 8
            self.keep.append(pl.multiple_of(low + self.bit[k] * half, step))
            self.give.append(pl.multiple_of(low + (1 - self.bit[k]) * half, step))
            low = self.keep[-1]
            other = me + (1 - 2 * self.bit[k]) * (1 << b)
            self.peer.append((section, spread(other)))

    def copy(self, k):
        half = self.g.shape[0] >> (k + 1)
        src = self.sent if k == 3 else self.g.at[pl.ds(self.give[k], half)]
        return pltpu.make_async_remote_copy(
            src_ref=src,
            dst_ref=self.got[k],
            send_sem=self.send_sem[k],
            recv_sem=self.recv_sem[k],
            device_id=self.peer[k],
            device_id_type=MESH,
        )

    def start(self, k):
        self.copy(k).start()

    def step(self, k):
        self.copy(k).wait_recv()
        got = self.got[k]
        if k < 2:
            at = pl.ds(self.keep[k], got.shape[0])
            self.g[at, :] = (self.g[at, :].astype(F32) + got[...].astype(F32)).astype(BF)
        elif k == 2:
            part = got.shape[0] // 2
            v = self.g[pl.ds(self.keep[2], 2 * part), :].astype(F32) + got[...].astype(F32)
            upper = self.bit[3] == 1
            self.sent[...] = jnp.where(upper, v[:part], v[part:]).astype(BF)
            self.fin[...] = jnp.where(upper, v[part:], v[:part])
        else:
            self.fin[...] += got[...].astype(F32)
        if k < 3:
            self.start(k + 1)

    def end(self):
        for k in range(4):
            self.copy(k).wait_send()


def group_rows(val, order):
    height = val.shape[0] // GROUP
    at = [0] * GROUP
    for c in range(GROUP):
        at[spot(c, order)] = c
    return jnp.concatenate([val[c * height : (c + 1) * height] for c in at], 0)


def weight_gradient(s, what, jobs):
    if what == "Wd":
        mine = [job for job in jobs.values() if job.whole == "down"]
        features = s.dffn.shape[1]
        chunk = mine[0].g.shape[0] // GROUP
        per = features // chunk
        for c in range(s.ha.shape[1] // features):
            v = tn(s.ha[:, c * features : (c + 1) * features], s.dffn[...]).astype(BF)
            for j in range(per):
                for job in mine:
                    p = spot(c * per + j, job.order) * chunk
                    job.g[p : p + chunk, :] = v[j * chunk : (j + 1) * chunk, job.at : job.at + job.width]
        for job in mine:
            job.start(0)
        return
    job = jobs["o0" if what == "Wo" else what[1:]]
    left, right = {"up": (s.m2, s.dpre), "out": (s.gated, s.dbr), "proj": (s.conv, s.dproj)}[job.whole]
    at = pl.ds(job.at, job.width)
    job.g[...] = group_rows(tn(left[...], right[:, at]), job.order).astype(BF)
    job.start(0)


OUTS = ("o_act", "o_dx", "o_cond", "o_ada", "o_conv", "o_proj", "o_out", "o_up", "o_down")
INS = ("patches", "condition", "count", "cotangent", "w_ada", "w_conv", "w_proj", "w_out", "w_up", "w_down")


def kernel(names, *refs):
    s = Refs(names, refs)
    section, place = lax.axis_index("section"), lax.axis_index("dp")
    stride = lax.axis_size("dp") // GROUP
    me, low = lax.div(place, stride), lax.rem(place, stride)
    first, second = section == 0, section == 1

    def spread(member):
        return member * stride + low

    partner = (1 - section, place)
    micro, length, features = s.inflow.shape
    s.result, s.dx = s.o_act.at[0, :, 0], s.o_dx.at[0, :, 0]
    s.fin_ada, s.fin_conv, s.fin_cond = s.o_ada.at[0], s.o_conv, s.o_cond
    s.fin_proj, s.fin_out, s.fin_up, s.fin_down = (o.at[0] for o in (s.o_proj, s.o_out, s.o_up, s.o_down))

    loads = {
        "ada": (s.w_ada.at[0], s.ada),
        "cond": (s.condition, s.cond),
        "wc": (s.w_conv.at[0], s.wc),
        "wp": (s.w_proj.at[0], s.wp),
        "wo": (s.w_out.at[0], s.wo),
        "wu": (s.w_up.at[0], s.wu),
        "wd": (s.w_down.at[0], s.wd),
    }
    order = list(loads)

    def load(name):
        return pltpu.make_async_copy(*loads[name], s.load_sem.at[order.index(name)])

    def load_patches():
        return pltpu.make_async_copy(s.patches.at[:, 0], s.inflow, s.load_sem.at[len(order)])

    def load_cotangent():
        return pltpu.make_async_copy(s.cotangent.at[:, 0], s.ups, s.load_sem.at[len(order)])

    load("cond").start()
    load("ada").start()
    pl.when(first)(lambda: load_patches().start())
    for name in order[2:4]:
        load(name).start()

    barrier = pltpu.get_barrier_semaphore()

    def greet(j, c):
        other = lax.rem(me + j, GROUP)
        pl.semaphore_signal(barrier, 1, device_id=(section, spread(other)), device_id_type=MESH)
        return c

    lax.fori_loop(1, GROUP, greet, 0)
    pl.semaphore_signal(barrier, 1, device_id=partner, device_id_type=MESH)

    zero = jnp.zeros((8, features), F32)
    for i in range(micro):
        s.mixed[i, 0:8, :] = zero
        s.mixed[i, length + 8 :, :] = zero
    s.dcv[0:8, :] = zero
    s.dcv[length + 8 :, :] = zero
    s.dwc[...] = zero

    load("cond").wait()
    conds = [s.cond[i : i + 1, :].astype(F32) for i in range(micro)]
    silus = [(v * sigmoid(v)).astype(BF).astype(F32) for v in conds]
    row = lax.broadcasted_iota(jnp.int32, (16, features), 0)
    act_rows = jnp.where(
        row < 6,
        jnp.broadcast_to(silus[0], (16, features)),
        jnp.where(row < 12, jnp.broadcast_to(silus[1], (16, features)), 0.0),
    ).astype(BF)
    s.own_act[...] = act_rows
    s.all_act[lax.rem(me, 2), lax.div(me, 2)] = act_rows
    load("ada").wait()
    for name in order[4:]:
        load(name).start()
    pl.when(second)(lambda: load_cotangent().start())
    for k in range(6):
        m = mm(act_rows, s.ada[:, k * features : (k + 1) * features])
        for i in range(micro):
            s.mod[i, k : k + 1, :] = m[6 * i : 6 * i + 1, :]

    def result_copy(i):
        return pltpu.make_async_remote_copy(
            src_ref=s.result.at[i],
            dst_ref=s.inflow.at[i],
            send_sem=s.hop_send.at[i],
            recv_sem=s.hop_recv.at[i],
            device_id=partner,
            device_id_type=MESH,
        )

    def dx_copy(i):
        return pltpu.make_async_remote_copy(
            src_ref=s.dx.at[i],
            dst_ref=s.ups.at[i],
            send_sem=s.hop_send.at[i],
            recv_sem=s.hop_recv.at[i],
            device_id=partner,
            device_id_type=MESH,
        )

    core, chip = lax.rem(me, 2), lax.div(me, 2)
    chips = GROUP // 2
    beside = (section, spread(me + 1 - 2 * core))

    def gather_copy(j, src, dst, send, recv, received=False):
        other = lax.rem(chip + j, chips)
        slot = other if received else chip
        return pltpu.make_async_remote_copy(
            src_ref=src,
            dst_ref=dst.at[core, slot],
            send_sem=send.at[j],
            recv_sem=recv.at[slot],
            device_id=(section, spread(2 * other + core)),
            device_id_type=MESH,
        )

    def share_copy(src, dst, send, recv, received=False):
        half = dst.at[1 - core if received else core]
        return pltpu.make_async_remote_copy(
            src_ref=half,
            dst_ref=half,
            send_sem=send.at[0],
            recv_sem=recv.at[chips],
            device_id=beside,
            device_id_type=MESH,
        )

    acts = (s.own_act, s.all_act, s.act_send, s.act_recv)
    mods = (s.own_mod, s.all_mod, s.mod_send, s.mod_recv)

    def each_chip(fn):
        def one(j, c):
            fn(j)
            return c

        lax.fori_loop(1, chips, one, 0)

    def share(what):
        each_chip(lambda j: gather_copy(j, *what, received=True).wait_recv())
        share_copy(*what).start()

    def do_forward(i):
        @pl.when(jnp.logical_and(first, i == 0))
        def _():
            load_patches().wait()

        pl.when(second)(lambda: result_copy(i).wait_recv())

        def loaded(name):
            pl.when(i == 0)(lambda: load(name).wait())

        @pl.when(jnp.logical_and(second, i == 0))
        def _():
            load_cotangent().wait()

        forward(s, i, second, s.count[i], loaded)

        @pl.when(i == 0)
        def _():
            pl.semaphore_wait(barrier, GROUP)
            each_chip(lambda j: gather_copy(j, *acts).start())

        pl.when(first)(lambda: result_copy(i).start())

    jobs = {name: Halving(s, name, section, spread, me) for name in PIECES}

    def take(words):
        for word in words:
            if word.startswith("W"):
                weight_gradient(s, word, jobs)
            else:
                jobs[word[:2]].step(int(word[2]))

    def do_backward(i):
        pl.when(first)(lambda: dx_copy(i).wait_recv())
        last = i == micro - 1

        def hook(name):
            @pl.when(jnp.logical_and(first, last))
            def _():
                take(TURNS[name])

        backward(s, i, second, s.count[i], hook)

        @pl.when(second)
        def _():
            dx_copy(i).start()

            @pl.when(last)
            def _():
                for name in ("down", "up", "out", "attend", "proj"):
                    take(TURNS[name])

    def turn(n, c):
        ahead = jnp.logical_or(n == 0, jnp.where(first, n == 1, n == micro))
        i = jnp.where(first, lax.rem(n, micro), lax.div(n, 2))
        pl.when(ahead)(lambda: do_forward(i))
        pl.when(jnp.logical_not(ahead))(lambda: do_backward(i))
        return c

    loop(2 * micro, turn)

    def gather_rows():
        for i in range(micro):
            for k in range(6):
                s.stage[6 * i + k : 6 * i + k + 1, :] = s.dmod[i, k : k + 1, :]
        s.stage[12 : 12 + TAPS, :] = s.dwc[0:TAPS, :]
        s.stage[15:16, :] = jnp.zeros((1, features), F32)
        own = s.stage[...].astype(BF)
        s.own_mod[...] = own
        s.all_mod[core, chip] = own
        each_chip(lambda j: gather_copy(j, *mods).start())
        share(acts)

    cond_copy = pltpu.make_async_remote_copy(
        src_ref=s.own_cond,
        dst_ref=s.got_cond,
        send_sem=s.cond_sem.at[0],
        recv_sem=s.cond_sem.at[1],
        device_id=partner,
        device_id_type=MESH,
    )

    def condition_gradient():
        tot = jnp.zeros((16, features), F32)
        for k in range(6):
            part = nt(s.own_mod[...], s.ada[:, k * features : (k + 1) * features])
            tot = tot + jnp.where(jnp.logical_or(row == k, row == 6 + k), part, 0.0)
        for i in range(micro):
            sg = sigmoid(conds[i])
            slope = sg + conds[i] * sg * (1.0 - sg)
            s.own_cond[i, :, :] = jnp.sum(tot[6 * i : 6 * i + 6], 0, keepdims=True) * slope
        cond_copy.start()

    def image_sums():
        share_copy(*acts, received=True).wait_recv()
        share_copy(*mods, received=True).wait_recv()
        chunk = features // GROUP
        n_rows = GROUP * 16
        flat_act = s.all_act[...].reshape(n_rows, features)
        flat_mod = s.all_mod[...].reshape(n_rows, features)
        pick = (
            lax.broadcasted_iota(jnp.int32, (chunk, features), 1)
            == me * chunk + lax.broadcasted_iota(jnp.int32, (chunk, features), 0)
        ).astype(F32).astype(BF)
        left = nt(pick, flat_act)
        lane = lax.rem(lax.broadcasted_iota(jnp.int32, (chunk, n_rows), 1), 16)
        for k in range(6):
            mine = jnp.logical_or(lane == k, lane == 6 + k)
            s.fin_ada[:, k * features : (k + 1) * features] = mm(
                jnp.where(mine, left, 0.0).astype(BF), flat_mod
            )
        picked = nt(flat_mod, pick).astype(BF)
        tap = lax.broadcasted_iota(jnp.int32, (8, n_rows), 0)
        at_tap = lax.rem(lax.broadcasted_iota(jnp.int32, (8, n_rows), 1), 16) == 12 + tap
        sums = mm(jnp.where(jnp.logical_and(at_tap, tap < TAPS), 1.0, 0.0).astype(BF), picked)
        for j in range(TAPS):
            s.fin_conv[j, :, :] = sums[j : j + 1, :]
        cond_copy.wait()
        s.fin_cond[...] = s.own_cond[...] + s.got_cond[...]

    ends = {"SHARE": lambda: share(mods), "GATHER": gather_rows, "COND": condition_gradient, "ADA": image_sums}
    for word in TURNS["tail"]:
        if word in ends:
            ends[word]()
        else:
            take((word,))

    for i in range(micro):
        pl.when(first)(lambda i=i: result_copy(i).wait_send())
        pl.when(second)(lambda i=i: dx_copy(i).wait_send())
    for job in jobs.values():
        job.end()
    for what in (acts, mods):
        each_chip(lambda j, what=what: gather_copy(j, *what).wait_send())
        share_copy(*what).wait_send()


def finish(n, *refs):
    held, given, sems = refs[:n], refs[n : 2 * n], refs[2 * n]
    outward = [pltpu.make_async_copy(a, b, sems.at[k]) for k, (a, b) in enumerate(zip(held, given))]
    for o in outward:
        o.start()
    for o in outward:
        o.wait()


def body(patches, condition, valid_count, cotangent, ada_weight, conv_weight, proj_weight, out_weight, up_weight, down_weight):
    micro, images, length, features = patches.shape
    hidden = up_weight.shape[2]
    heads = features // HD
    tokens = micro * length
    chunk, deep = features // GROUP, hidden // GROUP
    arrays = dict(
        ada=((features, 6 * features), BF),
        cond=((micro, features), BF),
        wc=((TAPS, features), BF),
        wp=((features, 4 * features), BF),
        wo=((features, features), BF),
        wu=((features, hidden), BF),
        wd=((hidden, features), BF),
        inflow=((micro, length, features), BF),
        ups=((micro, length, features), BF),
        mod=((micro, 8, features), F32),
        dmod=((micro, 8, features), F32),
        dwc=((8, features), F32),
        n1=((micro, length, features), F32),
        r1=((micro, length, 128), F32),
        mixed=((micro, length + 16, features), F32),
        conv=((tokens, features), BF),
        qkv=((micro, length, 3 * features), BF),
        sw=((micro, heads, length, length), BF),
        an=((micro, length, features), F32),
        ra=((micro, length, 128), F32),
        act=((micro, length, features), F32),
        dact=((micro, length, features), F32),
        gated=((tokens, features), BF),
        branch=((micro, length, features), F32),
        hid=((length, features), F32),
        wide_a=((length, features), F32),
        n2=((micro, length, features), F32),
        r2=((micro, length, 128), F32),
        m2=((tokens, features), BF),
        ffn=((micro, length, features), F32),
        ha=((tokens, hidden), BF),
        dgelu=((micro, length, hidden), F32),
        dffn=((tokens, features), BF),
        dpre=((tokens, hidden), BF),
        dbr=((tokens, features), BF),
        datt=((length, features), BF),
        dproj=((tokens, 4 * features), BF),
        dcv=((length + 16, features), F32),
        own_act=((16, features), BF),
        all_act=((2, GROUP // 2, 16, features), BF),
        own_mod=((16, features), BF),
        all_mod=((2, GROUP // 2, 16, features), BF),
        stage=((16, features), F32),
        own_cond=((micro, 1, features), F32),
        got_cond=((micro, 1, features), F32),
    )
    tall = dict(down=hidden, up=features, out=features, proj=features)
    for name, (whole, at, width, order) in PIECES.items():
        arrays["g_" + name] = ((tall[whole], width), BF)
        for k in range(4):
            arrays[f"got{k}_{name}"] = ((tall[whole] >> (k + 1), width), BF)
        arrays["sent_" + name] = ((tall[whole] // GROUP, width), BF)
    sems = dict(
        load_sem=(8,),
        hop_send=(2,),
        hop_recv=(2,),
        rs_send=(len(PIECES), 4),
        rs_recv=(len(PIECES), 4),
        act_send=(GROUP,),
        act_recv=(GROUP,),
        mod_send=(GROUP,),
        mod_recv=(GROUP,),
        cond_sem=(2,),
    )
    names = (*INS, *OUTS, *arrays, *sems)
    any_spec = pl.BlockSpec(memory_space=pl.ANY)
    out_shape = (
        ((1, micro, 1, length, features), BF),
        ((1, micro, 1, length, features), BF),
        ((micro, 1, features), F32),
        ((1, chunk, 6 * features), F32),
        ((TAPS, 1, chunk), F32),
        ((1, chunk, 4 * features), F32),
        ((1, chunk, features), F32),
        ((1, chunk, hidden), F32),
        ((1, deep, features), F32),
    )
    outs = pl.pallas_call(
        lambda *refs: kernel(names, *refs),
        out_shape=[pltpu.VMEM(*o) for o in out_shape],
        in_specs=[pl.BlockSpec(memory_space=pltpu.SMEM if n == "count" else pltpu.HBM) for n in INS],
        out_specs=[pl.BlockSpec(memory_space=pltpu.VMEM)] * len(OUTS),
        scratch_shapes=[pltpu.VMEM(*a) for a in arrays.values()]
        + [pltpu.SemaphoreType.DMA(n) for n in sems.values()],
        compiler_params=pltpu.CompilerParams(
            collective_id=0, has_side_effects=True, vmem_limit_bytes=60000 * 1024
        ),
        name="relay",
    )(
        patches,
        condition.reshape(micro, features),
        valid_count.reshape(micro),
        cotangent, ada_weight, conv_weight, proj_weight, out_weight, up_weight, down_weight)
    outs = pl.pallas_call(
        lambda *refs: finish(len(out_shape), *refs),
        out_shape=[jax.ShapeDtypeStruct(*o) for o in out_shape],
        in_specs=[pl.BlockSpec(memory_space=pltpu.VMEM)] * len(out_shape),
        out_specs=[pl.BlockSpec(memory_space=pltpu.HBM)] * len(out_shape),
        scratch_shapes=[pltpu.SemaphoreType.DMA((len(out_shape),))],
        compiler_params=pltpu.CompilerParams(vmem_limit_bytes=2000 * 1024),
        name="finish",
    )(*outs)
    outs = list(outs)
    outs[4] = outs[4].reshape(1, TAPS, chunk)
    stride = lax.axis_size("dp") // GROUP
    if stride > 1:
        teams = [[t * stride + j for j in range(stride)] for t in range(GROUP)]
        outs = [
            lax.psum_scatter(o, "dp", scatter_dimension=2 if n == 4 else 1, axis_index_groups=teams, tiled=True)
            if n >= 3
            else o
            for n, o in enumerate(outs)
        ]
    return tuple(outs)


def solution(mesh):
    by_section = P("section", None, None)
    placed = (
        P(None, "dp", None, None),
        P(None, "dp", None),
        P(None, "dp"),
        P(None, "dp", None, None),
        *(by_section,) * 6,
    )
    rows_out = P("section", "dp", None)
    return jax.shard_map(
        body,
        mesh=mesh,
        in_specs=placed,
        out_specs=(
            P("section", None, "dp", None, None),
            P("section", None, "dp", None, None),
            P(None, "dp", None),
            rows_out,
            P("section", None, "dp"),
            rows_out,
            rows_out,
            rows_out,
            rows_out,
        ),
        check_vma=False,
    )
```

```python
import jax
import jax.numpy as jnp
from jax import lax
from jax.experimental import pallas as pl
from jax.experimental.pallas import tpu as pltpu
from jax.sharding import PartitionSpec as P

F32, BF = jnp.float32, jnp.bfloat16
HD = 64
TAPS = 3
GROUP = 16
R = 64
MESH = pl.DeviceIdType.MESH
SCALE = HD**-0.5


def mm(a, b):
    return jnp.dot(a, b, preferred_element_type=F32)


def nt(a, b):
    return lax.dot_general(a, b, (((1,), (1,)), ((), ())), preferred_element_type=F32)


def tn(a, b):
    return lax.dot_general(a, b, (((0,), (0,)), ((), ())), preferred_element_type=F32)


def fold(v):
    return jnp.sum(v.reshape(v.shape[0] // 8, 8, v.shape[1]), 0)


def wide(col):
    return jnp.broadcast_to(col, (col.shape[0], 128))


def sigmoid(v):
    return 1.0 / (1.0 + jnp.exp(-v))


def stats(v):
    c = v - jnp.mean(v, -1, keepdims=True)
    s = lax.rsqrt(jnp.mean(c * c, -1, keepdims=True) + 1e-6)
    return c * s, s


def norm_back(g, n, s):
    return s * (g - jnp.mean(g, -1, keepdims=True) - n * jnp.mean(g * n, -1, keepdims=True))


def rows(r, extra=0):
    return pl.ds(r * R, R + extra)


def steps(n, body, init=0):
    for r in range(n):
        init = body(r, init)
    return init


def loop(n, body, init=0):
    return lax.fori_loop(0, n, body, init)


def token_rows(i, length, r=None):
    at, size, unit = (i * length, length, length) if r is None else (i * length + r * R, R, R)
    return pl.ds(at if isinstance(i, int) else pl.multiple_of(at, unit), size)


class Refs:
    def __init__(self, names, refs):
        self.__dict__.update(zip(names, refs, strict=True))


def triangle(second, length):
    sign = (-1 if second else 1) if isinstance(second, bool) else jnp.where(second, -1, 1)
    query = lax.broadcasted_iota(jnp.int32, (length, length), 0)
    key = lax.broadcasted_iota(jnp.int32, (length, length), 1)
    return (query - key) * sign >= 0


def shifted(buf, j, second):
    if isinstance(second, bool):
        return buf[8 + j : 8 + j + R] if second else buf[8 - j : 8 - j + R]
    return jnp.where(second, buf[8 + j : 8 + j + R], buf[8 - j : 8 - j + R])


def nothing(*_):
    return None


def half_rows(h, length):
    return pl.ds(h * (length // 2), length // 2)


def forward(s, i, second, count, loaded, arrive=nothing, depart=nothing):
    length, features = s.inflow.shape[1:]
    hidden = s.wu.shape[1]
    mod = s.mod.at[i]
    tok = token_rows(i, length)

    def trow(r):
        return token_rows(i, length, r)

    def place(r):
        return r * R + lax.broadcasted_iota(jnp.int32, (R, 1), 0)

    def first_norm(r, c):
        n, sc = stats(s.inflow[i, rows(r), :].astype(F32))
        s.n1[i, rows(r), :] = n
        s.r1[i, rows(r), :] = wide(sc)
        m = jnp.where(place(r) < count, n * (1.0 + mod[1:2, :]) + mod[0:1, :], 0.0)
        s.mixed[i, pl.ds(r * R + 8, R), :] = m
        return c

    def conv(r, c):
        buf = s.mixed[i, rows(r, 16), :]
        v = s.wc[0:1, :].astype(F32) * buf[8 : 8 + R]
        for j in range(1, TAPS):
            v = v + s.wc[j : j + 1, :].astype(F32) * shifted(buf, j, second)
        s.conv[trow(r), :] = jnp.where(place(r) < count, v, 0.0).astype(BF)
        return c

    def project(own, out):
        cv = s.conv[own, :]
        for c in range(3):
            p = mm(cv, s.wp[:, c * features : (c + 1) * features])
            s.qkv[i, out, c * features : (c + 1) * features] = (p * SCALE if c == 0 else p).astype(BF)
        s.wide_a[out, :] = mm(cv, s.wp[:, 3 * features :])

    per = length // R // 2
    if second:
        for h in (1, 0):
            arrive(h)
            for r in reversed(range(h * per, (h + 1) * per)):
                first_norm(r, 0)
            loaded("wc" if h else "")
            for r in range(h * per, (h + 1) * per):
                conv(r, 0)
            loaded("wp" if h else "")
            project(pl.ds(i * length + h * (length // 2), length // 2), half_rows(h, length))
    else:
        steps(length // R, first_norm)
        loaded("wc")
        steps(length // R, conv)
        loaded("wp")
        project(tok, slice(None))
    keep = triangle(second, length)
    lane = lax.broadcasted_iota(jnp.int32, (length, 2 * HD), 1) < HD

    def pair(p, c):
        def at(k):
            return pl.ds(k * features + p * 2 * HD, 2 * HD)

        q, k, v = (s.qkv[i, :, at(n)] for n in range(3))
        z = jnp.zeros_like(q)
        tot = None
        for h in range(2):
            mine = lane if h == 0 else jnp.logical_not(lane)
            sw = jnp.where(keep, nt(jnp.where(mine, q, z), k), 0.0).astype(BF)
            s.sw[i, 2 * p + h] = sw
            part = mm(sw, jnp.where(mine, v, z))
            tot = part if tot is None else tot + part
        s.an[i, :, at(0)] = tot
        return c

    steps(features // (2 * HD), pair)

    def gate(r, c):
        a = s.an[i, rows(r), :]
        sc = lax.rsqrt(jnp.mean(a * a, -1, keepdims=True) + 1e-6)
        an = a * sc
        g = s.wide_a[rows(r), :]
        sg = sigmoid(g)
        act = g * sg
        s.an[i, rows(r), :] = an
        s.ra[i, rows(r), :] = wide(sc)
        s.act[i, rows(r), :] = act
        s.dact[i, rows(r), :] = sg + act * (1.0 - sg)
        s.gated[trow(r), :] = (an * act).astype(BF)
        return c

    steps(length // R, gate)
    loaded("wo")
    s.branch[i] = mm(s.gated[tok, :], s.wo[...])

    def second_norm(r, c):
        v = s.inflow[i, rows(r), :].astype(F32) + mod[2:3, :] * s.branch[i, rows(r), :]
        n, sc = stats(v)
        s.hid[rows(r), :] = v
        s.n2[i, rows(r), :] = n
        s.r2[i, rows(r), :] = wide(sc)
        s.m2[trow(r), :] = (n * (1.0 + mod[4:5, :]) + mod[3:4, :]).astype(BF)
        return c

    steps(length // R, second_norm)
    loaded("wu")
    loaded("wd")
    width = 256

    def feed(own, out):
        for c in range(hidden // width):
            at = pl.ds(c * width, width)
            h = mm(s.m2[own, :], s.wu[:, at])
            k0, k1 = 0.7978845608028654, 0.044715
            hh = h * h
            t = jnp.tanh(h * (k0 + (k0 * k1) * hh))
            half = 0.5 * (1.0 + t)
            s.ha[own, at] = (h * half).astype(BF)
            s.dgelu[i, out, at] = half + (0.5 * h) * (1.0 - t * t) * (k0 + (3 * k0 * k1) * hh)
        s.ffn[i, out, :] = mm(s.ha[own, :], s.wd[...])

    def last(r):
        s.result[i, rows(r), :] = (s.hid[rows(r), :] + mod[5:6, :] * s.ffn[i, rows(r), :]).astype(BF)

    if second:
        feed(tok, slice(None))
        for r in range(2 * per):
            last(r)
    else:
        for h in (1, 0):
            feed(pl.ds(i * length + h * (length // 2), length // 2), half_rows(h, length))
            for r in range(h * per, (h + 1) * per):
                last(r)
            depart(h)


def backward(s, i, second, count, hook=nothing, arrive=nothing, depart=nothing):
    length, features = s.inflow.shape[1:]
    hidden = s.wu.shape[1]
    mod, dmod, up = s.mod.at[i], s.dmod.at[i], s.ups.at[i]
    tok = token_rows(i, length)

    def trow(r):
        return token_rows(i, length, r)

    def place(r):
        return r * R + lax.broadcasted_iota(jnp.int32, (R, 1), 0)

    zero = jnp.zeros((8, features), F32)

    def start(r, acc):
        u = up[rows(r), :].astype(F32)
        s.dffn[trow(r), :] = (mod[5:6, :] * u).astype(BF)
        return acc + fold(u * s.ffn[i, rows(r), :])

    width = 256
    per = length // R // 2

    def feed(own, out):
        for c in range(hidden // width):
            at = pl.ds(c * width, width)
            d = nt(s.dffn[own, :], s.wd[at, :])
            s.dpre[own, at] = (d * s.dgelu[i, out, at]).astype(BF)
        s.wide_a[out, :] = nt(s.dpre[own, :], s.wu[...])

    acc = zero
    if second:
        acc = steps(length // R, start, acc)
        feed(tok, slice(None))
    else:
        for h in (0, 1):
            arrive(h)
            for r in range(h * per, (h + 1) * per):
                acc = start(r, acc)
            if h:
                hook("down")
            feed(pl.ds(i * length + h * (length // 2), length // 2), half_rows(h, length))
    dmod[5:6, :] = jnp.sum(acc, 0, keepdims=True)
    hook("up")

    def mid(r, acc):
        dm = s.wide_a[rows(r), :]
        n = s.n2[i, rows(r), :]
        dh = up[rows(r), :].astype(F32) + norm_back(
            dm * (1.0 + mod[4:5, :]), n, s.r2[i, rows(r), :][:, :1]
        )
        s.hid[rows(r), :] = dh
        s.dbr[trow(r), :] = (mod[2:3, :] * dh).astype(BF)
        new = (fold(dm), fold(dm * n), fold(dh * s.branch[i, rows(r), :]))
        return tuple(a + b for a, b in zip(acc, new))

    acc = steps(length // R, mid, (zero,) * 3)
    for k, a in zip((3, 4, 2), acc):
        dmod[k : k + 1, :] = jnp.sum(a, 0, keepdims=True)
    hook("out")
    s.wide_a[...] = nt(s.dbr[tok, :], s.wo[...])

    def gate(r, c):
        dg = s.wide_a[rows(r), :]
        an = s.an[i, rows(r), :]
        dn = dg * s.act[i, rows(r), :]
        s.dproj[trow(r), 3 * features :] = (dg * an * s.dact[i, rows(r), :]).astype(BF)
        da = s.ra[i, rows(r), :][:, :1] * (dn - an * jnp.mean(dn * an, -1, keepdims=True))
        s.datt[rows(r), :] = da.astype(BF)
        return c

    steps(length // R, gate)
    hook("attend")
    keep = triangle(second, length)
    lane = lax.broadcasted_iota(jnp.int32, (length, 2 * HD), 1) < HD

    def pair(p, c):
        def at(k):
            return pl.ds(k * features + p * 2 * HD, 2 * HD)

        q, k, v = (s.qkv[i, :, at(n)] for n in range(3))
        g = s.datt[:, at(0)]
        z = jnp.zeros_like(q)
        dq = dk = dv = None
        for h in range(2):
            mine = lane if h == 0 else jnp.logical_not(lane)
            gm = jnp.where(mine, g, z)
            ds = jnp.where(keep, nt(gm, v), 0.0).astype(BF)
            a = mm(ds, jnp.where(mine, k, z))
            b = tn(ds, jnp.where(mine, q, z))
            e = tn(s.sw[i, 2 * p + h], gm)
            dq = a if dq is None else dq + a
            dk = b if dk is None else dk + b
            dv = e if dv is None else dv + e
        s.dproj[tok, at(0)] = (dq * SCALE).astype(BF)
        s.dproj[tok, at(1)] = dk.astype(BF)
        s.dproj[tok, at(2)] = dv.astype(BF)
        hook(f"pair{p}")
        return c

    steps(features // (2 * HD), pair)
    def mask_rows(r):
        at = pl.ds(r * R + 8, R)
        s.dcv[at, :] = jnp.where(place(r) < count, s.dcv[at, :], 0.0)

    def conv(r, acc):
        dbuf = s.dcv[rows(r, 16), :]
        mbuf = s.mixed[i, rows(r, 16), :]
        here = dbuf[8 : 8 + R]
        d = s.wc[0:1, :].astype(F32) * here
        taps = [fold(here * mbuf[8 : 8 + R])]
        for j in range(1, TAPS):
            d = d + s.wc[j : j + 1, :].astype(F32) * shifted(dbuf, j, (not second) if isinstance(second, bool) else jnp.logical_not(second))
            taps.append(fold(here * shifted(mbuf, j, second)))
        d = jnp.where(place(r) < count, d, 0.0)
        n = s.n1[i, rows(r), :]
        res = s.hid[rows(r), :] + norm_back(d * (1.0 + mod[1:2, :]), n, s.r1[i, rows(r), :][:, :1])
        s.dx[i, rows(r), :] = res.astype(BF)
        return tuple(a + b for a, b in zip(acc, (fold(d), fold(d * n), *taps)))

    acc = (zero,) * (2 + TAPS)
    if second:
        for h in (0, 1):
            own = pl.ds(i * length + h * (length // 2), length // 2)
            s.dcv[h * (length // 2) + 8 : (h + 1) * (length // 2) + 8, :] = nt(s.dproj[own, :], s.wp[...])
            for r in range(h * per, (h + 1) * per):
                mask_rows(r)
            for r in range(h * per, (h + 1) * per):
                acc = conv(r, acc)
            depart(h)
    else:
        s.dcv[8 : length + 8, :] = nt(s.dproj[tok, :], s.wp[...])
        hook("conv")
        for r in range(2 * per):
            mask_rows(r)
        acc = steps(length // R, conv, acc)
    for k in range(2):
        dmod[k : k + 1, :] = jnp.sum(acc[k], 0, keepdims=True)
    for j in range(TAPS):
        s.dwc[j : j + 1, :] += jnp.sum(acc[2 + j], 0, keepdims=True)


ACROSS, ALONG, BETWEEN = (0, 1, 2, 3), (0, 2, 3, 1), (0, 2, 1, 3)
PIECES = {
    "d0": ("down", 0, 128, ACROSS),
    "d1": ("down", 128, 128, BETWEEN),
    "d2": ("down", 256, 128, BETWEEN),
    "u0": ("up", 0, 384, ACROSS),
    "u1": ("up", 384, 128, BETWEEN),
    "u2": ("up", 512, 768, ACROSS),
    "u3": ("up", 1280, 256, ACROSS),
    "o0": ("out", 0, 384, ACROSS),
    "p0": ("proj", 0, 384, ACROSS),
    "p1": ("proj", 384, 512, ACROSS),
    "p2": ("proj", 896, 128, BETWEEN),
    "p3": ("proj", 1024, 256, ACROSS),
    "p4": ("proj", 1280, 256, ACROSS),
}
TURNS = {
    "down": ("Wd",),
    "up": ("d00", "Wu", "d10", "d20"),
    "out": ("Wo",),
    "attend": ("u00", "u10"),
    "pair0": ("u20", "u30", "o00"),
    "pair1": ("d01",),
    "pair2": ("Wp", "d11"),
    "conv": ("u01",),
    "tail": ("p00", "GATHER", "p10", "p20", "p30", "d21", "p40", "COND", "u11", "d02", "u21", "u02", "u31", "p21", "o01", "d12", "d03", "u22", "p01", "u03", "u32", "o02", "SHARE", "d13", "p11", "ADA", "u23", "p31", "p02", "u33", "d22", "o03", "p12", "p41", "u12", "p22", "p32", "p03", "d23", "p13", "p42", "u13", "p23", "p33", "p43"),
}


def spot(chunk, order):
    p = 0
    for bit in order:
        p = 2 * p + ((chunk >> bit) & 1)
    return p


class Halving:
    def __init__(self, s, name, section, spread, me):
        self.whole, self.at, self.width, self.order = PIECES[name]
        self.g = getattr(s, "g_" + name)
        self.got = [getattr(s, f"got{k}_" + name) for k in range(4)]
        self.sent = getattr(s, "sent_" + name)
        self.fin = getattr(s, "fin_" + self.whole).at[:, pl.ds(self.at, self.width)]
        index = list(PIECES).index(name)
        self.send_sem = [s.rs_send.at[index, k] for k in range(4)]
        self.recv_sem = [s.rs_recv.at[index, k] for k in range(4)]
        height = self.g.shape[0]
        low = 0
        self.keep, self.give, self.peer = [], [], []
        self.bit = [lax.rem(lax.div(me, 1 << b), 2) for b in self.order]
        for k, b in enumerate(self.order):
            half = height >> (k + 1)
            step = half if half % 16 == 0 else 8
            self.keep.append(pl.multiple_of(low + self.bit[k] * half, step))
            self.give.append(pl.multiple_of(low + (1 - self.bit[k]) * half, step))
            low = self.keep[-1]
            other = me + (1 - 2 * self.bit[k]) * (1 << b)
            self.peer.append((section, spread(other)))

    def copy(self, k):
        half = self.g.shape[0] >> (k + 1)
        src = self.sent if k == 3 else self.g.at[pl.ds(self.give[k], half)]
        return pltpu.make_async_remote_copy(
            src_ref=src,
            dst_ref=self.got[k],
            send_sem=self.send_sem[k],
            recv_sem=self.recv_sem[k],
            device_id=self.peer[k],
            device_id_type=MESH,
        )

    def start(self, k):
        self.copy(k).start()

    def step(self, k):
        self.copy(k).wait_recv()
        got = self.got[k]
        if k < 2:
            at = pl.ds(self.keep[k], got.shape[0])
            self.g[at, :] = (self.g[at, :].astype(F32) + got[...].astype(F32)).astype(BF)
        elif k == 2:
            part = got.shape[0] // 2
            v = self.g[pl.ds(self.keep[2], 2 * part), :].astype(F32) + got[...].astype(F32)
            upper = self.bit[3] == 1
            self.sent[...] = jnp.where(upper, v[:part], v[part:]).astype(BF)
            self.fin[...] = jnp.where(upper, v[part:], v[:part])
        else:
            self.fin[...] += got[...].astype(F32)
        if k < 3:
            self.start(k + 1)

    def end(self):
        for k in range(4):
            self.copy(k).wait_send()


def group_rows(val, order):
    height = val.shape[0] // GROUP
    at = [0] * GROUP
    for c in range(GROUP):
        at[spot(c, order)] = c
    return jnp.concatenate([val[c * height : (c + 1) * height] for c in at], 0)


def turn_operands(s):
    for left, out in ((s.ha, s.ha_t), (s.m2, s.m2_t), (s.gated, s.gated_t), (s.conv, s.conv_t)):
        width = 384

        def one(c, carry, left=left, out=out):
            at = pl.ds(pl.multiple_of(c * width, width), width)
            out[at, :] = left[:, at].T
            return carry

        loop(left.shape[1] // width, one)


OPERANDS = {"d": ("ha_t", "dffn"), "u": ("m2_t", "dpre"), "o": ("gated_t", "dbr"), "p": ("conv_t", "dproj")}


def first_products(s):
    for letter, (left, right) in OPERANDS.items():
        left, right, out = getattr(s, left), getattr(s, right), getattr(s, "part_" + letter)
        half, width = left.shape[1] // 2, 384
        if left.shape[0] > right.shape[1]:

            def one(c, carry, left=left, right=right, out=out):
                at = pl.ds(pl.multiple_of(c * width, width), width)
                out[at, :] = mm(left[at, :half], right[:half, :])
                return carry

            loop(left.shape[0] // width, one)
        else:

            def one(c, carry, left=left, right=right, out=out):
                at = pl.ds(pl.multiple_of(c * width, width), width)
                out[:, at] = mm(left[:, :half], right[:half, at])
                return carry

            loop(right.shape[1] // width, one)


def weight_gradient(s, letter, jobs, begun):
    mine = [job for name, job in jobs.items() if name[0] == letter]
    left, right = (getattr(s, name) for name in OPERANDS[letter])
    half = left.shape[1] // 2

    def product(at, to):
        if begun:
            return getattr(s, "part_" + letter)[at, to] + mm(left[at, half:], right[half:, to])
        return mm(left[at, :], right[:, to])

    if letter == "d":
        features = right.shape[1]
        chunk = left.shape[0] // GROUP
        per = features // chunk
        for c in range(left.shape[0] // features):
            v = product(slice(c * features, (c + 1) * features), slice(None)).astype(BF)
            for j in range(per):
                for job in mine:
                    p = spot(c * per + j, job.order) * chunk
                    job.g[p : p + chunk, :] = v[j * chunk : (j + 1) * chunk, job.at : job.at + job.width]
    else:
        for job in mine:
            v = product(slice(None), slice(job.at, job.at + job.width))
            job.g[...] = group_rows(v, job.order).astype(BF)
    for job in mine:
        job.start(0)


OUTS = ("o_act", "o_dx", "o_cond", "o_ada", "o_conv", "o_proj", "o_out", "o_up", "o_down")
INS = ("patches", "condition", "count", "cotangent", "w_ada", "w_conv", "w_proj", "w_out", "w_up", "w_down")


def kernel(names, *refs):
    s = Refs(names, refs)
    section, place = lax.axis_index("section"), lax.axis_index("dp")
    stride = lax.axis_size("dp") // GROUP
    me, low = lax.div(place, stride), lax.rem(place, stride)
    first, second = section == 0, section == 1

    def spread(member):
        return member * stride + low

    partner = (1 - section, place)
    micro, length, features = s.inflow.shape
    s.result, s.dx = s.o_act.at[0, :, 0], s.o_dx.at[0, :, 0]
    s.fin_ada, s.fin_conv, s.fin_cond = s.o_ada.at[0], s.o_conv, s.o_cond
    s.fin_proj, s.fin_out, s.fin_up, s.fin_down = (o.at[0] for o in (s.o_proj, s.o_out, s.o_up, s.o_down))

    loads = {
        "ada": (s.w_ada.at[0], s.ada),
        "cond": (s.condition, s.cond),
        "wc": (s.w_conv.at[0], s.wc),
        "wp": (s.w_proj.at[0], s.wp),
        "wo": (s.w_out.at[0], s.wo),
        "wu": (s.w_up.at[0], s.wu),
        "wd": (s.w_down.at[0], s.wd),
    }
    order = list(loads)

    def load(name):
        return pltpu.make_async_copy(*loads[name], s.load_sem.at[order.index(name)])

    def load_patches():
        return pltpu.make_async_copy(s.patches.at[:, 0], s.inflow, s.load_sem.at[len(order)])

    def load_cotangent():
        return pltpu.make_async_copy(s.cotangent.at[:, 0], s.ups, s.load_sem.at[len(order)])

    load("cond").start()
    load("ada").start()
    pl.when(first)(lambda: load_patches().start())
    for name in order[2:4]:
        load(name).start()

    barrier = pltpu.get_barrier_semaphore()

    def greet(j, c):
        other = lax.rem(me + j, GROUP)
        pl.semaphore_signal(barrier, 1, device_id=(section, spread(other)), device_id_type=MESH)
        return c

    lax.fori_loop(1, GROUP, greet, 0)
    pl.semaphore_signal(barrier, 1, device_id=partner, device_id_type=MESH)

    zero = jnp.zeros((8, features), F32)
    for i in range(micro):
        s.mixed[i, 0:8, :] = zero
        s.mixed[i, length + 8 :, :] = zero
    s.dcv[0:8, :] = zero
    s.dcv[length + 8 :, :] = zero
    s.dwc[...] = zero

    load("cond").wait()
    conds = [s.cond[i : i + 1, :].astype(F32) for i in range(micro)]
    silus = [(v * sigmoid(v)).astype(BF).astype(F32) for v in conds]
    row = lax.broadcasted_iota(jnp.int32, (16, features), 0)
    act_rows = jnp.where(
        row < 6,
        jnp.broadcast_to(silus[0], (16, features)),
        jnp.where(row < 12, jnp.broadcast_to(silus[1], (16, features)), 0.0),
    ).astype(BF)
    s.own_act[...] = act_rows
    s.all_act[lax.rem(me, 2), lax.div(me, 2)] = act_rows
    load("ada").wait()
    for name in order[4:]:
        load(name).start()
    pl.when(second)(lambda: load_cotangent().start())
    for k in range(6):
        m = mm(act_rows, s.ada[:, k * features : (k + 1) * features])
        for i in range(micro):
            s.mod[i, k : k + 1, :] = m[6 * i : 6 * i + 1, :]

    def hop(source, target, i, h):
        at = half_rows(h, length)
        return pltpu.make_async_remote_copy(
            src_ref=source.at[i, at],
            dst_ref=target.at[i, at],
            send_sem=s.hop_send.at[i, h],
            recv_sem=s.hop_recv.at[i, h],
            device_id=partner,
            device_id_type=MESH,
        )

    def result_copy(i, h):
        return hop(s.result, s.inflow, i, h)

    def dx_copy(i, h):
        return hop(s.dx, s.ups, i, h)

    core, chip = lax.rem(me, 2), lax.div(me, 2)
    chips = GROUP // 2
    beside = (section, spread(me + 1 - 2 * core))

    def gather_copy(j, src, dst, send, recv, received=False):
        other = lax.rem(chip + j, chips)
        slot = other if received else chip
        return pltpu.make_async_remote_copy(
            src_ref=src,
            dst_ref=dst.at[core, slot],
            send_sem=send.at[j],
            recv_sem=recv.at[slot],
            device_id=(section, spread(2 * other + core)),
            device_id_type=MESH,
        )

    def share_copy(src, dst, send, recv, received=False):
        half = dst.at[1 - core if received else core]
        return pltpu.make_async_remote_copy(
            src_ref=half,
            dst_ref=half,
            send_sem=send.at[0],
            recv_sem=recv.at[chips],
            device_id=beside,
            device_id_type=MESH,
        )

    acts = (s.own_act, s.all_act, s.act_send, s.act_recv)
    mods = (s.own_mod, s.all_mod, s.mod_send, s.mod_recv)

    def each_chip(fn):
        def one(j, c):
            fn(j)
            return c

        lax.fori_loop(1, chips, one, 0)

    def share(what):
        each_chip(lambda j: gather_copy(j, *what, received=True).wait_recv())
        share_copy(*what).start()

    jobs = {name: Halving(s, name, section, spread, me) for name in PIECES}

    def take(words, begun=False):
        for word in words:
            if word.startswith("W"):
                weight_gradient(s, word[1], jobs, begun)
            else:
                jobs[word[:2]].step(int(word[2]))

    def loaded(name):
        if name:
            load(name).wait()

    @pl.when(first)
    def _():
        load_patches().wait()
        for i in range(micro):

            def depart(h, i=i):
                if i == 0 and h == 1:
                    pl.semaphore_wait(barrier, GROUP)
                result_copy(i, h).start()

            forward(s, i, False, s.count[i], nothing if i else loaded, depart=depart)
        each_chip(lambda j: gather_copy(j, *acts).start())
        turn_operands(s)
        for i in range(micro):
            ending = i == micro - 1
            if ending:
                first_products(s)
            backward(
                s,
                i,
                False,
                s.count[i],
                (lambda name: take(TURNS[name], True) if name in TURNS else None) if ending else nothing,
                arrive=lambda h, i=i: dx_copy(i, h).wait_recv(),
            )

    @pl.when(second)
    def _():
        pl.semaphore_wait(barrier, GROUP)
        each_chip(lambda j: gather_copy(j, *acts).start())
        for i in range(micro):
            forward(
                s, i, True, s.count[i], nothing if i else loaded, arrive=lambda h, i=i: result_copy(i, h).wait_recv()
            )
            if i == 0:
                load_cotangent().wait()
            backward(s, i, True, s.count[i], depart=lambda h, i=i: dx_copy(i, h).start())
        turn_operands(s)
        for name in TURNS:
            if name != "tail":
                take(TURNS[name])

    def gather_rows():
        for i in range(micro):
            for k in range(6):
                s.stage[6 * i + k : 6 * i + k + 1, :] = s.dmod[i, k : k + 1, :]
        s.stage[12 : 12 + TAPS, :] = s.dwc[0:TAPS, :]
        s.stage[15:16, :] = jnp.zeros((1, features), F32)
        own = s.stage[...].astype(BF)
        s.own_mod[...] = own
        s.all_mod[core, chip] = own
        each_chip(lambda j: gather_copy(j, *mods).start())
        share(acts)

    cond_copy = pltpu.make_async_remote_copy(
        src_ref=s.own_cond,
        dst_ref=s.got_cond,
        send_sem=s.cond_sem.at[0],
        recv_sem=s.cond_sem.at[1],
        device_id=partner,
        device_id_type=MESH,
    )

    def condition_gradient():
        tot = jnp.zeros((16, features), F32)
        for k in range(6):
            part = nt(s.own_mod[...], s.ada[:, k * features : (k + 1) * features])
            tot = tot + jnp.where(jnp.logical_or(row == k, row == 6 + k), part, 0.0)
        for i in range(micro):
            sg = sigmoid(conds[i])
            slope = sg + conds[i] * sg * (1.0 - sg)
            s.own_cond[i, :, :] = jnp.sum(tot[6 * i : 6 * i + 6], 0, keepdims=True) * slope
        cond_copy.start()

    def image_sums():
        share_copy(*acts, received=True).wait_recv()
        share_copy(*mods, received=True).wait_recv()
        chunk = features // GROUP
        n_rows = GROUP * 16
        flat_act = s.all_act[...].reshape(n_rows, features)
        flat_mod = s.all_mod[...].reshape(n_rows, features)
        pick = (
            lax.broadcasted_iota(jnp.int32, (chunk, features), 1)
            == me * chunk + lax.broadcasted_iota(jnp.int32, (chunk, features), 0)
        ).astype(F32).astype(BF)
        left = nt(pick, flat_act)
        lane = lax.rem(lax.broadcasted_iota(jnp.int32, (chunk, n_rows), 1), 16)
        for k in range(6):
            mine = jnp.logical_or(lane == k, lane == 6 + k)
            s.fin_ada[:, k * features : (k + 1) * features] = mm(
                jnp.where(mine, left, 0.0).astype(BF), flat_mod
            )
        picked = nt(flat_mod, pick).astype(BF)
        tap = lax.broadcasted_iota(jnp.int32, (8, n_rows), 0)
        at_tap = lax.rem(lax.broadcasted_iota(jnp.int32, (8, n_rows), 1), 16) == 12 + tap
        sums = mm(jnp.where(jnp.logical_and(at_tap, tap < TAPS), 1.0, 0.0).astype(BF), picked)
        for j in range(TAPS):
            s.fin_conv[j, :, :] = sums[j : j + 1, :]
        cond_copy.wait()
        s.fin_cond[...] = s.own_cond[...] + s.got_cond[...]

    ends = {"SHARE": lambda: share(mods), "GATHER": gather_rows, "COND": condition_gradient, "ADA": image_sums}
    for word in TURNS["tail"]:
        if word in ends:
            ends[word]()
        else:
            take((word,))

    for i in range(micro):
        for h in range(2):
            pl.when(first)(lambda i=i, h=h: result_copy(i, h).wait_send())
            pl.when(second)(lambda i=i, h=h: dx_copy(i, h).wait_send())
    for job in jobs.values():
        job.end()
    for what in (acts, mods):
        each_chip(lambda j, what=what: gather_copy(j, *what).wait_send())
        share_copy(*what).wait_send()


def finish(n, *refs):
    held, given, sems = refs[:n], refs[n : 2 * n], refs[2 * n]
    outward = [pltpu.make_async_copy(a, b, sems.at[k]) for k, (a, b) in enumerate(zip(held, given))]
    for o in outward:
        o.start()
    for o in outward:
        o.wait()


def body(patches, condition, valid_count, cotangent, ada_weight, conv_weight, proj_weight, out_weight, up_weight, down_weight):
    micro, images, length, features = patches.shape
    hidden = up_weight.shape[2]
    heads = features // HD
    tokens = micro * length
    chunk, deep = features // GROUP, hidden // GROUP
    arrays = dict(
        ada=((features, 6 * features), BF),
        cond=((micro, features), BF),
        wc=((TAPS, features), BF),
        wp=((features, 4 * features), BF),
        wo=((features, features), BF),
        wu=((features, hidden), BF),
        wd=((hidden, features), BF),
        inflow=((micro, length, features), BF),
        ups=((micro, length, features), BF),
        mod=((micro, 8, features), F32),
        dmod=((micro, 8, features), F32),
        dwc=((8, features), F32),
        n1=((micro, length, features), F32),
        r1=((micro, length, 128), F32),
        mixed=((micro, length + 16, features), F32),
        conv=((tokens, features), BF),
        qkv=((micro, length, 3 * features), BF),
        sw=((micro, heads, length, length), BF),
        an=((micro, length, features), F32),
        ra=((micro, length, 128), F32),
        act=((micro, length, features), F32),
        dact=((micro, length, features), F32),
        gated=((tokens, features), BF),
        branch=((micro, length, features), F32),
        hid=((length, features), F32),
        wide_a=((length, features), F32),
        n2=((micro, length, features), F32),
        r2=((micro, length, 128), F32),
        m2=((tokens, features), BF),
        ffn=((micro, length, features), F32),
        ha=((tokens, hidden), BF),
        ha_t=((hidden, tokens), BF),
        m2_t=((features, tokens), BF),
        gated_t=((features, tokens), BF),
        conv_t=((features, tokens), BF),
        part_d=((hidden, features), F32),
        part_u=((features, hidden), F32),
        part_o=((features, features), F32),
        part_p=((features, 4 * features), F32),
        dgelu=((micro, length, hidden), F32),
        dffn=((tokens, features), BF),
        dpre=((tokens, hidden), BF),
        dbr=((tokens, features), BF),
        datt=((length, features), BF),
        dproj=((tokens, 4 * features), BF),
        dcv=((length + 16, features), F32),
        own_act=((16, features), BF),
        all_act=((2, GROUP // 2, 16, features), BF),
        own_mod=((16, features), BF),
        all_mod=((2, GROUP // 2, 16, features), BF),
        stage=((16, features), F32),
        own_cond=((micro, 1, features), F32),
        got_cond=((micro, 1, features), F32),
    )
    tall = dict(down=hidden, up=features, out=features, proj=features)
    for name, (whole, at, width, order) in PIECES.items():
        arrays["g_" + name] = ((tall[whole], width), BF)
        for k in range(4):
            arrays[f"got{k}_{name}"] = ((tall[whole] >> (k + 1), width), BF)
        arrays["sent_" + name] = ((tall[whole] // GROUP, width), BF)
    sems = dict(
        load_sem=(8,),
        hop_send=(2, 2),
        hop_recv=(2, 2),
        rs_send=(len(PIECES), 4),
        rs_recv=(len(PIECES), 4),
        act_send=(GROUP,),
        act_recv=(GROUP,),
        mod_send=(GROUP,),
        mod_recv=(GROUP,),
        cond_sem=(2,),
    )
    names = (*INS, *OUTS, *arrays, *sems)
    any_spec = pl.BlockSpec(memory_space=pl.ANY)
    out_shape = (
        ((1, micro, 1, length, features), BF),
        ((1, micro, 1, length, features), BF),
        ((micro, 1, features), F32),
        ((1, chunk, 6 * features), F32),
        ((TAPS, 1, chunk), F32),
        ((1, chunk, 4 * features), F32),
        ((1, chunk, features), F32),
        ((1, chunk, hidden), F32),
        ((1, deep, features), F32),
    )
    outs = pl.pallas_call(
        lambda *refs: kernel(names, *refs),
        out_shape=[pltpu.VMEM(*o) for o in out_shape],
        in_specs=[pl.BlockSpec(memory_space=pltpu.SMEM if n == "count" else pltpu.HBM) for n in INS],
        out_specs=[pl.BlockSpec(memory_space=pltpu.VMEM)] * len(OUTS),
        scratch_shapes=[pltpu.VMEM(*a) for a in arrays.values()]
        + [pltpu.SemaphoreType.DMA(n) for n in sems.values()],
        compiler_params=pltpu.CompilerParams(
            collective_id=0, has_side_effects=True, vmem_limit_bytes=60000 * 1024
        ),
        name="relay",
    )(
        patches,
        condition.reshape(micro, features),
        valid_count.reshape(micro),
        cotangent, ada_weight, conv_weight, proj_weight, out_weight, up_weight, down_weight)
    outs = pl.pallas_call(
        lambda *refs: finish(len(out_shape), *refs),
        out_shape=[jax.ShapeDtypeStruct(*o) for o in out_shape],
        in_specs=[pl.BlockSpec(memory_space=pltpu.VMEM)] * len(out_shape),
        out_specs=[pl.BlockSpec(memory_space=pltpu.HBM)] * len(out_shape),
        scratch_shapes=[pltpu.SemaphoreType.DMA((len(out_shape),))],
        compiler_params=pltpu.CompilerParams(vmem_limit_bytes=2000 * 1024),
        name="finish",
    )(*outs)
    outs = list(outs)
    outs[4] = outs[4].reshape(1, TAPS, chunk)
    stride = lax.axis_size("dp") // GROUP
    if stride > 1:
        teams = [[t * stride + j for j in range(stride)] for t in range(GROUP)]
        outs = [
            lax.psum_scatter(o, "dp", scatter_dimension=2 if n == 4 else 1, axis_index_groups=teams, tiled=True)
            if n >= 3
            else o
            for n, o in enumerate(outs)
        ]
    return tuple(outs)


def solution(mesh):
    by_section = P("section", None, None)
    placed = (
        P(None, "dp", None, None),
        P(None, "dp", None),
        P(None, "dp"),
        P(None, "dp", None, None),
        *(by_section,) * 6,
    )
    rows_out = P("section", "dp", None)
    return jax.shard_map(
        body,
        mesh=mesh,
        in_specs=placed,
        out_specs=(
            P("section", None, "dp", None, None),
            P("section", None, "dp", None, None),
            P(None, "dp", None),
            rows_out,
            P("section", None, "dp"),
            rows_out,
            rows_out,
            rows_out,
            rows_out,
        ),
        check_vma=False,
    )
```

```python
import jax
import jax.numpy as jnp
from jax import lax
from jax.experimental import pallas as pl
from jax.experimental.pallas import tpu as pltpu
from jax.sharding import PartitionSpec as P

F32, BF = jnp.float32, jnp.bfloat16
HD = 64
TAPS = 3
GROUP = 16
R = 64
MESH = pl.DeviceIdType.MESH
SCALE = HD**-0.5


def mm(a, b):
    return jnp.dot(a, b, preferred_element_type=F32)


def nt(a, b):
    return lax.dot_general(a, b, (((1,), (1,)), ((), ())), preferred_element_type=F32)


def tn(a, b):
    return lax.dot_general(a, b, (((0,), (0,)), ((), ())), preferred_element_type=F32)


def fold(v):
    return jnp.sum(v.reshape(v.shape[0] // 8, 8, v.shape[1]), 0)


def wide(col):
    return jnp.broadcast_to(col, (col.shape[0], 128))


def sigmoid(v):
    return 1.0 / (1.0 + jnp.exp(-v))


def stats(v):
    c = v - jnp.mean(v, -1, keepdims=True)
    s = lax.rsqrt(jnp.mean(c * c, -1, keepdims=True) + 1e-6)
    return c * s, s


def norm_back(g, n, s):
    return s * (g - jnp.mean(g, -1, keepdims=True) - n * jnp.mean(g * n, -1, keepdims=True))


def rows(r, extra=0):
    return pl.ds(r * R, R + extra)


def steps(n, body, init=0):
    for r in range(n):
        init = body(r, init)
    return init


def loop(n, body, init=0):
    return lax.fori_loop(0, n, body, init)


def token_rows(i, length, r=None):
    at, size, unit = (i * length, length, length) if r is None else (i * length + r * R, R, R)
    return pl.ds(at if isinstance(i, int) else pl.multiple_of(at, unit), size)


class Refs:
    def __init__(self, names, refs):
        self.__dict__.update(zip(names, refs, strict=True))


def triangle(second, length):
    sign = (-1 if second else 1) if isinstance(second, bool) else jnp.where(second, -1, 1)
    query = lax.broadcasted_iota(jnp.int32, (length, length), 0)
    key = lax.broadcasted_iota(jnp.int32, (length, length), 1)
    return (query - key) * sign >= 0


def shifted(buf, j, second):
    if isinstance(second, bool):
        return buf[8 + j : 8 + j + R] if second else buf[8 - j : 8 - j + R]
    return jnp.where(second, buf[8 + j : 8 + j + R], buf[8 - j : 8 - j + R])


def nothing(*_):
    return None


def half_rows(h, length):
    return pl.ds(h * (length // 2), length // 2)


def forward(s, i, second, count, loaded, arrive=nothing, depart=nothing):
    length, features = s.inflow.shape[1:]
    hidden = s.wu.shape[1]
    mod = s.mod.at[i]
    tok = token_rows(i, length)

    def trow(r):
        return token_rows(i, length, r)

    def place(r):
        return r * R + lax.broadcasted_iota(jnp.int32, (R, 1), 0)

    def first_norm(r, c):
        n, sc = stats(s.inflow[i, rows(r), :].astype(F32))
        s.n1[i, rows(r), :] = n
        s.r1[i, rows(r), :] = wide(sc)
        m = jnp.where(place(r) < count, n * (1.0 + mod[1:2, :]) + mod[0:1, :], 0.0)
        s.mixed[i, pl.ds(r * R + 8, R), :] = m
        return c

    def conv(r, c):
        buf = s.mixed[i, rows(r, 16), :]
        v = s.wc[0:1, :].astype(F32) * buf[8 : 8 + R]
        for j in range(1, TAPS):
            v = v + s.wc[j : j + 1, :].astype(F32) * shifted(buf, j, second)
        s.conv[trow(r), :] = jnp.where(place(r) < count, v, 0.0).astype(BF)
        return c

    def project(own, out):
        cv = s.conv[own, :]
        for c in range(3):
            p = mm(cv, s.wp[:, c * features : (c + 1) * features])
            s.qkv[i, out, c * features : (c + 1) * features] = (p * SCALE if c == 0 else p).astype(BF)
        s.wide_a[out, :] = mm(cv, s.wp[:, 3 * features :])

    per = length // R // 2
    if second:
        for h in (1, 0):
            arrive(h)
            for r in reversed(range(h * per, (h + 1) * per)):
                first_norm(r, 0)
            loaded("wc" if h else "")
            for r in range(h * per, (h + 1) * per):
                conv(r, 0)
            loaded("wp" if h else "")
            project(pl.ds(i * length + h * (length // 2), length // 2), half_rows(h, length))
    else:
        steps(length // R, first_norm)
        loaded("wc")
        steps(length // R, conv)
        loaded("wp")
        project(tok, slice(None))
    keep = triangle(second, length)
    lane = lax.broadcasted_iota(jnp.int32, (length, 2 * HD), 1) < HD

    def pair(p, c):
        def at(k):
            return pl.ds(k * features + p * 2 * HD, 2 * HD)

        q, k, v = (s.qkv[i, :, at(n)] for n in range(3))
        z = jnp.zeros_like(q)
        tot = None
        for h in range(2):
            mine = lane if h == 0 else jnp.logical_not(lane)
            sw = jnp.where(keep, nt(jnp.where(mine, q, z), k), 0.0).astype(BF)
            s.sw[i, 2 * p + h] = sw
            part = mm(sw, jnp.where(mine, v, z))
            tot = part if tot is None else tot + part
        s.an[i, :, at(0)] = tot
        return c

    steps(features // (2 * HD), pair)

    def gate(r, c):
        a = s.an[i, rows(r), :]
        sc = lax.rsqrt(jnp.mean(a * a, -1, keepdims=True) + 1e-6)
        an = a * sc
        g = s.wide_a[rows(r), :]
        sg = sigmoid(g)
        act = g * sg
        s.an[i, rows(r), :] = an
        s.ra[i, rows(r), :] = wide(sc)
        s.act[i, rows(r), :] = act
        s.dact[i, rows(r), :] = sg + act * (1.0 - sg)
        s.gated[trow(r), :] = (an * act).astype(BF)
        return c

    steps(length // R, gate)
    loaded("wo")
    s.branch[i] = mm(s.gated[tok, :], s.wo[...])

    def second_norm(r, c):
        v = s.inflow[i, rows(r), :].astype(F32) + mod[2:3, :] * s.branch[i, rows(r), :]
        n, sc = stats(v)
        s.hid[rows(r), :] = v
        s.n2[i, rows(r), :] = n
        s.r2[i, rows(r), :] = wide(sc)
        s.m2[trow(r), :] = (n * (1.0 + mod[4:5, :]) + mod[3:4, :]).astype(BF)
        return c

    steps(length // R, second_norm)
    loaded("wu")
    loaded("wd")
    width = 256

    def feed(own, out):
        for c in range(hidden // width):
            at = pl.ds(c * width, width)
            h = mm(s.m2[own, :], s.wu[:, at])
            k0, k1 = 0.7978845608028654, 0.044715
            hh = h * h
            t = jnp.tanh(h * (k0 + (k0 * k1) * hh))
            half = 0.5 * (1.0 + t)
            s.ha[own, at] = (h * half).astype(BF)
            s.dgelu[i, out, at] = half + (0.5 * h) * (1.0 - t * t) * (k0 + (3 * k0 * k1) * hh)
        s.ffn[i, out, :] = mm(s.ha[own, :], s.wd[...])

    def last(r):
        s.result[i, rows(r), :] = (s.hid[rows(r), :] + mod[5:6, :] * s.ffn[i, rows(r), :]).astype(BF)

    if second:
        feed(tok, slice(None))
        for r in range(2 * per):
            last(r)
    else:
        for h in (1, 0):
            feed(pl.ds(i * length + h * (length // 2), length // 2), half_rows(h, length))
            for r in range(h * per, (h + 1) * per):
                last(r)
            depart(h)


def backward(s, i, second, count, hook=nothing, arrive=nothing, depart=None):
    length, features = s.inflow.shape[1:]
    hidden = s.wu.shape[1]
    mod, dmod, up = s.mod.at[i], s.dmod.at[i], s.ups.at[i]
    tok = token_rows(i, length)

    def trow(r):
        return token_rows(i, length, r)

    def place(r):
        return r * R + lax.broadcasted_iota(jnp.int32, (R, 1), 0)

    zero = jnp.zeros((8, features), F32)

    def start(r, acc):
        u = up[rows(r), :].astype(F32)
        s.dffn[trow(r), :] = (mod[5:6, :] * u).astype(BF)
        return acc + fold(u * s.ffn[i, rows(r), :])

    width = 256
    per = length // R // 2

    def feed(own, out):
        for c in range(hidden // width):
            at = pl.ds(c * width, width)
            d = nt(s.dffn[own, :], s.wd[at, :])
            s.dpre[own, at] = (d * s.dgelu[i, out, at]).astype(BF)
        s.wide_a[out, :] = nt(s.dpre[own, :], s.wu[...])

    acc = zero
    for h in range(2):
        arrive(h)
        for r in range(h * per, (h + 1) * per):
            acc = start(r, acc)
    hook("down")
    feed(tok, slice(None))
    dmod[5:6, :] = jnp.sum(acc, 0, keepdims=True)
    hook("up")

    def mid(r, acc):
        dm = s.wide_a[rows(r), :]
        n = s.n2[i, rows(r), :]
        dh = up[rows(r), :].astype(F32) + norm_back(
            dm * (1.0 + mod[4:5, :]), n, s.r2[i, rows(r), :][:, :1]
        )
        s.hid[rows(r), :] = dh
        s.dbr[trow(r), :] = (mod[2:3, :] * dh).astype(BF)
        new = (fold(dm), fold(dm * n), fold(dh * s.branch[i, rows(r), :]))
        return tuple(a + b for a, b in zip(acc, new))

    acc = steps(length // R, mid, (zero,) * 3)
    for k, a in zip((3, 4, 2), acc):
        dmod[k : k + 1, :] = jnp.sum(a, 0, keepdims=True)
    hook("out")
    s.wide_a[...] = nt(s.dbr[tok, :], s.wo[...])

    def gate(r, c):
        dg = s.wide_a[rows(r), :]
        an = s.an[i, rows(r), :]
        dn = dg * s.act[i, rows(r), :]
        s.dproj[trow(r), 3 * features :] = (dg * an * s.dact[i, rows(r), :]).astype(BF)
        da = s.ra[i, rows(r), :][:, :1] * (dn - an * jnp.mean(dn * an, -1, keepdims=True))
        s.datt[rows(r), :] = da.astype(BF)
        return c

    steps(length // R, gate)
    hook("attend")
    keep = triangle(second, length)
    lane = lax.broadcasted_iota(jnp.int32, (length, 2 * HD), 1) < HD

    def pair(p, c):
        def at(k):
            return pl.ds(k * features + p * 2 * HD, 2 * HD)

        q, k, v = (s.qkv[i, :, at(n)] for n in range(3))
        g = s.datt[:, at(0)]
        z = jnp.zeros_like(q)
        dq = dk = dv = None
        for h in range(2):
            mine = lane if h == 0 else jnp.logical_not(lane)
            gm = jnp.where(mine, g, z)
            ds = jnp.where(keep, nt(gm, v), 0.0).astype(BF)
            a = mm(ds, jnp.where(mine, k, z))
            b = tn(ds, jnp.where(mine, q, z))
            e = tn(s.sw[i, 2 * p + h], gm)
            dq = a if dq is None else dq + a
            dk = b if dk is None else dk + b
            dv = e if dv is None else dv + e
        s.dproj[tok, at(0)] = (dq * SCALE).astype(BF)
        s.dproj[tok, at(1)] = dk.astype(BF)
        s.dproj[tok, at(2)] = dv.astype(BF)
        hook(f"pair{p}")
        return c

    steps(features // (2 * HD), pair)
    def mask_rows(r):
        at = pl.ds(r * R + 8, R)
        s.dcv[at, :] = jnp.where(place(r) < count, s.dcv[at, :], 0.0)

    def conv(r, acc):
        dbuf = s.dcv[rows(r, 16), :]
        mbuf = s.mixed[i, rows(r, 16), :]
        here = dbuf[8 : 8 + R]
        d = s.wc[0:1, :].astype(F32) * here
        taps = [fold(here * mbuf[8 : 8 + R])]
        for j in range(1, TAPS):
            d = d + s.wc[j : j + 1, :].astype(F32) * shifted(dbuf, j, (not second) if isinstance(second, bool) else jnp.logical_not(second))
            taps.append(fold(here * shifted(mbuf, j, second)))
        d = jnp.where(place(r) < count, d, 0.0)
        n = s.n1[i, rows(r), :]
        res = s.hid[rows(r), :] + norm_back(d * (1.0 + mod[1:2, :]), n, s.r1[i, rows(r), :][:, :1])
        s.dx[i, rows(r), :] = res.astype(BF)
        return tuple(a + b for a, b in zip(acc, (fold(d), fold(d * n), *taps)))

    acc = (zero,) * (2 + TAPS)
    if depart:
        for h in (0, 1):
            own = pl.ds(i * length + h * (length // 2), length // 2)
            s.dcv[h * (length // 2) + 8 : (h + 1) * (length // 2) + 8, :] = nt(s.dproj[own, :], s.wp[...])
            for r in range(h * per, (h + 1) * per):
                mask_rows(r)
            for r in range(h * per, (h + 1) * per):
                acc = conv(r, acc)
            depart(h)
    else:
        s.dcv[8 : length + 8, :] = nt(s.dproj[tok, :], s.wp[...])
        hook("conv")
        for r in range(2 * per):
            mask_rows(r)
        acc = steps(length // R, conv, acc)
    for k in range(2):
        dmod[k : k + 1, :] = jnp.sum(acc[k], 0, keepdims=True)
    for j in range(TAPS):
        s.dwc[j : j + 1, :] += jnp.sum(acc[2 + j], 0, keepdims=True)


ACROSS, ALONG, BETWEEN = (0, 1, 2, 3), (0, 2, 3, 1), (0, 2, 1, 3)
PIECES = {
    "d0": ("down", 0, 128, ACROSS),
    "d1": ("down", 128, 128, BETWEEN),
    "d2": ("down", 256, 128, BETWEEN),
    "u0": ("up", 0, 384, ACROSS),
    "u1": ("up", 384, 256, BETWEEN),
    "u2": ("up", 640, 640, ACROSS),
    "u3": ("up", 1280, 256, ACROSS),
    "o0": ("out", 0, 384, ACROSS),
    "p0": ("proj", 0, 384, ACROSS),
    "p1": ("proj", 384, 384, ACROSS),
    "p2": ("proj", 768, 256, BETWEEN),
    "p3": ("proj", 1024, 256, ACROSS),
    "p4": ("proj", 1280, 256, ACROSS),
}
TURNS = {
    "down": ("Wd",),
    "up": ("d00", "Wu", "d10", "d20"),
    "out": ("Wo",),
    "attend": ("u00", "u10"),
    "pair0": ("u20", "u30", "o00"),
    "pair1": ("d01",),
    "pair2": ("Wp", "d11"),
    "conv": ("u01",),
    "tail": ("p00", "p10", "GATHER", "p20", "p30", "d21", "p40", "COND", "u11", "u21", "d02", "u31", "u02", "o01", "d12", "p21", "p01", "u22", "d03", "u32", "p11", "u03", "o02", "d13", "SHARE", "p31", "p02", "d22", "u23", "ADA", "p41", "u33", "p12", "u12", "p22", "o03", "p32", "p03", "d23", "p42", "p13", "u13", "p23", "p33", "p43"),
}


def spot(chunk, order):
    p = 0
    for bit in order:
        p = 2 * p + ((chunk >> bit) & 1)
    return p


class Halving:
    def __init__(self, s, name, section, spread, me):
        self.whole, self.at, self.width, self.order = PIECES[name]
        self.g = getattr(s, "g_" + name)
        self.got = [getattr(s, f"got{k}_" + name) for k in range(4)]
        self.sent = getattr(s, "sent_" + name)
        self.fin = getattr(s, "fin_" + self.whole).at[:, pl.ds(self.at, self.width)]
        index = list(PIECES).index(name)
        self.send_sem = [s.rs_send.at[index, k] for k in range(4)]
        self.recv_sem = [s.rs_recv.at[index, k] for k in range(4)]
        height = self.g.shape[0]
        low = 0
        self.keep, self.give, self.peer = [], [], []
        self.bit = [lax.rem(lax.div(me, 1 << b), 2) for b in self.order]
        for k, b in enumerate(self.order):
            half = height >> (k + 1)
            step = half if half % 16 == 0 else 8
            self.keep.append(pl.multiple_of(low + self.bit[k] * half, step))
            self.give.append(pl.multiple_of(low + (1 - self.bit[k]) * half, step))
            low = self.keep[-1]
            other = me + (1 - 2 * self.bit[k]) * (1 << b)
            self.peer.append((section, spread(other)))

    def copy(self, k):
        half = self.g.shape[0] >> (k + 1)
        src = self.sent if k == 3 else self.g.at[pl.ds(self.give[k], half)]
        return pltpu.make_async_remote_copy(
            src_ref=src,
            dst_ref=self.got[k],
            send_sem=self.send_sem[k],
            recv_sem=self.recv_sem[k],
            device_id=self.peer[k],
            device_id_type=MESH,
        )

    def start(self, k):
        self.copy(k).start()

    def step(self, k):
        self.copy(k).wait_recv()
        got = self.got[k]
        if k < 2:
            at = pl.ds(self.keep[k], got.shape[0])
            self.g[at, :] = (self.g[at, :].astype(F32) + got[...].astype(F32)).astype(BF)
        elif k == 2:
            part = got.shape[0] // 2
            v = self.g[pl.ds(self.keep[2], 2 * part), :].astype(F32) + got[...].astype(F32)
            upper = self.bit[3] == 1
            self.sent[...] = jnp.where(upper, v[:part], v[part:]).astype(BF)
            self.fin[...] = jnp.where(upper, v[part:], v[:part])
        else:
            self.fin[...] += got[...].astype(F32)
        if k < 3:
            self.start(k + 1)

    def end(self):
        for k in range(4):
            self.copy(k).wait_send()


def group_rows(val, order):
    height = val.shape[0] // GROUP
    at = [0] * GROUP
    for c in range(GROUP):
        at[spot(c, order)] = c
    return jnp.concatenate([val[c * height : (c + 1) * height] for c in at], 0)


def turn_operands(s):
    for left, out in ((s.ha, s.ha_t), (s.m2, s.m2_t), (s.gated, s.gated_t), (s.conv, s.conv_t)):
        width = 384

        def one(c, carry, left=left, out=out):
            at = pl.ds(pl.multiple_of(c * width, width), width)
            out[at, :] = left[:, at].T
            return carry

        loop(left.shape[1] // width, one)


OPERANDS = {"d": ("ha_t", "dffn"), "u": ("m2_t", "dpre"), "o": ("gated_t", "dbr"), "p": ("conv_t", "dproj")}


def first_products(s):
    for letter, (left, right) in OPERANDS.items():
        left, right, out = getattr(s, left), getattr(s, right), getattr(s, "part_" + letter)
        half, width = left.shape[1] // 2, 384
        if left.shape[0] > right.shape[1]:

            def one(c, carry, left=left, right=right, out=out):
                at = pl.ds(pl.multiple_of(c * width, width), width)
                out[at, :] = mm(left[at, :half], right[:half, :])
                return carry

            loop(left.shape[0] // width, one)
        else:

            def one(c, carry, left=left, right=right, out=out):
                at = pl.ds(pl.multiple_of(c * width, width), width)
                out[:, at] = mm(left[:, :half], right[:half, at])
                return carry

            loop(right.shape[1] // width, one)


def weight_gradient(s, letter, jobs, begun):
    mine = [job for name, job in jobs.items() if name[0] == letter]
    left, right = (getattr(s, name) for name in OPERANDS[letter])
    half = left.shape[1] // 2

    def product(at, to):
        if begun:
            return getattr(s, "part_" + letter)[at, to] + mm(left[at, half:], right[half:, to])
        return mm(left[at, :], right[:, to])

    if letter == "d":
        features = right.shape[1]
        chunk = left.shape[0] // GROUP
        per = features // chunk
        for c in range(left.shape[0] // features):
            v = product(slice(c * features, (c + 1) * features), slice(None)).astype(BF)
            for j in range(per):
                for job in mine:
                    p = spot(c * per + j, job.order) * chunk
                    job.g[p : p + chunk, :] = v[j * chunk : (j + 1) * chunk, job.at : job.at + job.width]
    else:
        for job in mine:
            v = product(slice(None), slice(job.at, job.at + job.width))
            job.g[...] = group_rows(v, job.order).astype(BF)
    for job in mine:
        job.start(0)


OUTS = ("o_act", "o_dx", "o_cond", "o_ada", "o_conv", "o_proj", "o_out", "o_up", "o_down")
INS = ("patches", "condition", "count", "cotangent", "w_ada", "w_conv", "w_proj", "w_out", "w_up", "w_down")


def kernel(names, *refs):
    s = Refs(names, refs)
    section, place = lax.axis_index("section"), lax.axis_index("dp")
    stride = lax.axis_size("dp") // GROUP
    me, low = lax.div(place, stride), lax.rem(place, stride)
    first, second = section == 0, section == 1

    def spread(member):
        return member * stride + low

    partner = (1 - section, place)
    micro, length, features = s.inflow.shape
    s.result, s.dx = s.o_act.at[0, :, 0], s.o_dx.at[0, :, 0]
    s.fin_ada, s.fin_conv, s.fin_cond = s.o_ada.at[0], s.o_conv, s.o_cond
    s.fin_proj, s.fin_out, s.fin_up, s.fin_down = (o.at[0] for o in (s.o_proj, s.o_out, s.o_up, s.o_down))

    loads = {
        "ada": (s.w_ada.at[0], s.ada),
        "cond": (s.condition, s.cond),
        "wc": (s.w_conv.at[0], s.wc),
        "wp": (s.w_proj.at[0], s.wp),
        "wo": (s.w_out.at[0], s.wo),
        "wu": (s.w_up.at[0], s.wu),
        "wd": (s.w_down.at[0], s.wd),
    }
    order = list(loads)

    def load(name):
        return pltpu.make_async_copy(*loads[name], s.load_sem.at[order.index(name)])

    def load_patches():
        return pltpu.make_async_copy(s.patches.at[:, 0], s.inflow, s.load_sem.at[len(order)])

    def load_cotangent():
        return pltpu.make_async_copy(s.cotangent.at[:, 0], s.ups, s.load_sem.at[len(order)])

    load("cond").start()
    load("ada").start()
    pl.when(first)(lambda: load_patches().start())
    for name in order[2:4]:
        load(name).start()

    barrier = pltpu.get_barrier_semaphore()

    def greet(j, c):
        other = lax.rem(me + j, GROUP)
        pl.semaphore_signal(barrier, 1, device_id=(section, spread(other)), device_id_type=MESH)
        return c

    lax.fori_loop(1, GROUP, greet, 0)
    pl.semaphore_signal(barrier, 1, device_id=partner, device_id_type=MESH)

    zero = jnp.zeros((8, features), F32)
    for i in range(micro):
        s.mixed[i, 0:8, :] = zero
        s.mixed[i, length + 8 :, :] = zero
    s.dcv[0:8, :] = zero
    s.dcv[length + 8 :, :] = zero
    s.dwc[...] = zero

    load("cond").wait()
    conds = [s.cond[i : i + 1, :].astype(F32) for i in range(micro)]
    silus = [(v * sigmoid(v)).astype(BF).astype(F32) for v in conds]
    row = lax.broadcasted_iota(jnp.int32, (16, features), 0)
    act_rows = jnp.where(
        row < 6,
        jnp.broadcast_to(silus[0], (16, features)),
        jnp.where(row < 12, jnp.broadcast_to(silus[1], (16, features)), 0.0),
    ).astype(BF)
    s.own_act[...] = act_rows
    s.all_act[lax.rem(me, 2), lax.div(me, 2)] = act_rows
    load("ada").wait()
    for name in order[4:]:
        load(name).start()
    pl.when(second)(lambda: load_cotangent().start())
    for k in range(6):
        m = mm(act_rows, s.ada[:, k * features : (k + 1) * features])
        for i in range(micro):
            s.mod[i, k : k + 1, :] = m[6 * i : 6 * i + 1, :]

    def hop(source, target, i, h):
        at = half_rows(h, length)
        return pltpu.make_async_remote_copy(
            src_ref=source.at[i, at],
            dst_ref=target.at[i, at],
            send_sem=s.hop_send.at[i, h],
            recv_sem=s.hop_recv.at[i, h],
            device_id=partner,
            device_id_type=MESH,
        )

    def result_copy(i, h):
        return hop(s.result, s.inflow, i, h)

    def dx_copy(i, h):
        return hop(s.dx, s.ups, i, h)

    core, chip = lax.rem(me, 2), lax.div(me, 2)
    chips = GROUP // 2
    beside = (section, spread(me + 1 - 2 * core))

    def gather_copy(j, src, dst, send, recv, received=False):
        other = lax.rem(chip + j, chips)
        slot = other if received else chip
        return pltpu.make_async_remote_copy(
            src_ref=src,
            dst_ref=dst.at[core, slot],
            send_sem=send.at[j],
            recv_sem=recv.at[slot],
            device_id=(section, spread(2 * other + core)),
            device_id_type=MESH,
        )

    def share_copy(src, dst, send, recv, received=False):
        half = dst.at[1 - core if received else core]
        return pltpu.make_async_remote_copy(
            src_ref=half,
            dst_ref=half,
            send_sem=send.at[0],
            recv_sem=recv.at[chips],
            device_id=beside,
            device_id_type=MESH,
        )

    acts = (s.own_act, s.all_act, s.act_send, s.act_recv)
    mods = (s.own_mod, s.all_mod, s.mod_send, s.mod_recv)

    def each_chip(fn):
        def one(j, c):
            fn(j)
            return c

        lax.fori_loop(1, chips, one, 0)

    def share(what):
        each_chip(lambda j: gather_copy(j, *what, received=True).wait_recv())
        share_copy(*what).start()

    jobs = {name: Halving(s, name, section, spread, me) for name in PIECES}

    def take(words, begun=False):
        for word in words:
            if word.startswith("W"):
                weight_gradient(s, word[1], jobs, begun)
            else:
                jobs[word[:2]].step(int(word[2]))

    def loaded(name):
        if name:
            load(name).wait()

    @pl.when(first)
    def _():
        load_patches().wait()
        for i in range(micro):

            def depart(h, i=i):
                if i == 0 and h == 1:
                    pl.semaphore_wait(barrier, GROUP)
                result_copy(i, h).start()

            forward(s, i, False, s.count[i], nothing if i else loaded, depart=depart)
        each_chip(lambda j: gather_copy(j, *acts).start())
        turn_operands(s)
        for i in range(micro):
            ending = i == micro - 1
            if ending:
                first_products(s)
            backward(
                s,
                i,
                False,
                s.count[i],
                (lambda name: take(TURNS[name], True) if name in TURNS else None) if ending else nothing,
                arrive=lambda h, i=i: dx_copy(i, h).wait_recv(),
            )

    @pl.when(second)
    def _():
        pl.semaphore_wait(barrier, GROUP)
        each_chip(lambda j: gather_copy(j, *acts).start())
        for i in range(micro):
            forward(
                s, i, True, s.count[i], nothing if i else loaded, arrive=lambda h, i=i: result_copy(i, h).wait_recv()
            )
            if i == 0:
                load_cotangent().wait()
            if i == micro - 1:
                backward(s, i, True, s.count[i], depart=lambda h, i=i: dx_copy(i, h).start())
            else:
                backward(s, i, True, s.count[i])
                for h in range(2):
                    dx_copy(i, h).start()
        turn_operands(s)
        for name in TURNS:
            if name != "tail":
                take(TURNS[name])

    def gather_rows():
        for i in range(micro):
            for k in range(6):
                s.stage[6 * i + k : 6 * i + k + 1, :] = s.dmod[i, k : k + 1, :]
        s.stage[12 : 12 + TAPS, :] = s.dwc[0:TAPS, :]
        s.stage[15:16, :] = jnp.zeros((1, features), F32)
        own = s.stage[...].astype(BF)
        s.own_mod[...] = own
        s.all_mod[core, chip] = own
        each_chip(lambda j: gather_copy(j, *mods).start())
        share(acts)

    cond_copy = pltpu.make_async_remote_copy(
        src_ref=s.own_cond,
        dst_ref=s.got_cond,
        send_sem=s.cond_sem.at[0],
        recv_sem=s.cond_sem.at[1],
        device_id=partner,
        device_id_type=MESH,
    )

    def condition_gradient():
        tot = jnp.zeros((16, features), F32)
        for k in range(6):
            part = nt(s.own_mod[...], s.ada[:, k * features : (k + 1) * features])
            tot = tot + jnp.where(jnp.logical_or(row == k, row == 6 + k), part, 0.0)
        for i in range(micro):
            sg = sigmoid(conds[i])
            slope = sg + conds[i] * sg * (1.0 - sg)
            s.own_cond[i, :, :] = jnp.sum(tot[6 * i : 6 * i + 6], 0, keepdims=True) * slope
        cond_copy.start()

    def image_sums():
        share_copy(*acts, received=True).wait_recv()
        share_copy(*mods, received=True).wait_recv()
        chunk = features // GROUP
        n_rows = GROUP * 16
        flat_act = s.all_act[...].reshape(n_rows, features)
        flat_mod = s.all_mod[...].reshape(n_rows, features)
        pick = (
            lax.broadcasted_iota(jnp.int32, (chunk, features), 1)
            == me * chunk + lax.broadcasted_iota(jnp.int32, (chunk, features), 0)
        ).astype(F32).astype(BF)
        left = nt(pick, flat_act)
        lane = lax.rem(lax.broadcasted_iota(jnp.int32, (chunk, n_rows), 1), 16)
        for k in range(6):
            mine = jnp.logical_or(lane == k, lane == 6 + k)
            s.fin_ada[:, k * features : (k + 1) * features] = mm(
                jnp.where(mine, left, 0.0).astype(BF), flat_mod
            )
        picked = nt(flat_mod, pick).astype(BF)
        tap = lax.broadcasted_iota(jnp.int32, (8, n_rows), 0)
        at_tap = lax.rem(lax.broadcasted_iota(jnp.int32, (8, n_rows), 1), 16) == 12 + tap
        sums = mm(jnp.where(jnp.logical_and(at_tap, tap < TAPS), 1.0, 0.0).astype(BF), picked)
        for j in range(TAPS):
            s.fin_conv[j, :, :] = sums[j : j + 1, :]
        cond_copy.wait()
        s.fin_cond[...] = s.own_cond[...] + s.got_cond[...]

    ends = {"SHARE": lambda: share(mods), "GATHER": gather_rows, "COND": condition_gradient, "ADA": image_sums}
    for word in TURNS["tail"]:
        if word in ends:
            ends[word]()
        else:
            take((word,))

    for i in range(micro):
        for h in range(2):
            pl.when(first)(lambda i=i, h=h: result_copy(i, h).wait_send())
            pl.when(second)(lambda i=i, h=h: dx_copy(i, h).wait_send())
    for job in jobs.values():
        job.end()
    for what in (acts, mods):
        each_chip(lambda j, what=what: gather_copy(j, *what).wait_send())
        share_copy(*what).wait_send()


def finish(n, *refs):
    held, given, sems = refs[:n], refs[n : 2 * n], refs[2 * n]
    outward = [pltpu.make_async_copy(a, b, sems.at[k]) for k, (a, b) in enumerate(zip(held, given))]
    for o in outward:
        o.start()
    for o in outward:
        o.wait()


def body(patches, condition, valid_count, cotangent, ada_weight, conv_weight, proj_weight, out_weight, up_weight, down_weight):
    micro, images, length, features = patches.shape
    hidden = up_weight.shape[2]
    heads = features // HD
    tokens = micro * length
    chunk, deep = features // GROUP, hidden // GROUP
    arrays = dict(
        ada=((features, 6 * features), BF),
        cond=((micro, features), BF),
        wc=((TAPS, features), BF),
        wp=((features, 4 * features), BF),
        wo=((features, features), BF),
        wu=((features, hidden), BF),
        wd=((hidden, features), BF),
        inflow=((micro, length, features), BF),
        ups=((micro, length, features), BF),
        mod=((micro, 8, features), F32),
        dmod=((micro, 8, features), F32),
        dwc=((8, features), F32),
        n1=((micro, length, features), F32),
        r1=((micro, length, 128), F32),
        mixed=((micro, length + 16, features), F32),
        conv=((tokens, features), BF),
        qkv=((micro, length, 3 * features), BF),
        sw=((micro, heads, length, length), BF),
        an=((micro, length, features), F32),
        ra=((micro, length, 128), F32),
        act=((micro, length, features), F32),
        dact=((micro, length, features), F32),
        gated=((tokens, features), BF),
        branch=((micro, length, features), F32),
        hid=((length, features), F32),
        wide_a=((length, features), F32),
        n2=((micro, length, features), F32),
        r2=((micro, length, 128), F32),
        m2=((tokens, features), BF),
        ffn=((micro, length, features), F32),
        ha=((tokens, hidden), BF),
        ha_t=((hidden, tokens), BF),
        m2_t=((features, tokens), BF),
        gated_t=((features, tokens), BF),
        conv_t=((features, tokens), BF),
        part_d=((hidden, features), F32),
        part_u=((features, hidden), F32),
        part_o=((features, features), F32),
        part_p=((features, 4 * features), F32),
        dgelu=((micro, length, hidden), F32),
        dffn=((tokens, features), BF),
        dpre=((tokens, hidden), BF),
        dbr=((tokens, features), BF),
        datt=((length, features), BF),
        dproj=((tokens, 4 * features), BF),
        dcv=((length + 16, features), F32),
        own_act=((16, features), BF),
        all_act=((2, GROUP // 2, 16, features), BF),
        own_mod=((16, features), BF),
        all_mod=((2, GROUP // 2, 16, features), BF),
        stage=((16, features), F32),
        own_cond=((micro, 1, features), F32),
        got_cond=((micro, 1, features), F32),
    )
    tall = dict(down=hidden, up=features, out=features, proj=features)
    for name, (whole, at, width, order) in PIECES.items():
        arrays["g_" + name] = ((tall[whole], width), BF)
        for k in range(4):
            arrays[f"got{k}_{name}"] = ((tall[whole] >> (k + 1), width), BF)
        arrays["sent_" + name] = ((tall[whole] // GROUP, width), BF)
    sems = dict(
        load_sem=(8,),
        hop_send=(2, 2),
        hop_recv=(2, 2),
        rs_send=(len(PIECES), 4),
        rs_recv=(len(PIECES), 4),
        act_send=(GROUP,),
        act_recv=(GROUP,),
        mod_send=(GROUP,),
        mod_recv=(GROUP,),
        cond_sem=(2,),
    )
    names = (*INS, *OUTS, *arrays, *sems)
    any_spec = pl.BlockSpec(memory_space=pl.ANY)
    out_shape = (
        ((1, micro, 1, length, features), BF),
        ((1, micro, 1, length, features), BF),
        ((micro, 1, features), F32),
        ((1, chunk, 6 * features), F32),
        ((TAPS, 1, chunk), F32),
        ((1, chunk, 4 * features), F32),
        ((1, chunk, features), F32),
        ((1, chunk, hidden), F32),
        ((1, deep, features), F32),
    )
    outs = pl.pallas_call(
        lambda *refs: kernel(names, *refs),
        out_shape=[pltpu.VMEM(*o) for o in out_shape],
        in_specs=[pl.BlockSpec(memory_space=pltpu.SMEM if n == "count" else pltpu.HBM) for n in INS],
        out_specs=[pl.BlockSpec(memory_space=pltpu.VMEM)] * len(OUTS),
        scratch_shapes=[pltpu.VMEM(*a) for a in arrays.values()]
        + [pltpu.SemaphoreType.DMA(n) for n in sems.values()],
        compiler_params=pltpu.CompilerParams(
            collective_id=0, has_side_effects=True, vmem_limit_bytes=60000 * 1024
        ),
        name="relay",
    )(
        patches,
        condition.reshape(micro, features),
        valid_count.reshape(micro),
        cotangent, ada_weight, conv_weight, proj_weight, out_weight, up_weight, down_weight)
    outs = pl.pallas_call(
        lambda *refs: finish(len(out_shape), *refs),
        out_shape=[jax.ShapeDtypeStruct(*o) for o in out_shape],
        in_specs=[pl.BlockSpec(memory_space=pltpu.VMEM)] * len(out_shape),
        out_specs=[pl.BlockSpec(memory_space=pltpu.HBM)] * len(out_shape),
        scratch_shapes=[pltpu.SemaphoreType.DMA((len(out_shape),))],
        compiler_params=pltpu.CompilerParams(vmem_limit_bytes=2000 * 1024),
        name="finish",
    )(*outs)
    outs = list(outs)
    outs[4] = outs[4].reshape(1, TAPS, chunk)
    stride = lax.axis_size("dp") // GROUP
    if stride > 1:
        teams = [[t * stride + j for j in range(stride)] for t in range(GROUP)]
        outs = [
            lax.psum_scatter(o, "dp", scatter_dimension=2 if n == 4 else 1, axis_index_groups=teams, tiled=True)
            if n >= 3
            else o
            for n, o in enumerate(outs)
        ]
    return tuple(outs)


def solution(mesh):
    by_section = P("section", None, None)
    placed = (
        P(None, "dp", None, None),
        P(None, "dp", None),
        P(None, "dp"),
        P(None, "dp", None, None),
        *(by_section,) * 6,
    )
    rows_out = P("section", "dp", None)
    return jax.shard_map(
        body,
        mesh=mesh,
        in_specs=placed,
        out_specs=(
            P("section", None, "dp", None, None),
            P("section", None, "dp", None, None),
            P(None, "dp", None),
            rows_out,
            P("section", None, "dp"),
            rows_out,
            rows_out,
            rows_out,
            rows_out,
        ),
        check_vma=False,
    )
```

```python
import jax
import jax.numpy as jnp
from jax import lax
from jax.experimental import pallas as pl
from jax.experimental.pallas import tpu as pltpu
from jax.sharding import PartitionSpec as P

F32, BF = jnp.float32, jnp.bfloat16
HD = 64
TAPS = 3
GROUP = 16
R = 64
MESH = pl.DeviceIdType.MESH
SCALE = HD**-0.5


def mm(a, b):
    return jnp.dot(a, b, preferred_element_type=F32)


def nt(a, b):
    return lax.dot_general(a, b, (((1,), (1,)), ((), ())), preferred_element_type=F32)


def tn(a, b):
    return lax.dot_general(a, b, (((0,), (0,)), ((), ())), preferred_element_type=F32)


def fold(v):
    return jnp.sum(v.reshape(v.shape[0] // 8, 8, v.shape[1]), 0)


def wide(col):
    return jnp.broadcast_to(col, (col.shape[0], 128))


def sigmoid(v):
    return 1.0 / (1.0 + jnp.exp(-v))


def stats(v):
    c = v - jnp.mean(v, -1, keepdims=True)
    s = lax.rsqrt(jnp.mean(c * c, -1, keepdims=True) + 1e-6)
    return c * s, s


def norm_back(g, n, s):
    return s * (g - jnp.mean(g, -1, keepdims=True) - n * jnp.mean(g * n, -1, keepdims=True))


def rows(r, extra=0):
    return pl.ds(r * R, R + extra)


def steps(n, body, init=0):
    for r in range(n):
        init = body(r, init)
    return init


def loop(n, body, init=0):
    return lax.fori_loop(0, n, body, init)


def token_rows(i, length, r=None):
    at, size, unit = (i * length, length, length) if r is None else (i * length + r * R, R, R)
    return pl.ds(at if isinstance(i, int) else pl.multiple_of(at, unit), size)


class Refs:
    def __init__(self, names, refs):
        self.__dict__.update(zip(names, refs, strict=True))


def triangle(second, length):
    sign = (-1 if second else 1) if isinstance(second, bool) else jnp.where(second, -1, 1)
    query = lax.broadcasted_iota(jnp.int32, (length, length), 0)
    key = lax.broadcasted_iota(jnp.int32, (length, length), 1)
    return (query - key) * sign >= 0


def shifted(buf, j, second):
    if isinstance(second, bool):
        return buf[8 + j : 8 + j + R] if second else buf[8 - j : 8 - j + R]
    return jnp.where(second, buf[8 + j : 8 + j + R], buf[8 - j : 8 - j + R])


def input_norm(s, i, r):
    n, sc = stats(s.inflow[i, rows(r), :].astype(F32))
    s.n1[i, rows(r), :] = n
    s.r1[i, rows(r), :] = wide(sc)
    return n


def nothing(*_):
    return None


def half_rows(h, length):
    return pl.ds(h * (length // 2), length // 2)


def forward(s, i, second, count, loaded, arrive=nothing, depart=nothing, normed=False):
    length, features = s.inflow.shape[1:]
    hidden = s.wu.shape[1]
    mod = s.mod.at[i]
    tok = token_rows(i, length)

    def trow(r):
        return token_rows(i, length, r)

    def place(r):
        return r * R + lax.broadcasted_iota(jnp.int32, (R, 1), 0)

    def first_norm(r, c):
        n = s.n1[i, rows(r), :] if normed else input_norm(s, i, r)
        m = jnp.where(place(r) < count, n * (1.0 + mod[1:2, :]) + mod[0:1, :], 0.0)
        s.mixed[i, pl.ds(r * R + 8, R), :] = m
        return c

    def conv(r, c):
        buf = s.mixed[i, rows(r, 16), :]
        v = s.wc[0:1, :].astype(F32) * buf[8 : 8 + R]
        for j in range(1, TAPS):
            v = v + s.wc[j : j + 1, :].astype(F32) * shifted(buf, j, second)
        s.conv[trow(r), :] = jnp.where(place(r) < count, v, 0.0).astype(BF)
        return c

    def project(own, out):
        cv = s.conv[own, :]
        for c in range(3):
            p = mm(cv, s.wp[:, c * features : (c + 1) * features])
            s.qkv[i, out, c * features : (c + 1) * features] = (p * SCALE if c == 0 else p).astype(BF)
        s.wide_a[out, :] = mm(cv, s.wp[:, 3 * features :])

    per = length // R // 2
    if second:
        for h in (1, 0):
            arrive(h)
            for r in reversed(range(h * per, (h + 1) * per)):
                first_norm(r, 0)
            loaded("wc" if h else "")
            for r in range(h * per, (h + 1) * per):
                conv(r, 0)
            loaded("wp" if h else "")
            project(pl.ds(i * length + h * (length // 2), length // 2), half_rows(h, length))
    else:
        steps(length // R, first_norm)
        loaded("wc")
        steps(length // R, conv)
        loaded("wp")
        project(tok, slice(None))
    keep = triangle(second, length)
    lane = lax.broadcasted_iota(jnp.int32, (length, 2 * HD), 1) < HD

    def pair(p, c):
        def at(k):
            return pl.ds(k * features + p * 2 * HD, 2 * HD)

        q, k, v = (s.qkv[i, :, at(n)] for n in range(3))
        z = jnp.zeros_like(q)
        tot = None
        for h in range(2):
            mine = lane if h == 0 else jnp.logical_not(lane)
            sw = jnp.where(keep, nt(jnp.where(mine, q, z), k), 0.0).astype(BF)
            s.sw[i, 2 * p + h] = sw
            part = mm(sw, jnp.where(mine, v, z))
            tot = part if tot is None else tot + part
        s.an[i, :, at(0)] = tot
        return c

    steps(features // (2 * HD), pair)

    def gate(r, c):
        a = s.an[i, rows(r), :]
        sc = lax.rsqrt(jnp.mean(a * a, -1, keepdims=True) + 1e-6)
        an = a * sc
        g = s.wide_a[rows(r), :]
        sg = sigmoid(g)
        act = g * sg
        s.an[i, rows(r), :] = an
        s.ra[i, rows(r), :] = wide(sc)
        s.act[i, rows(r), :] = act
        s.dact[i, rows(r), :] = sg + act * (1.0 - sg)
        s.gated[trow(r), :] = (an * act).astype(BF)
        return c

    steps(length // R, gate)
    loaded("wo")
    s.branch[i] = mm(s.gated[tok, :], s.wo[...])

    def second_norm(r, c):
        v = s.inflow[i, rows(r), :].astype(F32) + mod[2:3, :] * s.branch[i, rows(r), :]
        n, sc = stats(v)
        s.hid[rows(r), :] = v
        s.n2[i, rows(r), :] = n
        s.r2[i, rows(r), :] = wide(sc)
        s.m2[trow(r), :] = (n * (1.0 + mod[4:5, :]) + mod[3:4, :]).astype(BF)
        return c

    steps(length // R, second_norm)
    loaded("wu")
    loaded("wd")
    width = 256

    def feed(own, out):
        for c in range(hidden // width):
            at = pl.ds(c * width, width)
            h = mm(s.m2[own, :], s.wu[:, at])
            k0, k1 = 0.7978845608028654, 0.044715
            hh = h * h
            t = jnp.tanh(h * (k0 + (k0 * k1) * hh))
            half = 0.5 * (1.0 + t)
            s.ha[own, at] = (h * half).astype(BF)
            s.dgelu[i, out, at] = half + (0.5 * h) * (1.0 - t * t) * (k0 + (3 * k0 * k1) * hh)
        s.ffn[i, out, :] = mm(s.ha[own, :], s.wd[...])

    def last(r):
        s.result[i, rows(r), :] = (s.hid[rows(r), :] + mod[5:6, :] * s.ffn[i, rows(r), :]).astype(BF)

    if second:
        feed(tok, slice(None))
        for r in range(2 * per):
            last(r)
    else:
        for h in (1, 0):
            feed(pl.ds(i * length + h * (length // 2), length // 2), half_rows(h, length))
            for r in range(h * per, (h + 1) * per):
                last(r)
            depart(h)


def backward(s, i, second, count, hook=nothing, arrive=nothing, depart=None):
    length, features = s.inflow.shape[1:]
    hidden = s.wu.shape[1]
    mod, dmod, up = s.mod.at[i], s.dmod.at[i], s.ups.at[i]
    tok = token_rows(i, length)

    def trow(r):
        return token_rows(i, length, r)

    def place(r):
        return r * R + lax.broadcasted_iota(jnp.int32, (R, 1), 0)

    zero = jnp.zeros((8, features), F32)

    def start(r, acc):
        u = up[rows(r), :].astype(F32)
        s.dffn[trow(r), :] = (mod[5:6, :] * u).astype(BF)
        return acc + fold(u * s.ffn[i, rows(r), :])

    width = 256
    per = length // R // 2

    def feed(own, out):
        for c in range(hidden // width):
            at = pl.ds(c * width, width)
            d = nt(s.dffn[own, :], s.wd[at, :])
            s.dpre[own, at] = (d * s.dgelu[i, out, at]).astype(BF)
        s.wide_a[out, :] = nt(s.dpre[own, :], s.wu[...])

    acc = zero
    for h in range(2):
        arrive(h)
        for r in range(h * per, (h + 1) * per):
            acc = start(r, acc)
    hook("down")
    feed(tok, slice(None))
    dmod[5:6, :] = jnp.sum(acc, 0, keepdims=True)
    hook("up")

    def mid(r, acc):
        dm = s.wide_a[rows(r), :]
        n = s.n2[i, rows(r), :]
        dh = up[rows(r), :].astype(F32) + norm_back(
            dm * (1.0 + mod[4:5, :]), n, s.r2[i, rows(r), :][:, :1]
        )
        s.hid[rows(r), :] = dh
        s.dbr[trow(r), :] = (mod[2:3, :] * dh).astype(BF)
        new = (fold(dm), fold(dm * n), fold(dh * s.branch[i, rows(r), :]))
        return tuple(a + b for a, b in zip(acc, new))

    acc = steps(length // R, mid, (zero,) * 3)
    for k, a in zip((3, 4, 2), acc):
        dmod[k : k + 1, :] = jnp.sum(a, 0, keepdims=True)
    hook("out")
    s.wide_a[...] = nt(s.dbr[tok, :], s.wo[...])

    def gate(r, c):
        dg = s.wide_a[rows(r), :]
        an = s.an[i, rows(r), :]
        dn = dg * s.act[i, rows(r), :]
        s.dproj[trow(r), 3 * features :] = (dg * an * s.dact[i, rows(r), :]).astype(BF)
        da = s.ra[i, rows(r), :][:, :1] * (dn - an * jnp.mean(dn * an, -1, keepdims=True))
        s.datt[rows(r), :] = da.astype(BF)
        return c

    steps(length // R, gate)
    hook("attend")
    keep = triangle(second, length)
    lane = lax.broadcasted_iota(jnp.int32, (length, 2 * HD), 1) < HD

    def pair(p, c):
        def at(k):
            return pl.ds(k * features + p * 2 * HD, 2 * HD)

        q, k, v = (s.qkv[i, :, at(n)] for n in range(3))
        g = s.datt[:, at(0)]
        z = jnp.zeros_like(q)
        dq = dk = dv = None
        for h in range(2):
            mine = lane if h == 0 else jnp.logical_not(lane)
            gm = jnp.where(mine, g, z)
            ds = jnp.where(keep, nt(gm, v), 0.0).astype(BF)
            a = mm(ds, jnp.where(mine, k, z))
            b = tn(ds, jnp.where(mine, q, z))
            e = tn(s.sw[i, 2 * p + h], gm)
            dq = a if dq is None else dq + a
            dk = b if dk is None else dk + b
            dv = e if dv is None else dv + e
        s.dproj[tok, at(0)] = (dq * SCALE).astype(BF)
        s.dproj[tok, at(1)] = dk.astype(BF)
        s.dproj[tok, at(2)] = dv.astype(BF)
        hook(f"pair{p}")
        return c

    steps(features // (2 * HD), pair)
    def mask_rows(r):
        at = pl.ds(r * R + 8, R)
        s.dcv[at, :] = jnp.where(place(r) < count, s.dcv[at, :], 0.0)

    def conv(r, acc):
        dbuf = s.dcv[rows(r, 16), :]
        mbuf = s.mixed[i, rows(r, 16), :]
        here = dbuf[8 : 8 + R]
        d = s.wc[0:1, :].astype(F32) * here
        taps = [fold(here * mbuf[8 : 8 + R])]
        for j in range(1, TAPS):
            d = d + s.wc[j : j + 1, :].astype(F32) * shifted(dbuf, j, (not second) if isinstance(second, bool) else jnp.logical_not(second))
            taps.append(fold(here * shifted(mbuf, j, second)))
        d = jnp.where(place(r) < count, d, 0.0)
        n = s.n1[i, rows(r), :]
        res = s.hid[rows(r), :] + norm_back(d * (1.0 + mod[1:2, :]), n, s.r1[i, rows(r), :][:, :1])
        s.dx[i, rows(r), :] = res.astype(BF)
        return tuple(a + b for a, b in zip(acc, (fold(d), fold(d * n), *taps)))

    acc = (zero,) * (2 + TAPS)
    if depart:
        for h in (0, 1):
            own = pl.ds(i * length + h * (length // 2), length // 2)
            s.dcv[h * (length // 2) + 8 : (h + 1) * (length // 2) + 8, :] = nt(s.dproj[own, :], s.wp[...])
            for r in range(h * per, (h + 1) * per):
                mask_rows(r)
            for r in range(h * per, (h + 1) * per):
                acc = conv(r, acc)
            depart(h)
    else:
        s.dcv[8 : length + 8, :] = nt(s.dproj[tok, :], s.wp[...])
        hook("conv")
        for r in range(2 * per):
            mask_rows(r)
        acc = steps(length // R, conv, acc)
    for k in range(2):
        dmod[k : k + 1, :] = jnp.sum(acc[k], 0, keepdims=True)
    for j in range(TAPS):
        s.dwc[j : j + 1, :] += jnp.sum(acc[2 + j], 0, keepdims=True)


ACROSS, ALONG, BETWEEN = (0, 1, 2, 3), (0, 2, 3, 1), (0, 2, 1, 3)
PIECES = {
    "d0": ("down", 0, 128, ACROSS),
    "d1": ("down", 128, 128, BETWEEN),
    "d2": ("down", 256, 128, BETWEEN),
    "u0": ("up", 0, 384, ACROSS),
    "u1": ("up", 384, 256, BETWEEN),
    "u2": ("up", 640, 640, ACROSS),
    "u3": ("up", 1280, 256, ACROSS),
    "o0": ("out", 0, 384, ACROSS),
    "p0": ("proj", 0, 384, ACROSS),
    "p1": ("proj", 384, 384, ACROSS),
    "p2": ("proj", 768, 256, BETWEEN),
    "p3": ("proj", 1024, 384, ACROSS),
    "p4": ("proj", 1408, 128, ACROSS),
}
TURNS = {
    "down": ("Wd",),
    "up": ("d00", "Wu", "d10", "d20"),
    "out": ("Wo",),
    "attend": ("u00", "u10"),
    "pair0": ("u20", "u30", "o00"),
    "pair1": ("d01",),
    "pair2": ("Wp", "d11"),
    "conv": ("u01",),
    "tail": ("p00", "p10", "GATHER", "p20", "p30", "d21", "p40", "COND", "u11", "u21", "d02", "u31", "u02", "o01", "d12", "p21", "p01", "u22", "d03", "u32", "p11", "u03", "o02", "d13", "SHARE", "p02", "p31", "u23", "ADA", "d22", "p41", "u33", "p12", "u12", "p22", "o03", "p03", "p32", "p42", "d23", "p13", "u13", "p23", "p33", "p43"),
}


def spot(chunk, order):
    p = 0
    for bit in order:
        p = 2 * p + ((chunk >> bit) & 1)
    return p


class Halving:
    def __init__(self, s, name, section, spread, me):
        self.whole, self.at, self.width, self.order = PIECES[name]
        self.g = getattr(s, "g_" + name)
        self.got = [getattr(s, f"got{k}_" + name) for k in range(4)]
        self.sent = getattr(s, "sent_" + name)
        self.fin = getattr(s, "fin_" + self.whole).at[:, pl.ds(self.at, self.width)]
        index = list(PIECES).index(name)
        self.send_sem = [s.rs_send.at[index, k] for k in range(4)]
        self.recv_sem = [s.rs_recv.at[index, k] for k in range(4)]
        height = self.g.shape[0]
        low = 0
        self.keep, self.give, self.peer = [], [], []
        self.bit = [lax.rem(lax.div(me, 1 << b), 2) for b in self.order]
        for k, b in enumerate(self.order):
            half = height >> (k + 1)
            step = half if half % 16 == 0 else 8
            self.keep.append(pl.multiple_of(low + self.bit[k] * half, step))
            self.give.append(pl.multiple_of(low + (1 - self.bit[k]) * half, step))
            low = self.keep[-1]
            other = me + (1 - 2 * self.bit[k]) * (1 << b)
            self.peer.append((section, spread(other)))

    def copy(self, k):
        half = self.g.shape[0] >> (k + 1)
        src = self.sent if k == 3 else self.g.at[pl.ds(self.give[k], half)]
        return pltpu.make_async_remote_copy(
            src_ref=src,
            dst_ref=self.got[k],
            send_sem=self.send_sem[k],
            recv_sem=self.recv_sem[k],
            device_id=self.peer[k],
            device_id_type=MESH,
        )

    def start(self, k):
        self.copy(k).start()

    def step(self, k):
        self.copy(k).wait_recv()
        got = self.got[k]
        if k < 2:
            at = pl.ds(self.keep[k], got.shape[0])
            self.g[at, :] = (self.g[at, :].astype(F32) + got[...].astype(F32)).astype(BF)
        elif k == 2:
            part = got.shape[0] // 2
            v = self.g[pl.ds(self.keep[2], 2 * part), :].astype(F32) + got[...].astype(F32)
            upper = self.bit[3] == 1
            self.sent[...] = jnp.where(upper, v[:part], v[part:]).astype(BF)
            self.fin[...] = jnp.where(upper, v[part:], v[:part])
        else:
            self.fin[...] += got[...].astype(F32)
        if k < 3:
            self.start(k + 1)

    def end(self):
        for k in range(4):
            self.copy(k).wait_send()


def group_rows(val, order):
    height = val.shape[0] // GROUP
    at = [0] * GROUP
    for c in range(GROUP):
        at[spot(c, order)] = c
    return jnp.concatenate([val[c * height : (c + 1) * height] for c in at], 0)


def turn_operands(s):
    for left, out in ((s.ha, s.ha_t), (s.m2, s.m2_t), (s.gated, s.gated_t), (s.conv, s.conv_t)):
        width = 384

        def one(c, carry, left=left, out=out):
            at = pl.ds(pl.multiple_of(c * width, width), width)
            out[at, :] = left[:, at].T
            return carry

        loop(left.shape[1] // width, one)


OPERANDS = {"d": ("ha_t", "dffn"), "u": ("m2_t", "dpre"), "o": ("gated_t", "dbr"), "p": ("conv_t", "dproj")}


def first_products(s):
    for letter, (left, right) in OPERANDS.items():
        left, right, out = getattr(s, left), getattr(s, right), getattr(s, "part_" + letter)
        half, width = left.shape[1] // 2, 384
        if left.shape[0] > right.shape[1]:

            def one(c, carry, left=left, right=right, out=out):
                at = pl.ds(pl.multiple_of(c * width, width), width)
                out[at, :] = mm(left[at, :half], right[:half, :])
                return carry

            loop(left.shape[0] // width, one)
        else:

            def one(c, carry, left=left, right=right, out=out):
                at = pl.ds(pl.multiple_of(c * width, width), width)
                out[:, at] = mm(left[:, :half], right[:half, at])
                return carry

            loop(right.shape[1] // width, one)


def weight_gradient(s, letter, jobs, begun):
    mine = [job for name, job in jobs.items() if name[0] == letter]
    left, right = (getattr(s, name) for name in OPERANDS[letter])
    half = left.shape[1] // 2

    def product(at, to):
        if begun:
            return getattr(s, "part_" + letter)[at, to] + mm(left[at, half:], right[half:, to])
        return mm(left[at, :], right[:, to])

    if letter == "d":
        features = right.shape[1]
        chunk = left.shape[0] // GROUP
        per = features // chunk
        for c in range(left.shape[0] // features):
            v = product(slice(c * features, (c + 1) * features), slice(None)).astype(BF)
            for j in range(per):
                for job in mine:
                    p = spot(c * per + j, job.order) * chunk
                    job.g[p : p + chunk, :] = v[j * chunk : (j + 1) * chunk, job.at : job.at + job.width]
    else:
        for job in mine:
            v = product(slice(None), slice(job.at, job.at + job.width))
            job.g[...] = group_rows(v, job.order).astype(BF)
    for job in mine:
        job.start(0)


OUTS = ("o_act", "o_dx", "o_cond", "o_ada", "o_conv", "o_proj", "o_out", "o_up", "o_down")
INS = ("patches", "condition", "count", "cotangent", "w_ada", "w_conv", "w_proj", "w_out", "w_up", "w_down")


def kernel(names, *refs):
    s = Refs(names, refs)
    section, place = lax.axis_index("section"), lax.axis_index("dp")
    stride = lax.axis_size("dp") // GROUP
    me, low = lax.div(place, stride), lax.rem(place, stride)
    first, second = section == 0, section == 1

    def spread(member):
        return member * stride + low

    partner = (1 - section, place)
    micro, length, features = s.inflow.shape
    s.result, s.dx = s.o_act.at[0, :, 0], s.o_dx.at[0, :, 0]
    s.fin_ada, s.fin_conv, s.fin_cond = s.o_ada.at[0], s.o_conv, s.o_cond
    s.fin_proj, s.fin_out, s.fin_up, s.fin_down = (o.at[0] for o in (s.o_proj, s.o_out, s.o_up, s.o_down))

    loads = {
        "ada": (s.w_ada.at[0], s.ada),
        "cond": (s.condition, s.cond),
        "wc": (s.w_conv.at[0], s.wc),
        "wp": (s.w_proj.at[0], s.wp),
        "wo": (s.w_out.at[0], s.wo),
        "wu": (s.w_up.at[0], s.wu),
        "wd": (s.w_down.at[0], s.wd),
    }
    order = list(loads)

    def load(name):
        return pltpu.make_async_copy(*loads[name], s.load_sem.at[order.index(name)])

    def load_patches():
        return pltpu.make_async_copy(s.patches.at[:, 0], s.inflow, s.load_sem.at[len(order)])

    def load_cotangent():
        return pltpu.make_async_copy(s.cotangent.at[:, 0], s.ups, s.load_sem.at[len(order)])

    load("cond").start()
    load("ada").start()
    pl.when(first)(lambda: load_patches().start())
    for name in order[2:4]:
        load(name).start()

    barrier = pltpu.get_barrier_semaphore()

    def greet(j, c):
        other = lax.rem(me + j, GROUP)
        pl.semaphore_signal(barrier, 1, device_id=(section, spread(other)), device_id_type=MESH)
        return c

    lax.fori_loop(1, GROUP, greet, 0)
    pl.semaphore_signal(barrier, 1, device_id=partner, device_id_type=MESH)

    zero = jnp.zeros((8, features), F32)
    for i in range(micro):
        s.mixed[i, 0:8, :] = zero
        s.mixed[i, length + 8 :, :] = zero
    s.dcv[0:8, :] = zero
    s.dcv[length + 8 :, :] = zero
    s.dwc[...] = zero

    load("cond").wait()
    conds = [s.cond[i : i + 1, :].astype(F32) for i in range(micro)]
    silus = [(v * sigmoid(v)).astype(BF).astype(F32) for v in conds]
    row = lax.broadcasted_iota(jnp.int32, (16, features), 0)
    act_rows = jnp.where(
        row < 6,
        jnp.broadcast_to(silus[0], (16, features)),
        jnp.where(row < 12, jnp.broadcast_to(silus[1], (16, features)), 0.0),
    ).astype(BF)
    s.own_act[...] = act_rows
    s.all_act[lax.rem(me, 2), lax.div(me, 2)] = act_rows

    @pl.when(first)
    def _():
        load_patches().wait()
        for i in range(micro):
            for r in range(length // R):
                input_norm(s, i, r)

    load("ada").wait()
    for name in order[4:]:
        load(name).start()
    pl.when(second)(lambda: load_cotangent().start())
    for k in range(6):
        m = mm(act_rows, s.ada[:, k * features : (k + 1) * features])
        for i in range(micro):
            s.mod[i, k : k + 1, :] = m[6 * i : 6 * i + 1, :]

    def hop(source, target, i, h):
        at = half_rows(h, length)
        return pltpu.make_async_remote_copy(
            src_ref=source.at[i, at],
            dst_ref=target.at[i, at],
            send_sem=s.hop_send.at[i, h],
            recv_sem=s.hop_recv.at[i, h],
            device_id=partner,
            device_id_type=MESH,
        )

    def result_copy(i, h):
        return hop(s.result, s.inflow, i, h)

    def dx_copy(i, h):
        return hop(s.dx, s.ups, i, h)

    core, chip = lax.rem(me, 2), lax.div(me, 2)
    chips = GROUP // 2
    beside = (section, spread(me + 1 - 2 * core))

    def gather_copy(j, src, dst, send, recv, received=False):
        other = lax.rem(chip + j, chips)
        slot = other if received else chip
        return pltpu.make_async_remote_copy(
            src_ref=src,
            dst_ref=dst.at[core, slot],
            send_sem=send.at[j],
            recv_sem=recv.at[slot],
            device_id=(section, spread(2 * other + core)),
            device_id_type=MESH,
        )

    def share_copy(src, dst, send, recv, received=False):
        half = dst.at[1 - core if received else core]
        return pltpu.make_async_remote_copy(
            src_ref=half,
            dst_ref=half,
            send_sem=send.at[0],
            recv_sem=recv.at[chips],
            device_id=beside,
            device_id_type=MESH,
        )

    acts = (s.own_act, s.all_act, s.act_send, s.act_recv)
    mods = (s.own_mod, s.all_mod, s.mod_send, s.mod_recv)

    def each_chip(fn):
        def one(j, c):
            fn(j)
            return c

        lax.fori_loop(1, chips, one, 0)

    def share(what):
        each_chip(lambda j: gather_copy(j, *what, received=True).wait_recv())
        share_copy(*what).start()

    jobs = {name: Halving(s, name, section, spread, me) for name in PIECES}

    def take(words, begun=False):
        for word in words:
            if word.startswith("W"):
                weight_gradient(s, word[1], jobs, begun)
            else:
                jobs[word[:2]].step(int(word[2]))

    def loaded(name):
        if name:
            load(name).wait()

    @pl.when(first)
    def _():
        for i in range(micro):

            def depart(h, i=i):
                if i == 0 and h == 1:
                    pl.semaphore_wait(barrier, GROUP)
                result_copy(i, h).start()

            forward(s, i, False, s.count[i], nothing if i else loaded, depart=depart, normed=True)
        each_chip(lambda j: gather_copy(j, *acts).start())
        turn_operands(s)
        for i in range(micro):
            ending = i == micro - 1
            if ending:
                first_products(s)
            backward(
                s,
                i,
                False,
                s.count[i],
                (lambda name: take(TURNS[name], True) if name in TURNS else None) if ending else nothing,
                arrive=lambda h, i=i: dx_copy(i, h).wait_recv(),
            )

    @pl.when(second)
    def _():
        pl.semaphore_wait(barrier, GROUP)
        each_chip(lambda j: gather_copy(j, *acts).start())
        for i in range(micro):
            forward(
                s, i, True, s.count[i], nothing if i else loaded, arrive=lambda h, i=i: result_copy(i, h).wait_recv()
            )
            if i == 0:
                load_cotangent().wait()
            if i == micro - 1:
                backward(s, i, True, s.count[i], depart=lambda h, i=i: dx_copy(i, h).start())
            else:
                backward(s, i, True, s.count[i])
                for h in range(2):
                    dx_copy(i, h).start()
        turn_operands(s)
        for name in TURNS:
            if name != "tail":
                take(TURNS[name])

    def gather_rows():
        for i in range(micro):
            for k in range(6):
                s.stage[6 * i + k : 6 * i + k + 1, :] = s.dmod[i, k : k + 1, :]
        s.stage[12 : 12 + TAPS, :] = s.dwc[0:TAPS, :]
        s.stage[15:16, :] = jnp.zeros((1, features), F32)
        own = s.stage[...].astype(BF)
        s.own_mod[...] = own
        s.all_mod[core, chip] = own
        each_chip(lambda j: gather_copy(j, *mods).start())
        share(acts)

    cond_copy = pltpu.make_async_remote_copy(
        src_ref=s.own_cond,
        dst_ref=s.got_cond,
        send_sem=s.cond_sem.at[0],
        recv_sem=s.cond_sem.at[1],
        device_id=partner,
        device_id_type=MESH,
    )

    def condition_gradient():
        tot = jnp.zeros((16, features), F32)
        for k in range(6):
            part = nt(s.own_mod[...], s.ada[:, k * features : (k + 1) * features])
            tot = tot + jnp.where(jnp.logical_or(row == k, row == 6 + k), part, 0.0)
        for i in range(micro):
            sg = sigmoid(conds[i])
            slope = sg + conds[i] * sg * (1.0 - sg)
            s.own_cond[i, :, :] = jnp.sum(tot[6 * i : 6 * i + 6], 0, keepdims=True) * slope
        cond_copy.start()

    def image_sums():
        share_copy(*acts, received=True).wait_recv()
        share_copy(*mods, received=True).wait_recv()
        chunk = features // GROUP
        n_rows = GROUP * 16
        flat_act = s.all_act[...].reshape(n_rows, features)
        flat_mod = s.all_mod[...].reshape(n_rows, features)
        pick = (
            lax.broadcasted_iota(jnp.int32, (chunk, features), 1)
            == me * chunk + lax.broadcasted_iota(jnp.int32, (chunk, features), 0)
        ).astype(F32).astype(BF)
        left = nt(pick, flat_act)
        lane = lax.rem(lax.broadcasted_iota(jnp.int32, (chunk, n_rows), 1), 16)
        for k in range(6):
            mine = jnp.logical_or(lane == k, lane == 6 + k)
            s.fin_ada[:, k * features : (k + 1) * features] = mm(
                jnp.where(mine, left, 0.0).astype(BF), flat_mod
            )
        picked = nt(flat_mod, pick).astype(BF)
        tap = lax.broadcasted_iota(jnp.int32, (8, n_rows), 0)
        at_tap = lax.rem(lax.broadcasted_iota(jnp.int32, (8, n_rows), 1), 16) == 12 + tap
        sums = mm(jnp.where(jnp.logical_and(at_tap, tap < TAPS), 1.0, 0.0).astype(BF), picked)
        for j in range(TAPS):
            s.fin_conv[j, :, :] = sums[j : j + 1, :]
        cond_copy.wait()
        s.fin_cond[...] = s.own_cond[...] + s.got_cond[...]

    ends = {"SHARE": lambda: share(mods), "GATHER": gather_rows, "COND": condition_gradient, "ADA": image_sums}
    for word in TURNS["tail"]:
        if word in ends:
            ends[word]()
        else:
            take((word,))

    for i in range(micro):
        for h in range(2):
            pl.when(first)(lambda i=i, h=h: result_copy(i, h).wait_send())
            pl.when(second)(lambda i=i, h=h: dx_copy(i, h).wait_send())
    for job in jobs.values():
        job.end()
    for what in (acts, mods):
        each_chip(lambda j, what=what: gather_copy(j, *what).wait_send())
        share_copy(*what).wait_send()


def finish(n, *refs):
    held, given, sems = refs[:n], refs[n : 2 * n], refs[2 * n]
    outward = [pltpu.make_async_copy(a, b, sems.at[k]) for k, (a, b) in enumerate(zip(held, given))]
    for o in outward:
        o.start()
    for o in outward:
        o.wait()


def body(patches, condition, valid_count, cotangent, ada_weight, conv_weight, proj_weight, out_weight, up_weight, down_weight):
    micro, images, length, features = patches.shape
    hidden = up_weight.shape[2]
    heads = features // HD
    tokens = micro * length
    chunk, deep = features // GROUP, hidden // GROUP
    arrays = dict(
        ada=((features, 6 * features), BF),
        cond=((micro, features), BF),
        wc=((TAPS, features), BF),
        wp=((features, 4 * features), BF),
        wo=((features, features), BF),
        wu=((features, hidden), BF),
        wd=((hidden, features), BF),
        inflow=((micro, length, features), BF),
        ups=((micro, length, features), BF),
        mod=((micro, 8, features), F32),
        dmod=((micro, 8, features), F32),
        dwc=((8, features), F32),
        n1=((micro, length, features), F32),
        r1=((micro, length, 128), F32),
        mixed=((micro, length + 16, features), F32),
        conv=((tokens, features), BF),
        qkv=((micro, length, 3 * features), BF),
        sw=((micro, heads, length, length), BF),
        an=((micro, length, features), F32),
        ra=((micro, length, 128), F32),
        act=((micro, length, features), F32),
        dact=((micro, length, features), F32),
        gated=((tokens, features), BF),
        branch=((micro, length, features), F32),
        hid=((length, features), F32),
        wide_a=((length, features), F32),
        n2=((micro, length, features), F32),
        r2=((micro, length, 128), F32),
        m2=((tokens, features), BF),
        ffn=((micro, length, features), F32),
        ha=((tokens, hidden), BF),
        ha_t=((hidden, tokens), BF),
        m2_t=((features, tokens), BF),
        gated_t=((features, tokens), BF),
        conv_t=((features, tokens), BF),
        part_d=((hidden, features), F32),
        part_u=((features, hidden), F32),
        part_o=((features, features), F32),
        part_p=((features, 4 * features), F32),
        dgelu=((micro, length, hidden), F32),
        dffn=((tokens, features), BF),
        dpre=((tokens, hidden), BF),
        dbr=((tokens, features), BF),
        datt=((length, features), BF),
        dproj=((tokens, 4 * features), BF),
        dcv=((length + 16, features), F32),
        own_act=((16, features), BF),
        all_act=((2, GROUP // 2, 16, features), BF),
        own_mod=((16, features), BF),
        all_mod=((2, GROUP // 2, 16, features), BF),
        stage=((16, features), F32),
        own_cond=((micro, 1, features), F32),
        got_cond=((micro, 1, features), F32),
    )
    tall = dict(down=hidden, up=features, out=features, proj=features)
    for name, (whole, at, width, order) in PIECES.items():
        arrays["g_" + name] = ((tall[whole], width), BF)
        for k in range(4):
            arrays[f"got{k}_{name}"] = ((tall[whole] >> (k + 1), width), BF)
        arrays["sent_" + name] = ((tall[whole] // GROUP, width), BF)
    sems = dict(
        load_sem=(8,),
        hop_send=(2, 2),
        hop_recv=(2, 2),
        rs_send=(len(PIECES), 4),
        rs_recv=(len(PIECES), 4),
        act_send=(GROUP,),
        act_recv=(GROUP,),
        mod_send=(GROUP,),
        mod_recv=(GROUP,),
        cond_sem=(2,),
    )
    names = (*INS, *OUTS, *arrays, *sems)
    any_spec = pl.BlockSpec(memory_space=pl.ANY)
    out_shape = (
        ((1, micro, 1, length, features), BF),
        ((1, micro, 1, length, features), BF),
        ((micro, 1, features), F32),
        ((1, chunk, 6 * features), F32),
        ((TAPS, 1, chunk), F32),
        ((1, chunk, 4 * features), F32),
        ((1, chunk, features), F32),
        ((1, chunk, hidden), F32),
        ((1, deep, features), F32),
    )
    outs = pl.pallas_call(
        lambda *refs: kernel(names, *refs),
        out_shape=[pltpu.VMEM(*o) for o in out_shape],
        in_specs=[pl.BlockSpec(memory_space=pltpu.SMEM if n == "count" else pltpu.HBM) for n in INS],
        out_specs=[pl.BlockSpec(memory_space=pltpu.VMEM)] * len(OUTS),
        scratch_shapes=[pltpu.VMEM(*a) for a in arrays.values()]
        + [pltpu.SemaphoreType.DMA(n) for n in sems.values()],
        compiler_params=pltpu.CompilerParams(
            collective_id=0, has_side_effects=True, vmem_limit_bytes=60000 * 1024
        ),
        name="relay",
    )(
        patches,
        condition.reshape(micro, features),
        valid_count.reshape(micro),
        cotangent, ada_weight, conv_weight, proj_weight, out_weight, up_weight, down_weight)
    outs = pl.pallas_call(
        lambda *refs: finish(len(out_shape), *refs),
        out_shape=[jax.ShapeDtypeStruct(*o) for o in out_shape],
        in_specs=[pl.BlockSpec(memory_space=pltpu.VMEM)] * len(out_shape),
        out_specs=[pl.BlockSpec(memory_space=pltpu.HBM)] * len(out_shape),
        scratch_shapes=[pltpu.SemaphoreType.DMA((len(out_shape),))],
        compiler_params=pltpu.CompilerParams(vmem_limit_bytes=2000 * 1024),
        name="finish",
    )(*outs)
    outs = list(outs)
    outs[4] = outs[4].reshape(1, TAPS, chunk)
    stride = lax.axis_size("dp") // GROUP
    if stride > 1:
        teams = [[t * stride + j for j in range(stride)] for t in range(GROUP)]
        outs = [
            lax.psum_scatter(o, "dp", scatter_dimension=2 if n == 4 else 1, axis_index_groups=teams, tiled=True)
            if n >= 3
            else o
            for n, o in enumerate(outs)
        ]
    return tuple(outs)


def solution(mesh):
    by_section = P("section", None, None)
    placed = (
        P(None, "dp", None, None),
        P(None, "dp", None),
        P(None, "dp"),
        P(None, "dp", None, None),
        *(by_section,) * 6,
    )
    rows_out = P("section", "dp", None)
    return jax.shard_map(
        body,
        mesh=mesh,
        in_specs=placed,
        out_specs=(
            P("section", None, "dp", None, None),
            P("section", None, "dp", None, None),
            P(None, "dp", None),
            rows_out,
            P("section", None, "dp"),
            rows_out,
            rows_out,
            rows_out,
            rows_out,
        ),
        check_vma=False,
    )
```

```python
import jax
import jax.numpy as jnp
from jax import lax
from jax.experimental import pallas as pl
from jax.experimental.pallas import tpu as pltpu
from jax.sharding import PartitionSpec as P

F32, BF = jnp.float32, jnp.bfloat16
HD = 64
TAPS = 3
GROUP = 16
R = 64
MESH = pl.DeviceIdType.MESH
SCALE = HD**-0.5


def mm(a, b):
    return jnp.dot(a, b, preferred_element_type=F32)


def nt(a, b):
    return lax.dot_general(a, b, (((1,), (1,)), ((), ())), preferred_element_type=F32)


def tn(a, b):
    return lax.dot_general(a, b, (((0,), (0,)), ((), ())), preferred_element_type=F32)


def fold(v):
    return jnp.sum(v.reshape(v.shape[0] // 8, 8, v.shape[1]), 0)


def wide(col):
    return jnp.broadcast_to(col, (col.shape[0], 128))


def sigmoid(v):
    return 1.0 / (1.0 + jnp.exp(-v))


def stats(v):
    c = v - jnp.mean(v, -1, keepdims=True)
    s = lax.rsqrt(jnp.mean(c * c, -1, keepdims=True) + 1e-6)
    return c * s, s


def norm_back(g, n, s):
    return s * (g - jnp.mean(g, -1, keepdims=True) - n * jnp.mean(g * n, -1, keepdims=True))


def rows(r, extra=0):
    return pl.ds(r * R, R + extra)


def steps(n, body, init=0):
    for r in range(n):
        init = body(r, init)
    return init


def loop(n, body, init=0):
    return lax.fori_loop(0, n, body, init)


def token_rows(i, length, r=None):
    at, size, unit = (i * length, length, length) if r is None else (i * length + r * R, R, R)
    return pl.ds(at if isinstance(i, int) else pl.multiple_of(at, unit), size)


class Refs:
    def __init__(self, names, refs):
        self.__dict__.update(zip(names, refs, strict=True))


def triangle(second, length):
    sign = (-1 if second else 1) if isinstance(second, bool) else jnp.where(second, -1, 1)
    query = lax.broadcasted_iota(jnp.int32, (length, length), 0)
    key = lax.broadcasted_iota(jnp.int32, (length, length), 1)
    return (query - key) * sign >= 0


def shifted(buf, j, second):
    if isinstance(second, bool):
        return buf[8 + j : 8 + j + R] if second else buf[8 - j : 8 - j + R]
    return jnp.where(second, buf[8 + j : 8 + j + R], buf[8 - j : 8 - j + R])


def input_norm(s, i, r):
    n, sc = stats(s.inflow[i, rows(r), :].astype(F32))
    s.n1[i, rows(r), :] = n
    s.r1[i, rows(r), :] = wide(sc)
    return n


def nothing(*_):
    return None


def half_rows(h, length):
    return pl.ds(h * (length // 2), length // 2)


def forward(s, i, second, count, loaded, arrive=nothing, depart=nothing, normed=False):
    length, features = s.inflow.shape[1:]
    hidden = s.wu.shape[1]
    mod = s.mod.at[i]
    tok = token_rows(i, length)

    def trow(r):
        return token_rows(i, length, r)

    def place(r):
        return r * R + lax.broadcasted_iota(jnp.int32, (R, 1), 0)

    def first_norm(r, c):
        n = s.n1[i, rows(r), :] if normed else input_norm(s, i, r)
        m = jnp.where(place(r) < count, n * (1.0 + mod[1:2, :]) + mod[0:1, :], 0.0)
        s.mixed[i, pl.ds(r * R + 8, R), :] = m
        return c

    def conv(r, c):
        buf = s.mixed[i, rows(r, 16), :]
        v = s.wc[0:1, :].astype(F32) * buf[8 : 8 + R]
        for j in range(1, TAPS):
            v = v + s.wc[j : j + 1, :].astype(F32) * shifted(buf, j, second)
        s.conv[trow(r), :] = jnp.where(place(r) < count, v, 0.0).astype(BF)
        return c

    def project(own, out):
        cv = s.conv[own, :]
        for c in range(3):
            p = mm(cv, s.wp[:, c * features : (c + 1) * features])
            s.qkv[i, out, c * features : (c + 1) * features] = (p * SCALE if c == 0 else p).astype(BF)
        s.wide_a[out, :] = mm(cv, s.wp[:, 3 * features :])

    per = length // R // 2
    if second:
        for h in (1, 0):
            arrive(h)
            for r in reversed(range(h * per, (h + 1) * per)):
                first_norm(r, 0)
            loaded("wc" if h else "")
            for r in range(h * per, (h + 1) * per):
                conv(r, 0)
            loaded("wp" if h else "")
            project(pl.ds(i * length + h * (length // 2), length // 2), half_rows(h, length))
    else:
        steps(length // R, first_norm)
        loaded("wc")
        steps(length // R, conv)
        loaded("wp")
        project(tok, slice(None))
    keep = triangle(second, length)
    lane = lax.broadcasted_iota(jnp.int32, (length, 2 * HD), 1) < HD

    def pair(p, c):
        def at(k):
            return pl.ds(k * features + p * 2 * HD, 2 * HD)

        q, k, v = (s.qkv[i, :, at(n)] for n in range(3))
        z = jnp.zeros_like(q)
        tot = None
        for h in range(2):
            mine = lane if h == 0 else jnp.logical_not(lane)
            sw = jnp.where(keep, nt(jnp.where(mine, q, z), k), 0.0).astype(BF)
            s.sw[i, 2 * p + h] = sw
            part = mm(sw, jnp.where(mine, v, z))
            tot = part if tot is None else tot + part
        s.an[i, :, at(0)] = tot
        return c

    steps(features // (2 * HD), pair)

    def gate(r, c):
        a = s.an[i, rows(r), :]
        sc = lax.rsqrt(jnp.mean(a * a, -1, keepdims=True) + 1e-6)
        an = a * sc
        g = s.wide_a[rows(r), :]
        sg = sigmoid(g)
        act = g * sg
        s.an[i, rows(r), :] = an
        s.ra[i, rows(r), :] = wide(sc)
        s.act[i, rows(r), :] = act
        s.dact[i, rows(r), :] = sg + act * (1.0 - sg)
        s.gated[trow(r), :] = (an * act).astype(BF)
        return c

    steps(length // R, gate)
    loaded("wo")
    s.branch[i] = mm(s.gated[tok, :], s.wo[...])

    def second_norm(r, c):
        v = s.inflow[i, rows(r), :].astype(F32) + mod[2:3, :] * s.branch[i, rows(r), :]
        n, sc = stats(v)
        s.hid[rows(r), :] = v
        s.n2[i, rows(r), :] = n
        s.r2[i, rows(r), :] = wide(sc)
        s.m2[trow(r), :] = (n * (1.0 + mod[4:5, :]) + mod[3:4, :]).astype(BF)
        return c

    steps(length // R, second_norm)
    loaded("wu")
    loaded("wd")
    width = 256

    def feed(own, out):
        for c in range(hidden // width):
            at = pl.ds(c * width, width)
            h = mm(s.m2[own, :], s.wu[:, at])
            k0, k1 = 0.7978845608028654, 0.044715
            hh = h * h
            t = jnp.tanh(h * (k0 + (k0 * k1) * hh))
            half = 0.5 * (1.0 + t)
            s.ha[own, at] = (h * half).astype(BF)
            s.dgelu[i, out, at] = half + (0.5 * h) * (1.0 - t * t) * (k0 + (3 * k0 * k1) * hh)
        s.ffn[i, out, :] = mm(s.ha[own, :], s.wd[...])

    def last(r):
        s.result[i, rows(r), :] = (s.hid[rows(r), :] + mod[5:6, :] * s.ffn[i, rows(r), :]).astype(BF)

    if second:
        feed(tok, slice(None))
        for r in range(2 * per):
            last(r)
    else:
        for h in (1, 0):
            feed(pl.ds(i * length + h * (length // 2), length // 2), half_rows(h, length))
            for r in range(h * per, (h + 1) * per):
                last(r)
            depart(h)


def backward(s, i, second, count, hook=nothing, arrive=nothing, depart=None):
    length, features = s.inflow.shape[1:]
    hidden = s.wu.shape[1]
    mod, dmod, up = s.mod.at[i], s.dmod.at[i], s.ups.at[i]
    tok = token_rows(i, length)

    def trow(r):
        return token_rows(i, length, r)

    def place(r):
        return r * R + lax.broadcasted_iota(jnp.int32, (R, 1), 0)

    zero = jnp.zeros((8, features), F32)

    def start(r, acc):
        u = up[rows(r), :].astype(F32)
        s.dffn[trow(r), :] = (mod[5:6, :] * u).astype(BF)
        return acc + fold(u * s.ffn[i, rows(r), :])

    width = 256
    per = length // R // 2

    def feed(own, out):
        for c in range(hidden // width):
            at = pl.ds(c * width, width)
            d = nt(s.dffn[own, :], s.wd[at, :])
            s.dpre[own, at] = (d * s.dgelu[i, out, at]).astype(BF)
        s.wide_a[out, :] = nt(s.dpre[own, :], s.wu[...])

    acc = zero
    for h in range(2):
        arrive(h)
        for r in range(h * per, (h + 1) * per):
            acc = start(r, acc)
    hook("down")
    feed(tok, slice(None))
    dmod[5:6, :] = jnp.sum(acc, 0, keepdims=True)
    hook("up")

    def mid(r, acc):
        dm = s.wide_a[rows(r), :]
        n = s.n2[i, rows(r), :]
        dh = up[rows(r), :].astype(F32) + norm_back(
            dm * (1.0 + mod[4:5, :]), n, s.r2[i, rows(r), :][:, :1]
        )
        s.hid[rows(r), :] = dh
        s.dbr[trow(r), :] = (mod[2:3, :] * dh).astype(BF)
        new = (fold(dm), fold(dm * n), fold(dh * s.branch[i, rows(r), :]))
        return tuple(a + b for a, b in zip(acc, new))

    acc = steps(length // R, mid, (zero,) * 3)
    for k, a in zip((3, 4, 2), acc):
        dmod[k : k + 1, :] = jnp.sum(a, 0, keepdims=True)
    hook("out")
    s.wide_a[...] = nt(s.dbr[tok, :], s.wo[...])

    def gate(r, c):
        dg = s.wide_a[rows(r), :]
        an = s.an[i, rows(r), :]
        dn = dg * s.act[i, rows(r), :]
        s.dproj[trow(r), 3 * features :] = (dg * an * s.dact[i, rows(r), :]).astype(BF)
        da = s.ra[i, rows(r), :][:, :1] * (dn - an * jnp.mean(dn * an, -1, keepdims=True))
        s.datt[rows(r), :] = da.astype(BF)
        return c

    steps(length // R, gate)
    hook("attend")
    keep = triangle(second, length)
    lane = lax.broadcasted_iota(jnp.int32, (length, 2 * HD), 1) < HD

    def pair(p, c):
        def at(k):
            return pl.ds(k * features + p * 2 * HD, 2 * HD)

        q, k, v = (s.qkv[i, :, at(n)] for n in range(3))
        g = s.datt[:, at(0)]
        z = jnp.zeros_like(q)
        dq = dk = dv = None
        for h in range(2):
            mine = lane if h == 0 else jnp.logical_not(lane)
            gm = jnp.where(mine, g, z)
            ds = jnp.where(keep, nt(gm, v), 0.0).astype(BF)
            a = mm(ds, jnp.where(mine, k, z))
            b = tn(ds, jnp.where(mine, q, z))
            e = tn(s.sw[i, 2 * p + h], gm)
            dq = a if dq is None else dq + a
            dk = b if dk is None else dk + b
            dv = e if dv is None else dv + e
        s.dproj[tok, at(0)] = (dq * SCALE).astype(BF)
        s.dproj[tok, at(1)] = dk.astype(BF)
        s.dproj[tok, at(2)] = dv.astype(BF)
        hook(f"pair{p}")
        return c

    steps(features // (2 * HD), pair)
    def mask_rows(r):
        at = pl.ds(r * R + 8, R)
        s.dcv[at, :] = jnp.where(place(r) < count, s.dcv[at, :], 0.0)

    def conv(r, acc):
        dbuf = s.dcv[rows(r, 16), :]
        mbuf = s.mixed[i, rows(r, 16), :]
        here = dbuf[8 : 8 + R]
        d = s.wc[0:1, :].astype(F32) * here
        taps = [fold(here * mbuf[8 : 8 + R])]
        for j in range(1, TAPS):
            d = d + s.wc[j : j + 1, :].astype(F32) * shifted(dbuf, j, (not second) if isinstance(second, bool) else jnp.logical_not(second))
            taps.append(fold(here * shifted(mbuf, j, second)))
        d = jnp.where(place(r) < count, d, 0.0)
        n = s.n1[i, rows(r), :]
        res = s.hid[rows(r), :] + norm_back(d * (1.0 + mod[1:2, :]), n, s.r1[i, rows(r), :][:, :1])
        s.dx[i, rows(r), :] = res.astype(BF)
        return tuple(a + b for a, b in zip(acc, (fold(d), fold(d * n), *taps)))

    acc = (zero,) * (2 + TAPS)
    if depart:
        for h in (0, 1):
            own = pl.ds(i * length + h * (length // 2), length // 2)
            s.dcv[h * (length // 2) + 8 : (h + 1) * (length // 2) + 8, :] = nt(s.dproj[own, :], s.wp[...])
            for r in range(h * per, (h + 1) * per):
                mask_rows(r)
            for r in range(h * per, (h + 1) * per):
                acc = conv(r, acc)
            depart(h)
    else:
        s.dcv[8 : length + 8, :] = nt(s.dproj[tok, :], s.wp[...])
        hook("conv")
        for r in range(2 * per):
            mask_rows(r)
        acc = steps(length // R, conv, acc)
    for k in range(2):
        dmod[k : k + 1, :] = jnp.sum(acc[k], 0, keepdims=True)
    for j in range(TAPS):
        s.dwc[j : j + 1, :] += jnp.sum(acc[2 + j], 0, keepdims=True)


ACROSS, ALONG, BETWEEN = (0, 1, 2, 3), (0, 2, 3, 1), (0, 2, 1, 3)
PIECES = {
    "d0": ("down", 0, 128, ACROSS),
    "d1": ("down", 128, 128, BETWEEN),
    "d2": ("down", 256, 128, BETWEEN),
    "u0": ("up", 0, 384, ACROSS),
    "u1": ("up", 384, 256, BETWEEN),
    "u2": ("up", 640, 640, ACROSS),
    "u3": ("up", 1280, 256, ACROSS),
    "o0": ("out", 0, 384, ACROSS),
    "p0": ("proj", 0, 384, ACROSS),
    "p1": ("proj", 384, 384, ACROSS),
    "p2": ("proj", 768, 256, BETWEEN),
    "p3": ("proj", 1024, 384, ACROSS),
    "p4": ("proj", 1408, 128, ACROSS),
}
TURNS = {
    "down": ("Wd",),
    "up": ("d00", "Wu", "d10", "d20"),
    "out": ("Wo",),
    "attend": ("u00", "u10"),
    "pair0": ("u20", "u30", "o00"),
    "pair1": ("d01",),
    "pair2": ("Wp", "d11"),
    "conv": ("u01",),
    "tail": ("p00", "p10", "GATHER", "p20", "p30", "d21", "p40", "COND", "u11", "u21", "d02", "u31", "u02", "o01", "d12", "p21", "p01", "u22", "d03", "u32", "p11", "u03", "o02", "d13", "SHARE", "p02", "p31", "u23", "ADA", "d22", "p41", "u33", "p12", "u12", "p22", "o03", "p03", "p32", "p42", "d23", "p13", "u13", "p23", "p33", "p43"),
}


def spot(chunk, order):
    p = 0
    for bit in order:
        p = 2 * p + ((chunk >> bit) & 1)
    return p


class Halving:
    def __init__(self, s, name, section, spread, me):
        self.whole, self.at, self.width, self.order = PIECES[name]
        self.g = getattr(s, "g_" + name)
        self.got = [getattr(s, f"got{k}_" + name) for k in range(4)]
        self.sent = getattr(s, "sent_" + name)
        self.fin = getattr(s, "fin_" + self.whole).at[:, pl.ds(self.at, self.width)]
        index = list(PIECES).index(name)
        self.send_sem = [s.rs_send.at[index, k] for k in range(4)]
        self.recv_sem = [s.rs_recv.at[index, k] for k in range(4)]
        height = self.g.shape[0]
        low = 0
        self.keep, self.give, self.peer = [], [], []
        self.bit = [lax.rem(lax.div(me, 1 << b), 2) for b in self.order]
        for k, b in enumerate(self.order):
            half = height >> (k + 1)
            step = half if half % 16 == 0 else 8
            self.keep.append(pl.multiple_of(low + self.bit[k] * half, step))
            self.give.append(pl.multiple_of(low + (1 - self.bit[k]) * half, step))
            low = self.keep[-1]
            other = me + (1 - 2 * self.bit[k]) * (1 << b)
            self.peer.append((section, spread(other)))

    def copy(self, k):
        half = self.g.shape[0] >> (k + 1)
        src = self.sent if k == 3 else self.g.at[pl.ds(self.give[k], half)]
        return pltpu.make_async_remote_copy(
            src_ref=src,
            dst_ref=self.got[k],
            send_sem=self.send_sem[k],
            recv_sem=self.recv_sem[k],
            device_id=self.peer[k],
            device_id_type=MESH,
        )

    def start(self, k):
        self.copy(k).start()

    def step(self, k):
        self.copy(k).wait_recv()
        got = self.got[k]
        if k < 2:
            at = pl.ds(self.keep[k], got.shape[0])
            self.g[at, :] = self.g[at, :] + got[...]
        elif k == 2:
            part = got.shape[0] // 2
            v = self.g[pl.ds(self.keep[2], 2 * part), :].astype(F32) + got[...].astype(F32)
            upper = self.bit[3] == 1
            self.sent[...] = jnp.where(upper, v[:part], v[part:]).astype(BF)
            self.fin[...] = jnp.where(upper, v[part:], v[:part])
        else:
            self.fin[...] += got[...].astype(F32)
        if k < 3:
            self.start(k + 1)

    def end(self):
        for k in range(4):
            self.copy(k).wait_send()


def group_rows(val, order):
    height = val.shape[0] // GROUP
    at = [0] * GROUP
    for c in range(GROUP):
        at[spot(c, order)] = c
    return jnp.concatenate([val[c * height : (c + 1) * height] for c in at], 0)


def turn_operands(s):
    for left, out in ((s.ha, s.ha_t), (s.m2, s.m2_t), (s.gated, s.gated_t), (s.conv, s.conv_t)):
        width = 384

        def one(c, carry, left=left, out=out):
            at = pl.ds(pl.multiple_of(c * width, width), width)
            out[at, :] = left[:, at].T
            return carry

        loop(left.shape[1] // width, one)


OPERANDS = {"d": ("ha_t", "dffn"), "u": ("m2_t", "dpre"), "o": ("gated_t", "dbr"), "p": ("conv_t", "dproj")}


def first_products(s):
    for letter, (left, right) in OPERANDS.items():
        left, right, out = getattr(s, left), getattr(s, right), getattr(s, "part_" + letter)
        half, width = left.shape[1] // 2, 384
        if left.shape[0] > right.shape[1]:

            def one(c, carry, left=left, right=right, out=out):
                at = pl.ds(pl.multiple_of(c * width, width), width)
                out[at, :] = mm(left[at, :half], right[:half, :])
                return carry

            loop(left.shape[0] // width, one)
        else:

            def one(c, carry, left=left, right=right, out=out):
                at = pl.ds(pl.multiple_of(c * width, width), width)
                out[:, at] = mm(left[:, :half], right[:half, at])
                return carry

            loop(right.shape[1] // width, one)


def weight_gradient(s, letter, jobs, begun):
    mine = [job for name, job in jobs.items() if name[0] == letter]
    left, right = (getattr(s, name) for name in OPERANDS[letter])
    half = left.shape[1] // 2

    def product(at, to):
        if begun:
            return getattr(s, "part_" + letter)[at, to] + mm(left[at, half:], right[half:, to])
        return mm(left[at, :], right[:, to])

    if letter == "d":
        features = right.shape[1]
        chunk = left.shape[0] // GROUP
        per = features // chunk
        for c in range(left.shape[0] // features):
            v = product(slice(c * features, (c + 1) * features), slice(None)).astype(BF)
            for j in range(per):
                for job in mine:
                    p = spot(c * per + j, job.order) * chunk
                    job.g[p : p + chunk, :] = v[j * chunk : (j + 1) * chunk, job.at : job.at + job.width]
    else:
        for job in mine:
            v = product(slice(None), slice(job.at, job.at + job.width))
            job.g[...] = group_rows(v, job.order).astype(BF)
    for job in mine:
        job.start(0)


OUTS = ("o_act", "o_dx", "o_cond", "o_ada", "o_conv", "o_proj", "o_out", "o_up", "o_down")
INS = ("patches", "condition", "count", "cotangent", "w_ada", "w_conv", "w_proj", "w_out", "w_up", "w_down")


def kernel(names, *refs):
    s = Refs(names, refs)
    section, place = lax.axis_index("section"), lax.axis_index("dp")
    stride = lax.axis_size("dp") // GROUP
    me, low = lax.div(place, stride), lax.rem(place, stride)
    first, second = section == 0, section == 1

    def spread(member):
        return member * stride + low

    partner = (1 - section, place)
    micro, length, features = s.inflow.shape
    s.result, s.dx = s.o_act.at[0, :, 0], s.o_dx.at[0, :, 0]
    s.fin_ada, s.fin_conv, s.fin_cond = s.o_ada.at[0], s.o_conv, s.o_cond
    s.fin_proj, s.fin_out, s.fin_up, s.fin_down = (o.at[0] for o in (s.o_proj, s.o_out, s.o_up, s.o_down))

    loads = {
        "ada": (s.w_ada.at[0], s.ada),
        "cond": (s.condition, s.cond),
        "wc": (s.w_conv.at[0], s.wc),
        "wp": (s.w_proj.at[0], s.wp),
        "wo": (s.w_out.at[0], s.wo),
        "wu": (s.w_up.at[0], s.wu),
        "wd": (s.w_down.at[0], s.wd),
    }
    order = list(loads)

    def load(name):
        return pltpu.make_async_copy(*loads[name], s.load_sem.at[order.index(name)])

    def load_patches():
        return pltpu.make_async_copy(s.patches.at[:, 0], s.inflow, s.load_sem.at[len(order)])

    def load_cotangent():
        return pltpu.make_async_copy(s.cotangent.at[:, 0], s.ups, s.load_sem.at[len(order)])

    load("cond").start()
    load("ada").start()
    pl.when(first)(lambda: load_patches().start())
    for name in order[2:4]:
        load(name).start()

    barrier = pltpu.get_barrier_semaphore()

    def greet(j, c):
        other = lax.rem(me + j, GROUP)
        pl.semaphore_signal(barrier, 1, device_id=(section, spread(other)), device_id_type=MESH)
        return c

    lax.fori_loop(1, GROUP, greet, 0)
    pl.semaphore_signal(barrier, 1, device_id=partner, device_id_type=MESH)

    zero = jnp.zeros((8, features), F32)
    for i in range(micro):
        s.mixed[i, 0:8, :] = zero
        s.mixed[i, length + 8 :, :] = zero
    s.dcv[0:8, :] = zero
    s.dcv[length + 8 :, :] = zero
    s.dwc[...] = zero

    load("cond").wait()
    conds = [s.cond[i : i + 1, :].astype(F32) for i in range(micro)]
    silus = [(v * sigmoid(v)).astype(BF).astype(F32) for v in conds]
    row = lax.broadcasted_iota(jnp.int32, (16, features), 0)
    act_rows = jnp.where(
        row < 6,
        jnp.broadcast_to(silus[0], (16, features)),
        jnp.where(row < 12, jnp.broadcast_to(silus[1], (16, features)), 0.0),
    ).astype(BF)
    s.own_act[...] = act_rows
    s.all_act[lax.rem(me, 2), lax.div(me, 2)] = act_rows

    @pl.when(first)
    def _():
        load_patches().wait()
        for i in range(micro):
            for r in range(length // R):
                input_norm(s, i, r)

    load("ada").wait()
    for name in order[4:]:
        load(name).start()
    pl.when(second)(lambda: load_cotangent().start())
    for k in range(6):
        m = mm(act_rows, s.ada[:, k * features : (k + 1) * features])
        for i in range(micro):
            s.mod[i, k : k + 1, :] = m[6 * i : 6 * i + 1, :]

    def hop(source, target, i, h):
        at = half_rows(h, length)
        return pltpu.make_async_remote_copy(
            src_ref=source.at[i, at],
            dst_ref=target.at[i, at],
            send_sem=s.hop_send.at[i, h],
            recv_sem=s.hop_recv.at[i, h],
            device_id=partner,
            device_id_type=MESH,
        )

    def result_copy(i, h):
        return hop(s.result, s.inflow, i, h)

    def dx_copy(i, h):
        return hop(s.dx, s.ups, i, h)

    core, chip = lax.rem(me, 2), lax.div(me, 2)
    chips = GROUP // 2
    beside = (section, spread(me + 1 - 2 * core))

    def gather_copy(j, src, dst, send, recv, received=False):
        other = lax.rem(chip + j, chips)
        slot = other if received else chip
        return pltpu.make_async_remote_copy(
            src_ref=src,
            dst_ref=dst.at[core, slot],
            send_sem=send.at[j],
            recv_sem=recv.at[slot],
            device_id=(section, spread(2 * other + core)),
            device_id_type=MESH,
        )

    def share_copy(src, dst, send, recv, received=False):
        half = dst.at[1 - core if received else core]
        return pltpu.make_async_remote_copy(
            src_ref=half,
            dst_ref=half,
            send_sem=send.at[0],
            recv_sem=recv.at[chips],
            device_id=beside,
            device_id_type=MESH,
        )

    acts = (s.own_act, s.all_act, s.act_send, s.act_recv)
    mods = (s.own_mod, s.all_mod, s.mod_send, s.mod_recv)

    def each_chip(fn):
        def one(j, c):
            fn(j)
            return c

        lax.fori_loop(1, chips, one, 0)

    def share(what):
        each_chip(lambda j: gather_copy(j, *what, received=True).wait_recv())
        share_copy(*what).start()

    jobs = {name: Halving(s, name, section, spread, me) for name in PIECES}

    def take(words, begun=False):
        for word in words:
            if word.startswith("W"):
                weight_gradient(s, word[1], jobs, begun)
            else:
                jobs[word[:2]].step(int(word[2]))

    def loaded(name):
        if name:
            load(name).wait()

    @pl.when(first)
    def _():
        for i in range(micro):

            def depart(h, i=i):
                if i == 0 and h == 1:
                    pl.semaphore_wait(barrier, GROUP)
                result_copy(i, h).start()

            forward(s, i, False, s.count[i], nothing if i else loaded, depart=depart, normed=True)
        each_chip(lambda j: gather_copy(j, *acts).start())
        turn_operands(s)
        for i in range(micro):
            ending = i == micro - 1
            if ending:
                first_products(s)
            backward(
                s,
                i,
                False,
                s.count[i],
                (lambda name: take(TURNS[name], True) if name in TURNS else None) if ending else nothing,
                arrive=lambda h, i=i: dx_copy(i, h).wait_recv(),
            )

    @pl.when(second)
    def _():
        pl.semaphore_wait(barrier, GROUP)
        each_chip(lambda j: gather_copy(j, *acts).start())
        for i in range(micro):
            forward(
                s, i, True, s.count[i], nothing if i else loaded, arrive=lambda h, i=i: result_copy(i, h).wait_recv()
            )
            if i == 0:
                load_cotangent().wait()
            if i == micro - 1:
                backward(s, i, True, s.count[i], depart=lambda h, i=i: dx_copy(i, h).start())
            else:
                backward(s, i, True, s.count[i])
                for h in range(2):
                    dx_copy(i, h).start()
        turn_operands(s)
        for name in TURNS:
            if name != "tail":
                take(TURNS[name])

    def gather_rows():
        for i in range(micro):
            for k in range(6):
                s.stage[6 * i + k : 6 * i + k + 1, :] = s.dmod[i, k : k + 1, :]
        s.stage[12 : 12 + TAPS, :] = s.dwc[0:TAPS, :]
        s.stage[15:16, :] = jnp.zeros((1, features), F32)
        own = s.stage[...].astype(BF)
        s.own_mod[...] = own
        s.all_mod[core, chip] = own
        each_chip(lambda j: gather_copy(j, *mods).start())
        share(acts)

    cond_copy = pltpu.make_async_remote_copy(
        src_ref=s.own_cond,
        dst_ref=s.got_cond,
        send_sem=s.cond_sem.at[0],
        recv_sem=s.cond_sem.at[1],
        device_id=partner,
        device_id_type=MESH,
    )

    def condition_gradient():
        tot = jnp.zeros((16, features), F32)
        for k in range(6):
            part = nt(s.own_mod[...], s.ada[:, k * features : (k + 1) * features])
            tot = tot + jnp.where(jnp.logical_or(row == k, row == 6 + k), part, 0.0)
        for i in range(micro):
            sg = sigmoid(conds[i])
            slope = sg + conds[i] * sg * (1.0 - sg)
            s.own_cond[i, :, :] = jnp.sum(tot[6 * i : 6 * i + 6], 0, keepdims=True) * slope
        cond_copy.start()

    def image_sums():
        share_copy(*acts, received=True).wait_recv()
        share_copy(*mods, received=True).wait_recv()
        chunk = features // GROUP
        n_rows = GROUP * 16
        flat_act = s.all_act[...].reshape(n_rows, features)
        flat_mod = s.all_mod[...].reshape(n_rows, features)
        pick = (
            lax.broadcasted_iota(jnp.int32, (chunk, features), 1)
            == me * chunk + lax.broadcasted_iota(jnp.int32, (chunk, features), 0)
        ).astype(F32).astype(BF)
        left = nt(pick, flat_act)
        lane = lax.rem(lax.broadcasted_iota(jnp.int32, (chunk, n_rows), 1), 16)
        for k in range(6):
            mine = jnp.logical_or(lane == k, lane == 6 + k)
            s.fin_ada[:, k * features : (k + 1) * features] = mm(
                jnp.where(mine, left, 0.0).astype(BF), flat_mod
            )
        picked = nt(flat_mod, pick).astype(BF)
        tap = lax.broadcasted_iota(jnp.int32, (8, n_rows), 0)
        at_tap = lax.rem(lax.broadcasted_iota(jnp.int32, (8, n_rows), 1), 16) == 12 + tap
        sums = mm(jnp.where(jnp.logical_and(at_tap, tap < TAPS), 1.0, 0.0).astype(BF), picked)
        for j in range(TAPS):
            s.fin_conv[j, :, :] = sums[j : j + 1, :]
        cond_copy.wait()
        s.fin_cond[...] = s.own_cond[...] + s.got_cond[...]

    ends = {"SHARE": lambda: share(mods), "GATHER": gather_rows, "COND": condition_gradient, "ADA": image_sums}
    for word in TURNS["tail"]:
        if word in ends:
            ends[word]()
        else:
            take((word,))

    for i in range(micro):
        for h in range(2):
            pl.when(first)(lambda i=i, h=h: result_copy(i, h).wait_send())
            pl.when(second)(lambda i=i, h=h: dx_copy(i, h).wait_send())
    for job in jobs.values():
        job.end()
    for what in (acts, mods):
        each_chip(lambda j, what=what: gather_copy(j, *what).wait_send())
        share_copy(*what).wait_send()


def finish(n, *refs):
    held, given, sems = refs[:n], refs[n : 2 * n], refs[2 * n]
    outward = [pltpu.make_async_copy(a, b, sems.at[k]) for k, (a, b) in enumerate(zip(held, given))]
    for o in outward:
        o.start()
    for o in outward:
        o.wait()


def body(patches, condition, valid_count, cotangent, ada_weight, conv_weight, proj_weight, out_weight, up_weight, down_weight):
    micro, images, length, features = patches.shape
    hidden = up_weight.shape[2]
    heads = features // HD
    tokens = micro * length
    chunk, deep = features // GROUP, hidden // GROUP
    arrays = dict(
        ada=((features, 6 * features), BF),
        cond=((micro, features), BF),
        wc=((TAPS, features), BF),
        wp=((features, 4 * features), BF),
        wo=((features, features), BF),
        wu=((features, hidden), BF),
        wd=((hidden, features), BF),
        inflow=((micro, length, features), BF),
        ups=((micro, length, features), BF),
        mod=((micro, 8, features), F32),
        dmod=((micro, 8, features), F32),
        dwc=((8, features), F32),
        n1=((micro, length, features), F32),
        r1=((micro, length, 128), F32),
        mixed=((micro, length + 16, features), F32),
        conv=((tokens, features), BF),
        qkv=((micro, length, 3 * features), BF),
        sw=((micro, heads, length, length), BF),
        an=((micro, length, features), F32),
        ra=((micro, length, 128), F32),
        act=((micro, length, features), F32),
        dact=((micro, length, features), F32),
        gated=((tokens, features), BF),
        branch=((micro, length, features), F32),
        hid=((length, features), F32),
        wide_a=((length, features), F32),
        n2=((micro, length, features), F32),
        r2=((micro, length, 128), F32),
        m2=((tokens, features), BF),
        ffn=((micro, length, features), F32),
        ha=((tokens, hidden), BF),
        ha_t=((hidden, tokens), BF),
        m2_t=((features, tokens), BF),
        gated_t=((features, tokens), BF),
        conv_t=((features, tokens), BF),
        part_d=((hidden, features), F32),
        part_u=((features, hidden), F32),
        part_o=((features, features), F32),
        part_p=((features, 4 * features), F32),
        dgelu=((micro, length, hidden), F32),
        dffn=((tokens, features), BF),
        dpre=((tokens, hidden), BF),
        dbr=((tokens, features), BF),
        datt=((length, features), BF),
        dproj=((tokens, 4 * features), BF),
        dcv=((length + 16, features), F32),
        own_act=((16, features), BF),
        all_act=((2, GROUP // 2, 16, features), BF),
        own_mod=((16, features), BF),
        all_mod=((2, GROUP // 2, 16, features), BF),
        stage=((16, features), F32),
        own_cond=((micro, 1, features), F32),
        got_cond=((micro, 1, features), F32),
    )
    tall = dict(down=hidden, up=features, out=features, proj=features)
    for name, (whole, at, width, order) in PIECES.items():
        arrays["g_" + name] = ((tall[whole], width), BF)
        for k in range(4):
            arrays[f"got{k}_{name}"] = ((tall[whole] >> (k + 1), width), BF)
        arrays["sent_" + name] = ((tall[whole] // GROUP, width), BF)
    sems = dict(
        load_sem=(8,),
        hop_send=(2, 2),
        hop_recv=(2, 2),
        rs_send=(len(PIECES), 4),
        rs_recv=(len(PIECES), 4),
        act_send=(GROUP,),
        act_recv=(GROUP,),
        mod_send=(GROUP,),
        mod_recv=(GROUP,),
        cond_sem=(2,),
    )
    names = (*INS, *OUTS, *arrays, *sems)
    any_spec = pl.BlockSpec(memory_space=pl.ANY)
    out_shape = (
        ((1, micro, 1, length, features), BF),
        ((1, micro, 1, length, features), BF),
        ((micro, 1, features), F32),
        ((1, chunk, 6 * features), F32),
        ((TAPS, 1, chunk), F32),
        ((1, chunk, 4 * features), F32),
        ((1, chunk, features), F32),
        ((1, chunk, hidden), F32),
        ((1, deep, features), F32),
    )
    outs = pl.pallas_call(
        lambda *refs: kernel(names, *refs),
        out_shape=[pltpu.VMEM(*o) for o in out_shape],
        in_specs=[pl.BlockSpec(memory_space=pltpu.SMEM if n == "count" else pltpu.HBM) for n in INS],
        out_specs=[pl.BlockSpec(memory_space=pltpu.VMEM)] * len(OUTS),
        scratch_shapes=[pltpu.VMEM(*a) for a in arrays.values()]
        + [pltpu.SemaphoreType.DMA(n) for n in sems.values()],
        compiler_params=pltpu.CompilerParams(
            collective_id=0, has_side_effects=True, vmem_limit_bytes=60000 * 1024
        ),
        name="relay",
    )(
        patches,
        condition.reshape(micro, features),
        valid_count.reshape(micro),
        cotangent, ada_weight, conv_weight, proj_weight, out_weight, up_weight, down_weight)
    outs = pl.pallas_call(
        lambda *refs: finish(len(out_shape), *refs),
        out_shape=[jax.ShapeDtypeStruct(*o) for o in out_shape],
        in_specs=[pl.BlockSpec(memory_space=pltpu.VMEM)] * len(out_shape),
        out_specs=[pl.BlockSpec(memory_space=pltpu.HBM)] * len(out_shape),
        scratch_shapes=[pltpu.SemaphoreType.DMA((len(out_shape),))],
        compiler_params=pltpu.CompilerParams(vmem_limit_bytes=2000 * 1024),
        name="finish",
    )(*outs)
    outs = list(outs)
    outs[4] = outs[4].reshape(1, TAPS, chunk)
    stride = lax.axis_size("dp") // GROUP
    if stride > 1:
        teams = [[t * stride + j for j in range(stride)] for t in range(GROUP)]
        outs = [
            lax.psum_scatter(o, "dp", scatter_dimension=2 if n == 4 else 1, axis_index_groups=teams, tiled=True)
            if n >= 3
            else o
            for n, o in enumerate(outs)
        ]
    return tuple(outs)


def solution(mesh):
    by_section = P("section", None, None)
    placed = (
        P(None, "dp", None, None),
        P(None, "dp", None),
        P(None, "dp"),
        P(None, "dp", None, None),
        *(by_section,) * 6,
    )
    rows_out = P("section", "dp", None)
    return jax.shard_map(
        body,
        mesh=mesh,
        in_specs=placed,
        out_specs=(
            P("section", None, "dp", None, None),
            P("section", None, "dp", None, None),
            P(None, "dp", None),
            rows_out,
            P("section", None, "dp"),
            rows_out,
            rows_out,
            rows_out,
            rows_out,
        ),
        check_vma=False,
    )
```
